32 devices in a mesh: dp: 8 (over z, x), tensor: 4 (over y, core).
Axes of the slice: x: 2, y: 2, z: 4, core: 2. Of those that a mesh axis runs over, the one named last changes fastest.
Arguments:
- layer_input: bfloat16 [8192, 512], P(('dp', 'tensor')), may hold values from -6 to 6
- segments: int32 [8, 1024], P('dp'), may hold values from 0 to 3, never falling along the last dimension, each value on 1 to 800 neighbouring positions
- norm1_gain: bfloat16 [512], replicated, may hold values from 0.5 to 1.5
- norm1_bias: bfloat16 [512], replicated, may hold values from -4 to 4
- w_query: bfloat16 [512, 512], P(None, 'tensor'), may hold values from -0.25 to 0.25
- b_query: bfloat16 [512], P('tensor'), may hold values from -6 to 6
- w_key: bfloat16 [512, 512], P(None, 'tensor'), may hold values from -0.25 to 0.25
- w_value: bfloat16 [512, 512], P(None, 'tensor'), may hold values from -0.25 to 0.25
- b_value: bfloat16 [512], P('tensor'), may hold values from -6 to 6
- w_out: bfloat16 [512, 512], P('tensor'), may hold values from -2 to 2
- b_out: bfloat16 [512], replicated, may hold values from -4 to 4
- gate1_w: bfloat16 [512, 512], P('tensor'), may hold values from -0.25 to 0.25
- gate1_b: bfloat16 [512], replicated, may hold values from -6 to 6
- norm2_gain: bfloat16 [512], replicated, may hold values from 0.5 to 1.5
- norm2_bias: bfloat16 [512], replicated, may hold values from -4 to 4
- w_in: bfloat16 [512, 2048], P(None, 'tensor'), may hold values from -0.25 to 0.25
- b_in: bfloat16 [2048], P('tensor'), may hold values from -6 to 6
- w_back: bfloat16 [2048, 512], P('tensor'), may hold values from -0.1875 to 0.1875
- b_back: bfloat16 [512], replicated, may hold values from -4 to 4
- gate2_w: bfloat16 [512, 512], P('tensor'), may hold values from -0.25 to 0.25
- gate2_b: bfloat16 [512], replicated, may hold values from -6 to 6
- cotangent: bfloat16 [8192, 512], P(('dp', 'tensor')), may hold values from -6 to 6
Outputs:
- output: bfloat16 [8192, 512], P(('dp', 'tensor'))
- input_grad: float32 [8192, 512], P(('dp', 'tensor'))
- grad_norm1_gain: float32 [512], replicated
- grad_norm1_bias: float32 [512], replicated
- grad_w_query: float32 [512, 512], P(None, 'tensor')
- grad_b_query: float32 [512], P('tensor')
- grad_w_key: float32 [512, 512], P(None, 'tensor')
- grad_w_value: float32 [512, 512], P(None, 'tensor')
- grad_b_value: float32 [512], P('tensor')
- grad_w_out: float32 [512, 512], P('tensor')
- grad_b_out: float32 [512], replicated
- grad_gate1_w: float32 [512, 512], P('tensor')
- grad_gate1_b: float32 [512], replicated
- grad_norm2_gain: float32 [512], replicated
- grad_norm2_bias: float32 [512], replicated
- grad_w_in: float32 [512, 2048], P(None, 'tensor')
- grad_b_in: float32 [2048], P('tensor')
- grad_w_back: float32 [2048, 512], P('tensor')
- grad_b_back: float32 [512], replicated
- grad_gate2_w: float32 [512, 512], P('tensor')
- grad_gate2_b: float32 [512], replicated
The draws below stay inside these ranges and needn't reach their ends.
Inputs may be any that keep to these rules, and one draw needn't show every extreme that they name: `segments`: document numbers never fall along a sequence; every sequence holds 4 documents, none longer than 800 tokens, and one document reaches that length.
All inputs are finite; a program needn't handle non-finite values.
Results may differ from the reference program's by a relative error of at most 0.014.
Values may be sent and summed in bfloat16 or wider, within the bound.
No kernel may reach another device: no remote copies, remote signals or barrier semaphores. Data moves between devices by JAX's collectives and lax.ppermute only.
A program may use at most 64 MiB of HBM per device.

```python
import math
import jax
import jax.numpy as jnp
import numpy as np
from jax import lax

D = 512
HEADS = 8
HD = 64
FF = 2048
SEQ_LEN = 1024
DOCS = 4
TOKENS = 8192
N_DP = 8


def block_scale(rng, dims, cuts, least, high):
    level = 1.0
    for position, blocks in cuts:
        heights = jax.random.uniform(jax.random.fold_in(jax.random.fold_in(rng, 6), position), (blocks,), jnp.float32, least / len(cuts), high / len(cuts))
        level = level * jnp.repeat(jnp.exp(heights), dims[position] // blocks).reshape((-1,) + (1,) * (len(dims) - 1 - position))
    return level


def split_up(number_of, total, bound, slope):
    portions = [(1 << 20) // math.isqrt(rank ** slope) + 1 for rank in range(2, number_of + 1)]
    spare, counts = total - bound - (number_of - 1), [1] * (number_of - 1)
    while spare > 0:
        candidates = [i for i in range(number_of - 1) if counts[i] < bound]
        whole, left = sum([portions[i] for i in candidates]), spare
        for i in candidates:
            addition = min(bound - counts[i], max(1, left * portions[i] // whole), spare)
            counts[i] = counts[i] + addition
            spare = spare - addition
    return np.array([bound] + counts)


def uneven_parts(rng, count, total, most, lean):
    if count == 2:
        one = jax.random.randint(rng, (), max(1, total - most), min(most, total - 1) + 1)
        return jnp.stack([one, total - one])
    sizes = jnp.asarray(split_up(count, total, most, lean), jnp.int32)
    couples = (count - 1) // 2
    source_of, taker = sizes[1:1 + 2 * couples:2], sizes[2:2 + 2 * couples:2]
    margin = jnp.minimum(source_of - 1, most - taker)
    moved = jax.random.randint(jax.random.fold_in(rng, 1), (couples,), 0, 1 << 20) % (margin + 1)
    sizes = sizes.at[1:1 + 2 * couples:2].set(source_of - moved).at[2:2 + 2 * couples:2].set(taker + moved)
    return sizes[jax.random.permutation(jax.random.fold_in(rng, 2), count)]


def bell_draw(own_key, shape, scale, limit, cuts=(), held_as=jnp.bfloat16):
    array = jax.random.normal(own_key, shape, jnp.float32) * scale
    if len(cuts) > 0:
        array = block_scale(own_key, shape, cuts, -0.22, 0.18) * array
    return jnp.clip(array, min=-limit, max=limit).astype(held_as)


def setup_inputs(seed: int = 0) -> dict:
    key_of = jax.random.split(jax.random.key(seed), 23)
    return {
        "layer_input": bell_draw(key_of[0], (TOKENS, D), 1.0, 6.0, ((0, 32),)),
        "segments": jax.vmap(lambda own: jnp.searchsorted(jnp.cumsum(uneven_parts(own, DOCS, SEQ_LEN, SEQ_LEN * 25 // 32, 2)), jnp.arange(SEQ_LEN), side="right"))(jax.random.split(key_of[1], N_DP)).reshape((N_DP, SEQ_LEN)).astype(jnp.int32),
        "norm1_gain": jnp.clip(1.0 + 0.1 * jax.random.normal(key_of[2], (D,), jnp.float32), 0.5, 1.5).astype(jnp.bfloat16),
        "norm1_bias": bell_draw(key_of[3], (D,), 0.3, 4.0),
        "w_query": bell_draw(key_of[4], (D, HEADS * HD), D ** -0.5, 0.25, ((1, 4),)),
        "b_query": bell_draw(key_of[5], (HEADS * HD,), 0.5, 6.0, ((0, 4),)),
        "w_key": bell_draw(key_of[6], (D, HEADS * HD), D ** -0.5, 0.25, ((1, 4),)),
        "w_value": bell_draw(key_of[7], (D, HEADS * HD), D ** -0.5, 0.25, ((1, 4),)),
        "b_value": bell_draw(key_of[8], (HEADS * HD,), 0.5, 6.0, ((0, 4),)),
        "w_out": bell_draw(key_of[9], (HEADS * HD, D), (max(1, 16 * HEADS * HD // SEQ_LEN)) ** -0.5, 2.0, ((0, 4),)),
        "b_out": bell_draw(key_of[10], (D,), 0.3, 4.0),
        "gate1_w": bell_draw(key_of[11], (D, D), D ** -0.5, 0.25, ((0, 4),)),
        "gate1_b": bell_draw(key_of[12], (D,), 1.0, 6.0),
        "norm2_gain": jnp.clip(1.0 + 0.1 * jax.random.normal(key_of[13], (D,), jnp.float32), 0.5, 1.5).astype(jnp.bfloat16),
        "norm2_bias": bell_draw(key_of[14], (D,), 0.3, 4.0),
        "w_in": bell_draw(key_of[15], (D, FF), D ** -0.5, 0.25, ((1, 4),)),
        "b_in": bell_draw(key_of[16], (FF,), 0.5, 6.0, ((0, 4),)),
        "w_back": bell_draw(key_of[17], (FF, D), (FF // 2) ** -0.5, 0.1875, ((0, 4),)),
        "b_back": bell_draw(key_of[18], (D,), 0.3, 4.0),
        "gate2_w": bell_draw(key_of[19], (D, D), D ** -0.5, 0.25, ((0, 4),)),
        "gate2_b": bell_draw(key_of[20], (D,), 1.0, 6.0),
        "cotangent": bell_draw(key_of[21], (TOKENS, D), 1.0, 6.0, ((0, 32),)),
    }


EPSILON = 1e-05

@jax.custom_vjp
def low(v):
    return lax.optimization_barrier(v.astype(jnp.bfloat16)).astype(jnp.float32)

@jax.custom_vjp
def low_back(v):
    return v

def low_keep(v):
    return (low(v), None)

def low_pass(kept, grad):
    return (grad,)

def back_keep(v):
    return (v, None)

def back_low(kept, grad):
    return (low(grad),)
low.defvjp(low_keep, low_pass)
low_back.defvjp(back_keep, back_low)

def highest(left, right):
    return jnp.dot(left, right, precision=lax.Precision.HIGHEST, preferred_element_type=jnp.float32)

def layer_norm(values, gain, shift):
    centred = values - lax.optimization_barrier(jnp.mean(values, axis=-1, keepdims=True))
    spread = lax.optimization_barrier(jnp.mean(centred * centred, axis=-1, keepdims=True))
    return centred * lax.rsqrt(spread + EPSILON) * gain + shift

def head_major(matrix):
    return matrix.reshape(matrix.shape[0], -1, HD).transpose(1, 0, 2)

def attend_block(query_block, mask_block, heads_k, heads_v):
    scale_factor = HD ** (-0.5)
    scores = jnp.einsum('hqd,hkd->hqk', query_block, heads_k, precision=lax.Precision.HIGHEST) * scale_factor
    scores = low_back(scores)
    scores = jnp.where(mask_block[None], scores, -1e+30)
    totals = jax.nn.logsumexp(scores, axis=-1, keepdims=True)
    probs = low(jnp.exp(scores - totals))
    return jnp.einsum('hqk,hkd->hqd', probs, heads_v, precision=lax.Precision.HIGHEST)

def sequence_forward(weights, inputs, segment_row):
    norm1_gain, norm1_bias, w_query, b_query, w_key, w_value, b_value, w_out, b_out, gate1_w, gate1_b, norm2_gain, norm2_bias, w_in, b_in, w_back, b_back, gate2_w, gate2_b = weights
    rows = inputs.shape[0]
    block = min(512, rows)
    count = rows // block
    normed = low(layer_norm(inputs, norm1_gain, norm1_bias))
    query = low(low_back(highest(normed, w_query) + b_query))
    keys = low(low_back(highest(normed, w_key)))
    values = low(low_back(highest(normed, w_value) + b_value))
    places = lax.iota(jnp.int32, rows)
    allowed = (segment_row[:, None] == segment_row[None, :]) & (places[None, :] <= places[:, None])
    query_blocks = head_major(query).reshape(HEADS, count, block, HD).transpose(1, 0, 2, 3)
    heads_k = head_major(keys)
    heads_v = head_major(values)
    mask_blocks = allowed.reshape(count, block, rows)
    blockwise = jax.checkpoint(attend_block)
    mixed = lax.map(lambda pieces: blockwise(pieces[0], pieces[1], heads_k, heads_v), (query_blocks, mask_blocks))
    attended = low(low_back(mixed.transpose(0, 2, 1, 3).reshape(rows, HEADS * HD)))
    branch = low_back(highest(attended, w_out) + b_out)
    gate_one = jax.nn.sigmoid(low_back(highest(normed, gate1_w) + gate1_b))
    middle = inputs + gate_one * branch
    normed_two = low(layer_norm(middle, norm2_gain, norm2_bias))
    hidden = low(jax.nn.gelu(low_back(highest(normed_two, w_in) + b_in), approximate=True))
    ffn_out = low_back(highest(hidden, w_back) + b_back)
    gate_two = jax.nn.sigmoid(low_back(highest(normed_two, gate2_w) + gate2_b))
    return middle + gate_two * ffn_out

def reference(layer_input, segments, norm1_gain, norm1_bias, w_query, b_query, w_key, w_value, b_value, w_out, b_out, gate1_w, gate1_b, norm2_gain, norm2_bias, w_in, b_in, w_back, b_back, gate2_w, gate2_b, cotangent):
    weights = tuple((item.astype(jnp.float32) for item in (norm1_gain, norm1_bias, w_query, b_query, w_key, w_value, b_value, w_out, b_out, gate1_w, gate1_b, norm2_gain, norm2_bias, w_in, b_in, w_back, b_back, gate2_w, gate2_b)))

    def per_sequence(totals, pieces):
        inputs_row, segment_row, cotangent_row = pieces
        result_row, pullback = jax.vjp(lambda params, start: sequence_forward(params, start, segment_row), weights, inputs_row.astype(jnp.float32))
        weight_grads, start_grad = pullback(cotangent_row.astype(jnp.float32))
        totals = jax.tree.map(jnp.add, totals, weight_grads)
        return (totals, (result_row.astype(jnp.bfloat16), start_grad))
    zeroes = jax.tree.map(jnp.zeros_like, weights)
    totals, (results, input_grads) = lax.scan(per_sequence, zeroes, (layer_input.reshape(N_DP, SEQ_LEN, D), segments, cotangent.reshape(N_DP, SEQ_LEN, D)))
    return (results.reshape(TOKENS, D), input_grads.reshape(TOKENS, D), totals[0], totals[1], totals[2], totals[3], totals[4], totals[5], totals[6], totals[7], totals[8], totals[9], totals[10], totals[11], totals[12], totals[13], totals[14], totals[15], totals[16], totals[17], totals[18])
```

```python
import functools

import jax
import jax.numpy as jnp
from jax import lax
from jax.experimental import pallas as pl
from jax.experimental.pallas import tpu as pltpu
from jax.sharding import PartitionSpec as P

HD = 64
EPSILON = 1e-05
F32 = jnp.float32
BF16 = jnp.bfloat16
NEG = -1e30
PX = 2
LOCAL = (0, PX, 1, 1 ^ PX)
VMEM_LIMIT = 60 * 1024 * 1024


def nn(a, b):
    return lax.dot_general(a, b, (((1,), (0,)), ((), ())), preferred_element_type=F32)


def nt(a, b):
    return lax.dot_general(a, b, (((1,), (1,)), ((), ())), preferred_element_type=F32)


def tn(a, b):
    return lax.dot_general(a, b, (((0,), (0,)), ((), ())), preferred_element_type=F32)


VM = pl.BlockSpec(memory_space=pltpu.VMEM)
SM = pl.BlockSpec(memory_space=pltpu.SMEM)


def call(body, outs, args, smem=0, scratch=(), flops=0, nbytes=None, name=None, aliases=None):
    if nbytes is None:
        nbytes = sum(a.size * a.dtype.itemsize for a in args) + sum(
            o.size * o.dtype.itemsize for o in outs
        )
    return pl.pallas_call(
        body,
        out_shape=tuple(outs),
        in_specs=[SM] * smem + [VM] * (len(args) - smem),
        out_specs=tuple([VM] * len(outs)),
        scratch_shapes=list(scratch),
        compiler_params=pltpu.CompilerParams(vmem_limit_bytes=VMEM_LIMIT),
        cost_estimate=pl.CostEstimate(flops=flops, bytes_accessed=nbytes, transcendentals=0),
        name=name,
        input_output_aliases=aliases or {},
    )(*args)


def sds(shape, dtype):
    return jax.ShapeDtypeStruct(shape, dtype)


def norm_unit(values):
    centred = values - jnp.mean(values, axis=-1, keepdims=True)
    spread = jnp.mean(centred * centred, axis=-1, keepdims=True)
    inverse = lax.rsqrt(spread + EPSILON)
    return centred * inverse, inverse


def sigmoid(v):
    return 1.0 / (1.0 + jnp.exp(-v))


C0 = 0.7978845608028654
C1 = 0.044715


def gelu_parts(u):
    square = u * u
    t = jnp.tanh(C0 * u * (1.0 + C1 * square))
    half = 0.5 * (1.0 + t)
    value = u * half
    slope = half + (0.5 * C0) * u * (1.0 - t * t) * (1.0 + (3.0 * C1) * square)
    return value, slope


def attend_query_block(qb, tb, segs, segv, qz, k, vt, p_ref, ot_ref, invl_ref, s_sc, m_sc, l_sc, o_sc, segc):
    rows = 256
    tq = tb[qb]
    m_sc[...] = jnp.full(m_sc.shape, NEG, F32)
    l_sc[...] = jnp.zeros(l_sc.shape, F32)
    o_sc[...] = jnp.zeros(o_sc.shape, F32)
    seg_q = segv[tq].astype(F32)

    def active(kb):
        tk = tb[kb]
        return (tk <= tq) & (segs[tk, 0, rows - 1] >= segs[tq, 0, 0])

    @pl.loop(0, 4)
    def _(kb):
        @pl.when(active(kb))
        def _():
            tk = tb[kb]
            krows = pl.ds(pl.multiple_of(kb * rows, rows), rows)
            kpos = tk * rows + lax.broadcasted_iota(jnp.int32, (rows, rows), 0)
            qpos = tq * rows + lax.broadcasted_iota(jnp.int32, (rows, rows), 1)
            seg_k = segc[pl.ds(pl.multiple_of(tk * rows, rows), rows), 0:1]
            bias = jnp.where((kpos <= qpos) & (seg_k == seg_q), 0.0, NEG)
            for h in range(4):
                pair = 128 * (h // 2)
                s = nn(k[krows, pair : pair + 128], qz[h]) + bias
                s_sc[h, krows, :] = s
                m_sc[h] = jnp.maximum(m_sc[h], jnp.max(s.reshape(rows // 8, 8, rows), axis=0))

    for h in range(4):
        m_sc[h] = jnp.broadcast_to(jnp.max(m_sc[h], axis=0, keepdims=True), (8, rows))

    @pl.loop(0, 4)
    def _(kb):
        @pl.when(active(kb))
        def _():
            krows = pl.ds(pl.multiple_of(kb * rows, rows), rows)
            for h in range(4):
                e = jnp.exp(s_sc[h, krows, :] - m_sc[h, 0:1, :])
                l_sc[h] = l_sc[h] + jnp.sum(e.reshape(rows // 8, 8, rows), axis=0)
                pb = e.astype(BF16)
                p_ref[h, krows, :] = pb
                o_sc[h] = o_sc[h] + nn(vt[64 * h : 64 * h + 64, krows], pb)

    for h in range(4):
        invl = 1.0 / jnp.sum(l_sc[h], axis=0, keepdims=True)
        invl_ref[h] = jnp.broadcast_to(invl, (8, rows))
        ot_ref[64 * h : 64 * h + 64, :] = (o_sc[h] * invl).astype(BF16)


def fill_qz(qz, qt):
    zero = jnp.zeros((64, 256), BF16)
    for h in range(4):
        mine = qt[64 * h : 64 * h + 64, :]
        qz[h] = jnp.concatenate([mine, zero] if h % 2 == 0 else [zero, mine], axis=0)


def fill_segc(segc, segv):
    for t in range(4):
        row = jnp.broadcast_to(segv[t].astype(F32), (128, 256))
        segc[256 * t : 256 * t + 256, :] = row.T


def first_kernel(
    tb, segs, segv, x0, x1, x2, x3, vecs, qkv0, qkv1,
    n_ref, qt0_ref, qt1_ref, k_ref, vt_ref, p_ref, ot_ref, att_ref, invl_ref,
    qz, s_sc, m_sc, l_sc, o_sc, segc,
):
    for i, x in enumerate((x0, x1, x2, x3)):
        unit, _ = norm_unit(x[...].astype(F32))
        n_ref[256 * i : 256 * i + 256, :] = (unit * vecs[0:1, :] + vecs[1:2, :]).astype(BF16)
    n = n_ref[...]
    for c, w in enumerate((qkv0, qkv1)):
        cols = slice(128 * c, 128 * c + 128)
        q = nn(n[0:512], w[0:512, 0:128]) + w[512:513, 0:128].astype(F32)
        qt = (q.astype(BF16).astype(F32) * HD ** (-0.5)).T.astype(BF16)
        qt0_ref[cols, :] = qt[:, 0:256]
        qt1_ref[cols, :] = qt[:, 256:512]
        k_ref[:, cols] = nn(n, w[0:512, 128:256]).astype(BF16)
        v = nn(n, w[0:512, 256:384]) + w[512:513, 256:384].astype(F32)
        vt_ref[cols, :] = v.T.astype(BF16)
    fill_segc(segc, segv)
    fill_qz(qz, qt1_ref)
    attend_query_block(1, tb, segs, segv, qz, k_ref, vt_ref, p_ref, ot_ref, invl_ref, s_sc, m_sc, l_sc, o_sc, segc)
    att_ref[...] = ot_ref[...].astype(F32).T.astype(BF16)


def second_kernel(
    tb, segs, segv, qt0, k, vt,
    p_ref, ot_ref, att_ref, invl_ref,
    qz, s_sc, m_sc, l_sc, o_sc, segc,
):
    fill_segc(segc, segv)
    fill_qz(qz, qt0)
    attend_query_block(0, tb, segs, segv, qz, k, vt, p_ref, ot_ref, invl_ref, s_sc, m_sc, l_sc, o_sc, segc)
    att_ref[...] = ot_ref[...].astype(F32).T.astype(BF16)


ATT_SCRATCH = (
    pltpu.VMEM((4, 128, 256), BF16),
    pltpu.VMEM((4, 1024, 256), F32),
    pltpu.VMEM((4, 8, 256), F32),
    pltpu.VMEM((4, 8, 256), F32),
    pltpu.VMEM((4, 64, 256), F32),
    pltpu.VMEM((1024, 128), F32),
)


def gather_gate(tb, pieces, start, scratch):
    for i, piece in enumerate(pieces):
        scratch[pl.ds(pl.multiple_of(tb[i] * 128, 128), 128), :] = piece[start : start + 128, :]


def out_kernel(
    tb, x0, n, att, attp, vecs, e0, e1, e2, e3,
    n2_ref, mid_ref, branch_ref, gate_ref,
    gw,
):
    gather_gate(tb, (e0, e1, e2, e3), 128, gw)
    branch = nn(att[:, 0:128], e0[0:128, :]) + nn(att[:, 128:256], e2[0:128, :])
    branch = branch + nn(attp[:, 0:128], e1[0:128, :]) + nn(attp[:, 128:256], e3[0:128, :])
    branch = branch + vecs[2:3, :]
    gate = sigmoid(nn(n[0:256, :], gw[...]) + vecs[3:4, :])
    middle = x0[...].astype(F32) + gate * branch
    unit, _ = norm_unit(middle)
    n2_ref[...] = (unit * vecs[4:5, :] + vecs[5:6, :]).astype(BF16)
    mid_ref[...] = middle
    branch_ref[...] = branch
    gate_ref[...] = gate


def ffn_kernel(
    tb, n2, mid, ct, vecs, f0, f1, f2, f3,
    out_ref, fg_ref, ltg_ref, hid_ref, slope_ref,
    gw,
):
    gather_gate(tb, (f0, f1, f2, f3), 1024, gw)
    n2v = n2[...]
    total = jnp.zeros((256, 512), F32)
    for i, f in enumerate((f0, f2, f1, f3)):
        u = nn(n2v, f[0:512, :]) + f[1152:1153, :].astype(F32)
        value, slope = gelu_parts(u)
        value = value.astype(BF16)
        hid_ref[:, 512 * i : 512 * i + 512] = value
        slope_ref[:, 512 * i : 512 * i + 512] = slope.astype(BF16)
        total = total + nn(value, f[512:1024, :])
    ffn = total + vecs[6:7, :]
    gate = sigmoid(nn(n2v, gw[...]) + vecs[7:8, :])
    up = ct[...].astype(F32)
    out_ref[...] = (mid[...] + gate * ffn).astype(BF16)
    fg_ref[...] = (gate * up).astype(BF16)
    ltg_ref[...] = (up * ffn * (gate * (1.0 - gate))).astype(BF16)


def back_kernel(
    tb, fg, ltg, slope, mid, branch, gate, ct, vecs, f0, f1, f2, f3, e0, e1, e2, e3,
    dot_ref, dotp_ref, mg_ref, bg_ref, log_ref, hg_ref, sums_ref,
    gw,
):
    gather_gate(tb, (f0, f1, f2, f3), 1024, gw)
    fgv = fg[...]
    ltgv = ltg[...]
    ng = nt(ltgv, gw[...])
    for i, f in enumerate((f0, f2, f1, f3)):
        hg = nt(fgv, f[512:1024, :]) * slope[:, 512 * i : 512 * i + 512].astype(F32)
        hg = hg.astype(BF16)
        if i < 2:
            hg_ref[:, 512 * i : 512 * i + 512] = hg
        ng = ng + nt(hg, f[0:512, :])
    unit, inverse = norm_unit(mid[...])
    g = ng * vecs[4:5, :]
    back = inverse * (g - jnp.mean(g, axis=-1, keepdims=True) - unit * jnp.mean(g * unit, axis=-1, keepdims=True))
    mg = ct[...].astype(F32) + back
    mg_ref[...] = mg
    gatev = gate[...]
    bg = (gatev * mg).astype(BF16)
    log = (mg * branch[...] * (gatev * (1.0 - gatev))).astype(BF16)
    bg_ref[...] = bg
    log_ref[...] = log
    dot_ref[0:128, :] = nt(e0[0:128, :], bg).astype(BF16)
    dot_ref[128:256, :] = nt(e2[0:128, :], bg).astype(BF16)
    dotp_ref[0:128, :] = nt(e1[0:128, :], bg).astype(BF16)
    dotp_ref[128:256, :] = nt(e3[0:128, :], bg).astype(BF16)
    rows = [fgv.astype(F32), ltgv.astype(F32), bg.astype(F32), log.astype(F32), ng * unit, ng]
    sums_ref[...] = jnp.zeros((8, 512), F32)
    for i, r in enumerate(rows):
        sums_ref[i : i + 1, :] = jnp.sum(r, axis=0, keepdims=True)


def ffn_weight_kernel(
    n2, n2p, fg, fgp, hid, hg, f0, f2,
    keep_ref, send_ref,
):
    n2v, n2pv, fgv, fgpv = n2[...], n2p[...], fg[...], fgp[...]
    for i, f in enumerate((f0, f2)):
        cols = slice(512 * i, 512 * i + 512)
        u = nn(n2pv, f[0:512, :]) + f[1152:1153, :].astype(F32)
        value, slope = gelu_parts(u)
        hidp = value.astype(BF16)
        hgp = (nt(fgpv, f[512:1024, :]) * slope).astype(BF16)
        hgo = hg[:, cols]
        win = tn(n2v, hgo) + tn(n2pv, hgp)
        wback = tn(hid[:, cols], fgv) + tn(hidp, fgpv)
        bias = jnp.sum(hgo.astype(F32), axis=0, keepdims=True) + jnp.sum(hgp.astype(F32), axis=0, keepdims=True)
        dst = keep_ref if i == 0 else send_ref
        dst[0:512, :] = win.astype(dst.dtype)
        dst[512:1024, :] = wback.astype(dst.dtype)
        dst[1024:1032, :] = jnp.broadcast_to(bias, (8, 512)).astype(dst.dtype)


def small_weight_kernel(
    tb, n, n2, ltg, log, att, attp, bg,
    keep_ref, send_ref,
    g1, g2,
):
    g2[...] = tn(n2[...], ltg[...])
    g1[...] = tn(n[0:256, :], log[...])
    bgv = bg[...]
    wo = (tn(att[:, 0:128], bgv), tn(attp[:, 0:128], bgv), tn(att[:, 128:256], bgv), tn(attp[:, 128:256], bgv))
    for i in range(4):
        src = pl.ds(pl.multiple_of(tb[i] * 128, 128), 128)
        dst = keep_ref if i < 2 else send_ref
        base = 384 * (i % 2)
        dst[base : base + 128, :] = g2[src, :].astype(dst.dtype)
        dst[base + 128 : base + 256, :] = g1[src, :].astype(dst.dtype)
        dst[base + 256 : base + 384, :] = wo[i].astype(dst.dtype)


def prepare_kernel(n, k, qkv0, qkv1, v_ref, kt_ref):
    nv = n[...]
    for c, w in enumerate((qkv0, qkv1)):
        v = nn(nv, w[0:512, 256:384]) + w[512:513, 256:384].astype(F32)
        v_ref[:, 128 * c : 128 * c + 128] = v.astype(BF16)
    kt_ref[...] = k[...].astype(F32).T.astype(BF16)


def attend_back(qb, tb, segs, p, dot, ot, invl, qt, kt, v, dk, dv, dq, doz, dos, dlt):
    rows = 256
    tq = tb[qb]
    zero = jnp.zeros((64, rows), BF16)
    for h in range(4):
        hs = slice(64 * h, 64 * h + 64)
        scale = invl[h, 0:1, :]
        dv_h = dot[hs, :].astype(F32)
        delta = jnp.sum(dv_h * ot[hs, :].astype(F32), axis=0, keepdims=True) * scale
        dlt[h] = jnp.broadcast_to(delta, (8, rows))
        mine = (dv_h * scale).astype(BF16)
        dos[hs, :] = mine
        doz[h] = jnp.concatenate([mine, zero] if h % 2 == 0 else [zero, mine], axis=0)
    dq[...] = jnp.zeros(dq.shape, F32)

    @pl.loop(0, 4)
    def _(kb):
        tk = tb[kb]

        @pl.when((tk <= tq) & (segs[tk, 0, rows - 1] >= segs[tq, 0, 0]))
        def _():
            ks = pl.ds(pl.multiple_of(kb * rows, rows), rows)
            for h in range(4):
                pair = 128 * (h // 2)
                hs = slice(64 * h, 64 * h + 64)
                ph = p[h, ks, :]
                dp = nn(v[ks, pair : pair + 128], doz[h])
                ds = (ph.astype(F32) * (dp - dlt[h, 0:1, :])).astype(BF16)
                dv[hs, ks] = dv[hs, ks] + nt(dos[hs, :], ph)
                dk[hs, ks] = dk[hs, ks] + nt(qt[hs, :], ds)
                dq[hs, :] = dq[hs, :] + nn(kt[hs, ks], ds)


def back_first_kernel(
    tb, segs, p, dot, ot, invl, qt, kt, v,
    dk_ref, dv_ref, dq_ref,
    dq, doz, dos, dlt,
):
    dk_ref[...] = jnp.zeros(dk_ref.shape, F32)
    dv_ref[...] = jnp.zeros(dv_ref.shape, F32)
    attend_back(0, tb, segs, p, dot, ot, invl, qt, kt, v, dk_ref, dv_ref, dq, doz, dos, dlt)
    dq_ref[...] = (dq[...] * HD ** (-0.5)).astype(BF16)


def back_second_kernel(
    tb, segs, p, dot, ot, invl, qt, kt, v, dk0, dv0, dq0, n,
    dqt_ref, dkt_ref, dvt_ref, keep_ref, send_ref, bias_ref,
    dk, dv, dq, doz, dos, dlt,
):
    dk[...] = dk0[...]
    dv[...] = dv0[...]
    attend_back(1, tb, segs, p, dot, ot, invl, qt, kt, v, dk, dv, dq, doz, dos, dlt)
    dqt_ref[:, 0:256] = dq0[...]
    dqt_ref[:, 256:512] = (dq[...] * HD ** (-0.5)).astype(BF16)
    dkt_ref[...] = dk[...].astype(BF16)
    dvt_ref[...] = dv[...].astype(BF16)
    nv = n[...]
    wq = nn(dqt_ref[...], nv[0:512, :])
    wk = nn(dkt_ref[...], nv)
    wv = nn(dvt_ref[...], nv)
    for i, w in enumerate((wq, wk, wv)):
        keep_ref[128 * i : 128 * i + 128, :] = w[0:128, :]
        send_ref[128 * i : 128 * i + 128, :] = w[128:256, :].astype(BF16)
    ones_q = jnp.ones((8, 512), BF16)
    ones_v = jnp.ones((8, 1024), BF16)
    bias_ref[:, 0:256] = nt(ones_q, dqt_ref[...])
    bias_ref[:, 256:512] = nt(ones_v, dvt_ref[...])


def input_kernel(dqt, dkt, dvt, qkv0, qkv1, own_ref, par_ref, send_ref):
    def weight(part):
        cols = slice(128 * part, 128 * part + 128)
        return jnp.concatenate([qkv0[0:512, cols], qkv1[0:512, cols]], axis=1)

    wk, wv = weight(1), weight(2)
    g = nn(wk, dkt[...]) + nn(wv, dvt[...])
    send_ref[...] = g[:, 512:1024].astype(BF16)
    g0 = g[:, 0:512] + nn(weight(0), dqt[...])
    own_ref[...] = g0[:, 0:256]
    par_ref[...] = g0[:, 256:512]


def last_kernel(tb, own, sib, par, x0, mg, log, vecs, e0, e1, e2, e3, grad_ref, sums_ref, gw):
    gather_gate(tb, (e0, e1, e2, e3), 128, gw)
    total = own[...] + sib[:, 0:256].astype(F32) + par[...].astype(F32)
    ng = total.T + nt(log[...], gw[...])
    unit, inverse = norm_unit(x0[...].astype(F32))
    g = ng * vecs[0:1, :]
    back = inverse * (g - jnp.mean(g, axis=-1, keepdims=True) - unit * jnp.mean(g * unit, axis=-1, keepdims=True))
    grad_ref[...] = mg[...] + back
    sums_ref[...] = jnp.zeros((8, 512), F32)
    sums_ref[0:1, :] = jnp.sum(ng * unit, axis=0, keepdims=True)
    sums_ref[1:2, :] = jnp.sum(ng, axis=0, keepdims=True)


def body(
    layer_input, segments, norm1_gain, norm1_bias, w_query, b_query, w_key, w_value, b_value,
    w_out, b_out, gate1_w, gate1_b, norm2_gain, norm2_bias, w_in, b_in, w_back, b_back,
    gate2_w, gate2_b, cotangent, *, n_dp,
):
    def hop(value, mask):
        return lax.ppermute(value, "tensor", [(i, i ^ mask) for i in range(4)])

    t = lax.axis_index("tensor").astype(jnp.int32)
    tb = t ^ jnp.array(LOCAL, jnp.int32)
    seg = segments.reshape(4, 1, 256)
    x0 = layer_input
    x1 = hop(x0, PX)
    x2 = hop(x0, 1)
    x3 = hop(x1, 1)
    zero128 = jnp.zeros((128,), BF16)
    row_qkv = jnp.concatenate([b_query, zero128, b_value])[None]
    qkv0 = jnp.concatenate(
        [jnp.concatenate([w_query, w_key, w_value], axis=1), row_qkv, jnp.zeros((7, 384), BF16)], axis=0
    )
    qkv1 = hop(qkv0, 1)
    e0 = jnp.concatenate([w_out, gate1_w], axis=0)
    f0 = jnp.concatenate([w_in, w_back, gate2_w, b_in[None], jnp.zeros((7, 512), BF16)], axis=0)
    e2 = hop(e0, 1)
    f2 = hop(f0, 1)
    x1b, e0b, f0b = lax.optimization_barrier((x1, e0, f0))
    e1 = hop(e0b, PX)
    e3 = hop(e1, 1)
    f1 = hop(f0b, PX)
    f3 = hop(f1, 1)
    vecs = jnp.stack(
        [norm1_gain, norm1_bias, b_out, gate1_b, norm2_gain, norm2_bias, b_back, gate2_b]
    ).astype(F32)

    n, qt0, qt1, k, vt, p1, ot1, att1, invl1 = call(
        first_kernel,
        [
            sds((1024, 512), BF16), sds((256, 256), BF16), sds((256, 256), BF16), sds((1024, 256), BF16),
            sds((256, 1024), BF16), sds((4, 1024, 256), BF16), sds((256, 256), BF16), sds((256, 256), BF16),
            sds((4, 8, 256), F32),
        ],
        [tb, seg, seg, x0, x1b, x2, x3, vecs, qkv0, qkv1],
        smem=2, scratch=ATT_SCRATCH, flops=2_000_000_000, name="first",
    )
    attp = hop(att1, PX)
    p0, ot0, att0, invl0 = call(
        second_kernel,
        [sds((4, 1024, 256), BF16), sds((256, 256), BF16), sds((256, 256), BF16), sds((4, 8, 256), F32)],
        [tb, seg, seg, qt0, k, vt],
        smem=2, scratch=ATT_SCRATCH, flops=2_000_000_000, name="second",
    )
    n2, mid, branch, gate = call(
        out_kernel,
        [sds((256, 512), BF16), sds((256, 512), F32), sds((256, 512), F32), sds((256, 512), F32)],
        [tb, x0, n, att0, attp, vecs, e0, e1, e2, e3],
        smem=1, scratch=[pltpu.VMEM((512, 512), BF16)], flops=270_000_000, name="out",
    )
    n2p = hop(n2, PX)
    result, fg, ltg, hid, slope = call(
        ffn_kernel,
        [
            sds((256, 512), BF16), sds((256, 512), BF16), sds((256, 512), BF16), sds((256, 2048), BF16),
            sds((256, 2048), BF16),
        ],
        [tb, n2, mid, cotangent, vecs, f0, f1, f2, f3],
        smem=1, scratch=[pltpu.VMEM((512, 512), BF16)], flops=1_200_000_000, name="ffn",
    )
    fgp = hop(fg, PX)
    dot0, dotp, mg, bg, log, hg, sums = call(
        back_kernel,
        [
            sds((256, 256), BF16), sds((256, 256), BF16), sds((256, 512), F32), sds((256, 512), BF16),
            sds((256, 512), BF16), sds((256, 1024), BF16), sds((8, 512), F32),
        ],
        [tb, fg, ltg, slope, mid, branch, gate, cotangent, vecs, f0, f1, f2, f3, e0, e1, e2, e3],
        smem=1, scratch=[pltpu.VMEM((512, 512), BF16)], flops=1_400_000_000, name="back",
    )
    dot1 = hop(dotp, PX)
    fkeep, fsend = call(
        ffn_weight_kernel,
        [sds((1032, 512), F32), sds((1032, 512), BF16)],
        [n2, n2p, fg, fgp, hid, hg, f0, f2],
        flops=1_600_000_000, name="ffn_weight",
    )
    frecv = hop(fsend, 1)
    fsum = fkeep + frecv.astype(F32)
    skeep, ssend = call(
        small_weight_kernel,
        [sds((768, 512), F32), sds((768, 512), BF16)],
        [tb, n, n2, ltg, log, att0, attp, bg],
        smem=1, scratch=[pltpu.VMEM((512, 512), F32), pltpu.VMEM((512, 512), F32)],
        flops=400_000_000, name="small_weight",
    )
    srecv = hop(ssend, 1)
    ssum = skeep + srecv.astype(F32)
    spar = hop(ssum[384:768].astype(BF16), PX)
    stot = (ssum[0:384] + spar.astype(F32)).astype(BF16)
    sums = sums + hop(sums, 1)
    sums = sums + hop(sums, PX)

    v, kt = call(
        prepare_kernel, [sds((1024, 256), BF16), sds((256, 1024), BF16)], [n, k, qkv0, qkv1],
        flops=270_000_000, name="prepare",
    )
    back_scratch = [
        pltpu.VMEM((256, 256), F32), pltpu.VMEM((4, 128, 256), BF16), pltpu.VMEM((256, 256), BF16),
        pltpu.VMEM((4, 8, 256), F32),
    ]
    dk0, dv0, dq0 = call(
        back_first_kernel,
        [sds((256, 1024), F32), sds((256, 1024), F32), sds((256, 256), BF16)],
        [tb, seg, p0, dot0, ot0, invl0, qt0, kt, v],
        smem=2, scratch=back_scratch, flops=2_000_000_000, name="attn_back0",
    )
    dqt, dkt, dvt, akeep, asend, abias = call(
        back_second_kernel,
        [
            sds((256, 512), BF16), sds((256, 1024), BF16), sds((256, 1024), BF16), sds((384, 512), F32),
            sds((384, 512), BF16), sds((8, 512), F32),
        ],
        [tb, seg, p1, dot1, ot1, invl1, qt1, kt, v, dk0, dv0, dq0, n],
        smem=2, scratch=[pltpu.VMEM((256, 1024), F32), pltpu.VMEM((256, 1024), F32)] + back_scratch,
        flops=2_500_000_000, name="attn_back1",
    )
    arecv = hop(asend, 1)
    asum = (akeep + arecv.astype(F32)).astype(BF16)
    bq_s = abias[0, 128:256]
    bv_s = abias[0, 384:512]
    brecv = hop(jnp.concatenate([bq_s, bv_s])[None], 1)[0]
    bq = abias[0, 0:128] + brecv[0:128]
    bv = abias[0, 256:384] + brecv[128:256]
    gown, gpar, gsend = call(
        input_kernel,
        [sds((512, 256), F32), sds((512, 256), F32), sds((512, 512), BF16)],
        [dqt, dkt, dvt, qkv0, qkv1],
        flops=700_000_000, name="input_grad",
    )
    gsib = hop(gsend, 1)
    gp = hop((gpar + gsib[:, 256:512].astype(F32)).astype(BF16), PX)
    input_grad, sums1 = call(
        last_kernel,
        [sds((256, 512), F32), sds((8, 512), F32)],
        [tb, gown, gsib, gp, x0, mg, log, vecs, e0, e1, e2, e3],
        smem=1, scratch=[pltpu.VMEM((512, 512), BF16)], flops=140_000_000, name="last",
    )
    sums1 = sums1 + hop(sums1, 1)
    sums1 = sums1 + hop(sums1, PX)

    def scatter(matrix):
        pieces = matrix.astype(BF16).reshape(n_dp, -1, 512)
        got = lax.all_to_all(pieces, "dp", 0, 0, tiled=True)
        return jnp.sum(got.astype(F32), axis=0).astype(BF16)

    def gather(piece, small):
        rows = piece.shape[0]
        both = jnp.concatenate([piece, small.astype(BF16)], axis=0)
        got = lax.all_to_all(jnp.broadcast_to(both[None], (n_dp,) + both.shape), "dp", 0, 0, tiled=True)
        return (
            got[:, :rows].astype(F32).reshape(n_dp * rows, 512),
            jnp.sum(got[:, rows:].astype(F32), axis=0),
        )

    small_f = jnp.concatenate([sums[0:6], fsum[1024:1025], jnp.zeros((1, 512), F32)], axis=0)
    f_all, f_small = gather(scatter(fsum[0:1024]), small_f)
    s_all, s_small = gather(scatter(stot), jnp.zeros((8, 512), F32))
    small_a = jnp.concatenate(
        [sums1[0:2], jnp.concatenate([bq, bv, jnp.zeros((256,), F32)])[None], jnp.zeros((5, 512), F32)], axis=0
    )
    a_all, a_small = gather(scatter(asum), small_a)
    return (
        result,
        input_grad,
        a_small[0],
        a_small[1],
        a_all[0:128].T,
        a_small[2, 0:128],
        a_all[128:256].T,
        a_all[256:384].T,
        a_small[2, 128:256],
        s_all[256:384],
        f_small[2],
        s_all[128:256],
        f_small[3],
        f_small[4],
        f_small[5],
        f_all[0:512],
        f_small[6],
        f_all[512:1024],
        f_small[0],
        s_all[0:128],
        f_small[1],
    )


def solution(mesh):
    tok = P(("dp", "tensor"), None)
    col = P(None, "tensor")
    row = P("tensor", None)
    vec = P("tensor")
    rep = P()
    return jax.shard_map(
        functools.partial(body, n_dp=mesh.shape["dp"]),
        mesh=mesh,
        in_specs=(
            tok, P("dp", None), rep, rep, col, vec, col, col, vec, row, rep, row, rep, rep, rep,
            col, vec, row, rep, row, rep, tok,
        ),
        out_specs=(
            tok, tok, rep, rep, col, vec, col, col, vec, row, rep, row, rep, rep, rep,
            col, vec, row, rep, row, rep,
        ),
        check_vma=False,
    )
```

```python
import functools
import math

import jax
import jax.numpy as jnp
from jax import lax
from jax.experimental import pallas as pl
from jax.experimental.pallas import tpu as pltpu
from jax.sharding import PartitionSpec as P

HD = 64
EPSILON = 1e-05
F32 = jnp.float32
BF16 = jnp.bfloat16
NEG = -1e30
PX = 2
LOCAL = (0, PX, 1, 1 ^ PX)
SPARE = 4 * 1024 * 1024


def nn(a, b):
    return lax.dot_general(a, b, (((1,), (0,)), ((), ())), preferred_element_type=F32)


def nt(a, b):
    return lax.dot_general(a, b, (((1,), (1,)), ((), ())), preferred_element_type=F32)


def tn(a, b):
    return lax.dot_general(a, b, (((0,), (0,)), ((), ())), preferred_element_type=F32)


VM = pl.BlockSpec(memory_space=pltpu.VMEM)
SM = pl.BlockSpec(memory_space=pltpu.SMEM)


def call(body, outs, args, smem=0, scratch=(), name=None, space=VM, limit=None):
    nbytes = sum(a.size * a.dtype.itemsize for a in args) + sum(o.size * o.dtype.itemsize for o in outs)
    held = sum(math.prod(s.shape) * 4 for s in scratch)
    limit = limit or nbytes + held + SPARE
    return pl.pallas_call(
        body,
        out_shape=tuple(outs),
        in_specs=[SM] * smem + [space] * (len(args) - smem),
        out_specs=tuple([VM] * len(outs)),
        scratch_shapes=list(scratch),
        compiler_params=pltpu.CompilerParams(vmem_limit_bytes=limit),
        cost_estimate=pl.CostEstimate(flops=0, bytes_accessed=0, transcendentals=0),
        name=name,
    )(*args)


def sds(shape, dtype):
    return jax.ShapeDtypeStruct(shape, dtype)


def norm_unit(values):
    centred = values - jnp.mean(values, axis=-1, keepdims=True)
    spread = jnp.mean(centred * centred, axis=-1, keepdims=True)
    inverse = lax.rsqrt(spread + EPSILON)
    return centred * inverse, inverse


def sigmoid(v):
    return 1.0 / (1.0 + jnp.exp(-v))


C0 = 0.7978845608028654
C1 = 0.044715


def gelu_parts(u):
    square = u * u
    t = jnp.tanh(C0 * u * (1.0 + C1 * square))
    half = 0.5 * (1.0 + t)
    value = u * half
    slope = half + (0.5 * C0) * u * (1.0 - t * t) * (1.0 + (3.0 * C1) * square)
    return value, slope


def attend_query_block(qb, tb, segs, segv, qz, k, vt, p_ref, ot_ref, invl_ref, s_sc, m_sc, l_sc, o_sc, segc):
    rows = 256
    tq = tb[qb]
    m_sc[...] = jnp.full(m_sc.shape, NEG, F32)
    l_sc[...] = jnp.zeros(l_sc.shape, F32)
    o_sc[...] = jnp.zeros(o_sc.shape, F32)
    seg_q = segv[0:1, pl.ds(pl.multiple_of(tq * rows, rows), rows)].astype(F32)

    def active(kb):
        tk = tb[kb]
        return (tk <= tq) & (segs[0, tk * rows + rows - 1] >= segs[0, tq * rows])

    @pl.loop(0, 4)
    def _(kb):
        @pl.when(active(kb))
        def _():
            tk = tb[kb]
            krows = pl.ds(pl.multiple_of(kb * rows, rows), rows)
            kpos = tk * rows + lax.broadcasted_iota(jnp.int32, (rows, rows), 0)
            qpos = tq * rows + lax.broadcasted_iota(jnp.int32, (rows, rows), 1)
            seg_k = segc[pl.ds(pl.multiple_of(tk * rows, rows), rows), 0:1]
            bias = jnp.where((kpos <= qpos) & (seg_k == seg_q), 0.0, NEG)
            for h in range(4):
                pair = 128 * (h // 2)
                s = nn(k[krows, pair : pair + 128], qz[h]) + bias
                s_sc[h, krows, :] = s
                m_sc[h] = jnp.maximum(m_sc[h], jnp.max(s.reshape(rows // 8, 8, rows), axis=0))

    for h in range(4):
        m_sc[h] = jnp.broadcast_to(jnp.max(m_sc[h], axis=0, keepdims=True), (8, rows))

    @pl.loop(0, 4)
    def _(kb):
        @pl.when(active(kb))
        def _():
            krows = pl.ds(pl.multiple_of(kb * rows, rows), rows)
            for h in range(4):
                e = jnp.exp(s_sc[h, krows, :] - m_sc[h, 0:1, :])
                l_sc[h] = l_sc[h] + jnp.sum(e.reshape(rows // 8, 8, rows), axis=0)
                pb = e.astype(BF16)
                p_ref[h, krows, :] = pb
                o_sc[h] = o_sc[h] + nn(vt[64 * h : 64 * h + 64, krows], pb)

    for h in range(4):
        invl = 1.0 / jnp.sum(l_sc[h], axis=0, keepdims=True)
        invl_ref[h] = jnp.broadcast_to(invl, (8, rows))
        ot_ref[64 * h : 64 * h + 64, :] = (o_sc[h] * invl).astype(BF16)


def fill_qz(qz, qt):
    zero = jnp.zeros((64, 256), BF16)
    for h in range(4):
        mine = qt[64 * h : 64 * h + 64, :]
        qz[h] = jnp.concatenate([mine, zero] if h % 2 == 0 else [zero, mine], axis=0)


def fill_segc(segc, segv):
    for t in range(4):
        row = jnp.broadcast_to(segv[0:1, 256 * t : 256 * t + 256].astype(F32), (128, 256))
        segc[256 * t : 256 * t + 256, :] = row.T


def first_kernel(
    tb, segs, segv, x0, x1, x2, x3, vecs, qkv0, qkv1,
    n_ref, qt0_ref, qt1_ref, k_ref, vt_ref, p_ref, ot_ref, att_ref, invl_ref,
    qz, s_sc, m_sc, l_sc, o_sc, segc,
):
    for i, x in enumerate((x0, x1, x2, x3)):
        unit, _ = norm_unit(x[...].astype(F32))
        n_ref[256 * i : 256 * i + 256, :] = (unit * vecs[0:1, :] + vecs[1:2, :]).astype(BF16)
    n = n_ref[...]
    for c, w in enumerate((qkv0, qkv1)):
        cols = slice(128 * c, 128 * c + 128)
        q = nn(n[0:512], w[0:512, 0:128]) + w[512:513, 0:128].astype(F32)
        qt = (q.astype(BF16).astype(F32) * HD ** (-0.5)).T.astype(BF16)
        qt0_ref[cols, :] = qt[:, 0:256]
        qt1_ref[cols, :] = qt[:, 256:512]
        k_ref[:, cols] = nn(n, w[0:512, 128:256]).astype(BF16)
        v = nn(n, w[0:512, 256:384]) + w[512:513, 256:384].astype(F32)
        vt_ref[cols, :] = v.T.astype(BF16)
    fill_segc(segc, segv)
    fill_qz(qz, qt1_ref)
    attend_query_block(1, tb, segs, segv, qz, k_ref, vt_ref, p_ref, ot_ref, invl_ref, s_sc, m_sc, l_sc, o_sc, segc)
    att_ref[...] = ot_ref[...].astype(F32).T.astype(BF16)


def second_kernel(
    tb, segs, segv, qt0, k, vt,
    p_ref, ot_ref, att_ref, invl_ref,
    qz, s_sc, m_sc, l_sc, o_sc, segc,
):
    fill_segc(segc, segv)
    fill_qz(qz, qt0)
    attend_query_block(0, tb, segs, segv, qz, k, vt, p_ref, ot_ref, invl_ref, s_sc, m_sc, l_sc, o_sc, segc)
    att_ref[...] = ot_ref[...].astype(F32).T.astype(BF16)


ATT_SCRATCH = (
    pltpu.VMEM((4, 128, 256), BF16),
    pltpu.VMEM((4, 1024, 256), F32),
    pltpu.VMEM((4, 8, 256), F32),
    pltpu.VMEM((4, 8, 256), F32),
    pltpu.VMEM((4, 64, 256), F32),
    pltpu.VMEM((1024, 128), F32),
)


def gather_gate(tb, pieces, start, scratch):
    for i, piece in enumerate(pieces):
        scratch[pl.ds(pl.multiple_of(tb[i] * 128, 128), 128), :] = piece[start : start + 128, :]


def out_kernel(
    tb, x0, n, att, attp, vecs, e0, e1, e2, e3,
    n2_ref, mid_ref, branch_ref, gate_ref,
    gw,
):
    gather_gate(tb, (e0, e1, e2, e3), 128, gw)
    branch = nn(att[:, 0:128], e0[0:128, :]) + nn(att[:, 128:256], e2[0:128, :])
    branch = branch + nn(attp[:, 0:128], e1[0:128, :]) + nn(attp[:, 128:256], e3[0:128, :])
    branch = branch + vecs[2:3, :]
    gate = sigmoid(nn(n[0:256, :], gw[...]) + vecs[3:4, :])
    middle = x0[...].astype(F32) + gate * branch
    unit, _ = norm_unit(middle)
    n2_ref[...] = (unit * vecs[4:5, :] + vecs[5:6, :]).astype(BF16)
    mid_ref[...] = middle
    branch_ref[...] = branch
    gate_ref[...] = gate


def pair_up(a, b, start):
    return jnp.concatenate([a[start : start + 128, :], b[start : start + 128, :]], axis=0)


def pair_bias(a, b):
    return jnp.concatenate([a[256:257, 0:128], b[256:257, 0:128]], axis=1).astype(F32)


def ffn_first_kernel(
    tb, n2, vecs, win0, wback0, c2,
    total_ref, hid_ref, slope_ref,
):
    n2v = n2[...]
    total = jnp.zeros((256, 512), F32)
    for i, (b, w, wb) in enumerate(((vecs[8:9, :], win0[...], wback0[...]), (c2[384:385, :], c2[392:904, :], c2[904:1416, :]))):
        value, slope = gelu_parts(nn(n2v, w) + b.astype(F32))
        value = value.astype(BF16)
        hid_ref[:, 512 * i : 512 * i + 512] = value
        slope_ref[:, 512 * i : 512 * i + 512] = slope.astype(BF16)
        total = total + nn(value, wb)
    total_ref[...] = total


def ffn_kernel(
    tb, n2, mid, ct, vecs, e0, e1, e2, e3, total0, s0, s1, s2, s3, s4, s5, s6, s7,
    out_ref, fg_ref, ltg_ref, slope_ref,
    gw,
):
    gather_gate(tb, (e0, e1, e2, e3), 256, gw)
    n2v = n2[...]
    total = total0[...]
    for i, (a, b) in enumerate(((s0, s1), (s2, s3), (s4, s5), (s6, s7))):
        value, slope = gelu_parts(nt(n2v, pair_up(a, b, 0)) + pair_bias(a, b))
        slope_ref[:, 256 * i : 256 * i + 256] = slope.astype(BF16)
        total = total + nn(value.astype(BF16), pair_up(a, b, 128))
    ffn = total + vecs[6:7, :]
    gate = sigmoid(nn(n2v, gw[...]) + vecs[7:8, :])
    up = ct[...].astype(F32)
    out_ref[...] = (mid[...] + gate * ffn).astype(BF16)
    fg_ref[...] = (gate * up).astype(BF16)
    ltg_ref[...] = (up * ffn * (gate * (1.0 - gate))).astype(BF16)


def back_kernel(
    tb, fg, ltg, slope0, slope1, mid, branch, gate, ct, vecs, e0, e1, e2, e3,
    win0, wback0, s0, s1, s2, s3, s4, s5, s6, s7,
    dot_ref, dotp_ref, mg_ref, bg_ref, log_ref, hg_ref, sums_ref,
    gw,
):
    gather_gate(tb, (e0, e1, e2, e3), 256, gw)
    fgv = fg[...]
    ltgv = ltg[...]
    ng = nt(ltgv, gw[...])
    for i, (w, wb) in enumerate(((win0[...], wback0[...]), (e2[392:904, :], e2[904:1416, :]))):
        hg = (nt(fgv, wb) * slope0[:, 512 * i : 512 * i + 512].astype(F32)).astype(BF16)
        hg_ref[:, 512 * i : 512 * i + 512] = hg
        ng = ng + nt(hg, w)
    for i, (a, b) in enumerate(((s0, s1), (s2, s3), (s4, s5), (s6, s7))):
        hg = (nt(fgv, pair_up(a, b, 128)) * slope1[:, 256 * i : 256 * i + 256].astype(F32)).astype(BF16)
        ng = ng + nn(hg, pair_up(a, b, 0))
    unit, inverse = norm_unit(mid[...])
    g = ng * vecs[4:5, :]
    back = inverse * (g - jnp.mean(g, axis=-1, keepdims=True) - unit * jnp.mean(g * unit, axis=-1, keepdims=True))
    mg = ct[...].astype(F32) + back
    mg_ref[...] = mg
    gatev = gate[...]
    bg = (gatev * mg).astype(BF16)
    log = (mg * branch[...] * (gatev * (1.0 - gatev))).astype(BF16)
    bg_ref[...] = bg
    log_ref[...] = log
    dot_ref[0:128, :] = nt(e0[0:128, :], bg).astype(BF16)
    dot_ref[128:256, :] = nt(e2[0:128, :], bg).astype(BF16)
    dotp_ref[0:128, :] = nt(e1[0:128, :], bg).astype(BF16)
    dotp_ref[128:256, :] = nt(e3[0:128, :], bg).astype(BF16)
    rows = [fgv.astype(F32), ltgv.astype(F32), bg.astype(F32), log.astype(F32), ng * unit, ng]
    sums_ref[...] = jnp.zeros((8, 512), F32)
    for i, r in enumerate(rows):
        sums_ref[i : i + 1, :] = jnp.sum(r, axis=0, keepdims=True)


def ffn_back_weight_kernel(
    tb, n2p, fg, fgp, hid, vecs, win0, c2,
    keep_ref, send_ref, slope_ref,
):
    fgv, fgpv, n2pv = fg[...], fgp[...], n2p[...]
    for i, (b, w) in enumerate(((vecs[8:9, :], win0[...]), (c2[384:385, :], c2[392:904, :]))):
        cols = slice(512 * i, 512 * i + 512)
        value, slope = gelu_parts(nn(n2pv, w) + b.astype(F32))
        slope_ref[:, cols] = slope.astype(BF16)
        wback = tn(hid[:, cols], fgv) + tn(value.astype(BF16), fgpv)
        dst = keep_ref if i == 0 else send_ref
        dst[...] = wback.astype(dst.dtype)


def ffn_in_weight_kernel(
    tb, n2, n2p, fgp, hg, slope, wback0, c2,
    keep_ref, send_ref,
):
    n2v, n2pv, fgpv = n2[...], n2p[...], fgp[...]
    for i, wb in enumerate((wback0[...], c2[904:1416, :])):
        cols = slice(512 * i, 512 * i + 512)
        hgp = (nt(fgpv, wb) * slope[:, cols].astype(F32)).astype(BF16)
        hgo = hg[:, cols]
        win = tn(n2v, hgo) + tn(n2pv, hgp)
        bias = jnp.sum(hgo.astype(F32), axis=0, keepdims=True) + jnp.sum(hgp.astype(F32), axis=0, keepdims=True)
        dst = keep_ref if i == 0 else send_ref
        dst[0:512, :] = win.astype(dst.dtype)
        dst[512:520, :] = jnp.broadcast_to(bias, (8, 512)).astype(dst.dtype)


def small_weight_kernel(
    tb, n, n2, ltg, log, att, attp, bg, sums,
    keep_ref, send_ref,
    g1, g2,
):
    keep_ref[768:776, :] = sums[...]
    send_ref[768:776, :] = sums[...].astype(BF16)
    g2[...] = tn(n2[...], ltg[...])
    g1[...] = tn(n[0:256, :], log[...])
    bgv = bg[...]
    wo = (tn(att[:, 0:128], bgv), tn(attp[:, 0:128], bgv), tn(att[:, 128:256], bgv), tn(attp[:, 128:256], bgv))
    for i in range(4):
        src = pl.ds(pl.multiple_of(tb[i] * 128, 128), 128)
        dst = keep_ref if i < 2 else send_ref
        base = 384 * (i % 2)
        dst[base : base + 128, :] = g2[src, :].astype(dst.dtype)
        dst[base + 128 : base + 256, :] = g1[src, :].astype(dst.dtype)
        dst[base + 256 : base + 384, :] = wo[i].astype(dst.dtype)


def prepare_kernel(tb, n, k, qkv0, qkv1, v_ref, kt_ref):
    nv = n[...]
    for c, w in enumerate((qkv0, qkv1)):
        v = nn(nv, w[0:512, 256:384]) + w[512:513, 256:384].astype(F32)
        v_ref[:, 128 * c : 128 * c + 128] = v.astype(BF16)
    kt_ref[...] = k[...].astype(F32).T.astype(BF16)


def attend_back(qb, tb, segs, p, dot, ot, invl, qt, kt, v, dk, dv, dq, doz, dos, dlt):
    rows = 256
    tq = tb[qb]
    zero = jnp.zeros((64, rows), BF16)
    for h in range(4):
        hs = slice(64 * h, 64 * h + 64)
        scale = invl[h, 0:1, :]
        dv_h = dot[hs, :].astype(F32)
        delta = jnp.sum(dv_h * ot[hs, :].astype(F32), axis=0, keepdims=True) * scale
        dlt[h] = jnp.broadcast_to(delta, (8, rows))
        mine = (dv_h * scale).astype(BF16)
        dos[hs, :] = mine
        doz[h] = jnp.concatenate([mine, zero] if h % 2 == 0 else [zero, mine], axis=0)
    dq[...] = jnp.zeros(dq.shape, F32)

    @pl.loop(0, 4)
    def _(kb):
        tk = tb[kb]

        @pl.when((tk <= tq) & (segs[0, tk * rows + rows - 1] >= segs[0, tq * rows]))
        def _():
            ks = pl.ds(pl.multiple_of(kb * rows, rows), rows)
            for h in range(4):
                pair = 128 * (h // 2)
                hs = slice(64 * h, 64 * h + 64)
                ph = p[h, ks, :]
                dp = nn(v[ks, pair : pair + 128], doz[h])
                ds = (ph.astype(F32) * (dp - dlt[h, 0:1, :])).astype(BF16)
                dv[hs, ks] = dv[hs, ks] + nt(dos[hs, :], ph)
                dk[hs, ks] = dk[hs, ks] + nt(qt[hs, :], ds)
                dq[hs, :] = dq[hs, :] + nn(kt[hs, ks], ds)


def back_first_kernel(
    tb, segs, p, dot, ot, invl, qt, kt, v,
    dk_ref, dv_ref, dq_ref,
    dq, doz, dos, dlt,
):
    dk_ref[...] = jnp.zeros(dk_ref.shape, F32)
    dv_ref[...] = jnp.zeros(dv_ref.shape, F32)
    attend_back(0, tb, segs, p, dot, ot, invl, qt, kt, v, dk_ref, dv_ref, dq, doz, dos, dlt)
    dq_ref[...] = (dq[...] * HD ** (-0.5)).astype(BF16)


def back_second_kernel(
    tb, segs, p, dot, ot, invl, qt, kt, v, dk0, dv0, dq0, n,
    dqt_ref, dkt_ref, dvt_ref, keep_ref, send_ref,
    dk, dv, dq, doz, dos, dlt,
):
    dk[...] = dk0[...]
    dv[...] = dv0[...]
    attend_back(1, tb, segs, p, dot, ot, invl, qt, kt, v, dk, dv, dq, doz, dos, dlt)
    dqt_ref[:, 0:256] = dq0[...]
    dqt_ref[:, 256:512] = (dq[...] * HD ** (-0.5)).astype(BF16)
    dkt_ref[...] = dk[...].astype(BF16)
    dvt_ref[...] = dv[...].astype(BF16)
    nv = n[...]
    wq = nn(dqt_ref[...], nv[0:512, :])
    wk = nn(dkt_ref[...], nv)
    wv = nn(dvt_ref[...], nv)
    for i, w in enumerate((wq, wk, wv)):
        keep_ref[128 * i : 128 * i + 128, :] = w[0:128, :]
        send_ref[128 * i : 128 * i + 128, :] = w[128:256, :].astype(BF16)
    ones_q = jnp.ones((8, 512), BF16)
    ones_v = jnp.ones((8, 1024), BF16)
    bq = nt(ones_q, dqt_ref[...])
    bv = nt(ones_v, dvt_ref[...])
    empty = jnp.zeros((8, 256), F32)
    keep_ref[384:392, :] = jnp.concatenate([bq[:, 0:128], bv[:, 0:128], empty], axis=1)
    send_ref[384:392, :] = jnp.concatenate([bq[:, 128:256], bv[:, 128:256], empty], axis=1).astype(BF16)


def input_kernel(tb, dqt, dkt, dvt, qkv0, qkv1, own_ref, par_ref, send_ref):
    def weight(part):
        cols = slice(128 * part, 128 * part + 128)
        return jnp.concatenate([qkv0[0:512, cols], qkv1[0:512, cols]], axis=1)

    wk, wv = weight(1), weight(2)
    g = nn(wk, dkt[...]) + nn(wv, dvt[...])
    send_ref[...] = g[:, 512:1024].astype(BF16)
    g0 = g[:, 0:512] + nn(weight(0), dqt[...])
    own_ref[...] = g0[:, 0:256]
    par_ref[...] = g0[:, 256:512]


def last_kernel(tb, own, sib, par, x0, mg, log, vecs, e0, e1, e2, e3, grad_ref, sums_ref, gw):
    gather_gate(tb, (e0, e1, e2, e3), 128, gw)
    total = own[...] + sib[:, 0:256].astype(F32) + par[...].astype(F32)
    ng = total.T + nt(log[...], gw[...])
    unit, inverse = norm_unit(x0[...].astype(F32))
    g = ng * vecs[0:1, :]
    back = inverse * (g - jnp.mean(g, axis=-1, keepdims=True) - unit * jnp.mean(g * unit, axis=-1, keepdims=True))
    grad_ref[...] = mg[...] + back
    sums_ref[...] = jnp.zeros((8, 512), F32)
    sums_ref[0:1, :] = jnp.sum(ng * unit, axis=0, keepdims=True)
    sums_ref[1:2, :] = jnp.sum(ng, axis=0, keepdims=True)


def pack_kernel(
    pos, w_in, w_back, w_out, g1, g2, wq, wk, wv, *refs,
):
    vectors, (s_ref, e_ref, c_ref, qkv_ref, vecs), (sems, cut, *lines) = refs[:11], refs[11:16], refs[16:]
    start = pl.multiple_of((pos[4] & 3) * 128, 128)
    moves = [
        (w_in.at[:, pl.ds(start, 128)], cut),
        (w_back.at[pl.ds(start, 128), :], s_ref.at[128:256, :]),
        (w_out, e_ref.at[0:128, :]),
        (g1, e_ref.at[128:256, :]),
        (g2, e_ref.at[256:384, :]),
        (w_out, c_ref.at[0:128, :]),
        (g1, c_ref.at[128:256, :]),
        (g2, c_ref.at[256:384, :]),
        (w_in, c_ref.at[392:904, :]),
        (w_back, c_ref.at[904:1416, :]),
        (wq, qkv_ref.at[0:512, 0:128]),
        (wk, qkv_ref.at[0:512, 128:256]),
        (wv, qkv_ref.at[0:512, 256:384]),
    ] + list(zip(vectors, lines))
    copies = [pltpu.make_async_copy(src, dst, sems.at[i]) for i, (src, dst) in enumerate(moves)]
    for copy in copies:
        copy.start()
    for copy in copies:
        copy.wait()
    for i, v in enumerate(lines[:9]):
        vecs[i : i + 1, :] = v[...].astype(F32).reshape(1, 512)
    bq = lines[9][...].astype(F32).reshape(1, 128)
    bv = lines[10][...].astype(F32).reshape(1, 128)
    vecs[9:16, :] = jnp.zeros((7, 512), F32)
    s_ref[0:128, :] = cut[...].astype(F32).T.astype(BF16)
    bias = vecs[8:9, pl.ds(start, 128)]
    s_ref[256:264, :] = jnp.broadcast_to(jnp.concatenate([bias] * 4, axis=1), (8, 512)).astype(BF16)
    b_in = jnp.broadcast_to(vecs[8:9, :], (8, 512)).astype(BF16)
    e_ref[384:392, :] = b_in
    c_ref[384:392, :] = b_in
    for i, bias in enumerate((bq, jnp.zeros_like(bq), bv)):
        qkv_ref[512:520, 128 * i : 128 * i + 128] = jnp.broadcast_to(bias, (8, 128)).astype(BF16)


def half_rows_kernel(tb, keep, recv, out_ref):
    out_ref[...] = (keep[384:, :] + recv[384:, :].astype(F32)).astype(BF16)


def half_columns_kernel(tb, keep, recv, out_ref):
    half = keep.shape[1]
    out_ref[...] = (keep[...] + recv[:, half:].astype(F32)).astype(BF16)


def stages_of(n_dp):
    return [(shift, 2) for shift in range(n_dp.bit_length() - 1)]


def dp_hop(value, mask, n_dp):
    return lax.ppermute(value, "dp", [(i, i ^ mask) for i in range(n_dp)])


def padded(rows, n_dp):
    unit = 8 * n_dp
    return -(-rows // unit) * unit


def split_into(total, pos, shift, size, outs):
    rows = total.shape[0] // size
    mine = (pos[4] >> shift) & (size - 1)
    for k, out in enumerate(outs):
        at = pl.multiple_of((mine ^ k) * rows, 8)
        out[...] = total[pl.ds(at, rows), :].astype(out.dtype)


def split_kernel(pos, *refs, parts, shift, size):
    count = sum(len(p[1]) for p in parts)
    ins, outs, total = refs[:count], refs[count:-1], refs[-1]
    at, used = 0, 0
    for rows, takes in parts:
        value = ins[used][takes[0] : takes[0] + rows, :].astype(F32)
        for ref, start in zip(ins[used + 1 : used + len(takes)], takes[1:]):
            value = value + ref[start : start + rows, :].astype(F32)
        total[at : at + rows, :] = value
        used += len(takes)
        at += rows
    if at < total.shape[0]:
        total[at:, :] = jnp.zeros((total.shape[0] - at, 512), F32)
    split_into(total, pos, shift, size, outs)


def small_kernel(pos, *refs, rows, count, small):
    out = refs[-1]
    value = refs[0][...].astype(F32)
    for r in refs[1:count]:
        value = value + r[...].astype(F32)
    out[0:rows, :] = value.astype(BF16)
    if small:
        at = count
        out[rows : rows + 8, :] = jnp.zeros((8, 512), BF16)
        for first, size, starts in small:
            block = refs[at][starts[0] : starts[0] + size, :].astype(F32)
            for r, start in zip(refs[at + 1 : at + len(starts)], starts[1:]):
                block = block + r[start : start + size, :].astype(F32)
            out[rows + first : rows + first + size, :] = block.astype(BF16)
            at += len(starts)


def join_kernel(pos, *refs):
    out = refs[-1]
    size = refs[0].shape[0]
    for i, r in enumerate(refs[:-1]):
        out[i * size : i * size + size] = r[...]


def unpack_kernel(pos, *refs, count, plan, rows, has_small, stages):
    place = 0
    for shift, size in stages:
        place = place * size + ((pos[4] >> shift) & (size - 1))
    blocks, outs, scratch = refs[:count], refs[count:-1], refs[-1]
    each = blocks[0].shape[0]
    for i in range(count * each):
        at = pl.multiple_of((place ^ i) * rows, 8)
        scratch[pl.ds(at, rows), :] = blocks[i // each][i % each, 0:rows, :].astype(F32)
    for out, (start, size, flip) in zip(outs, plan):
        block = scratch[start : start + size, :]
        out[...] = block.T if flip else block
    if has_small:
        total = jnp.zeros((8, 512), F32)
        for b in blocks:
            total = total + jnp.sum(b[:, rows:, :].astype(F32), axis=0)
        outs[len(plan)][...] = total


def unpack_call(pos, blocks, stages, plan, small):
    rows = blocks[0].shape[1] - (8 if small else 0)
    shapes = [sds((512, size) if flip else (size, 512), F32) for _, size, flip in plan]
    if small:
        shapes = shapes + [sds((8, 512), F32)]
    total = rows * sum(b.shape[0] for b in blocks)
    return call(
        functools.partial(
            unpack_kernel, count=len(blocks), plan=plan, rows=rows, has_small=bool(small), stages=tuple(stages)
        ),
        shapes, [pos] + blocks, smem=1, scratch=[pltpu.VMEM((total, 512), F32)], name="unpack",
    )


def body(
    layer_input, segments, norm1_gain, norm1_bias, w_query, b_query, w_key, w_value, b_value,
    w_out, b_out, gate1_w, gate1_b, norm2_gain, norm2_bias, w_in, b_in, w_back, b_back,
    gate2_w, gate2_b, cotangent, *, n_dp,
):
    def hop(value, mask):
        return lax.ppermute(value, "tensor", [(i, i ^ mask) for i in range(4)])

    def dhop(value, mask):
        return dp_hop(value, mask, n_dp)

    def after(value, *deps):
        return lax.optimization_barrier((value,) + deps)[0]

    t = lax.axis_index("tensor").astype(jnp.int32)
    me = lax.axis_index("dp").astype(jnp.int32)
    tb = jnp.where(jnp.arange(8) < 4, t ^ jnp.array(LOCAL + (0,) * 4, jnp.int32), me)
    seg = segments
    x0 = layer_input
    last = [None]

    def step(kernel, outs, args, name, scratch=(), smem=1, space=VM, then=(), limit=None):
        pos = tb if last[0] is None else after(tb, last[0], *then)
        got = call(kernel, outs, [pos] + args, smem=smem, scratch=scratch, name=name, space=space, limit=limit)
        last[0] = got[0]
        return got

    x1 = hop(x0, PX)
    x2 = hop(x0, 1)
    s0, e0, c0, qkv0, vecs = step(
        pack_kernel,
        [sds((264, 512), BF16), sds((392, 512), BF16), sds((1416, 512), BF16), sds((520, 384), BF16), sds((16, 512), F32)],
        [w_in, w_back, w_out, gate1_w, gate2_w, w_query, w_key, w_value, norm1_gain, norm1_bias, b_out, gate1_b,
         norm2_gain, norm2_bias, b_back, gate2_b, b_in, b_query, b_value],
        "pack",
        [pltpu.SemaphoreType.DMA((24,)), pltpu.VMEM((512, 128), BF16)]
        + [pltpu.VMEM((512,), BF16)] * 9 + [pltpu.VMEM((128,), BF16)] * 2,
        space=pl.BlockSpec(memory_space=pltpu.MemorySpace.HBM), limit=60 * 1024 * 1024,
    )
    qkv1 = hop(qkv0, 1)
    sy = hop(s0, PX)
    x3 = hop(x1, 1)
    e1 = hop(after(e0, x1), PX)
    c2 = hop(after(c0, qkv1), 1)

    n, qt0, qt1, k, vt, p1, ot1, att1, invl1 = step(
        first_kernel,
        [
            sds((1024, 512), BF16), sds((256, 256), BF16), sds((256, 256), BF16), sds((1024, 256), BF16),
            sds((256, 1024), BF16), sds((4, 1024, 256), BF16), sds((256, 256), BF16), sds((256, 256), BF16),
            sds((4, 8, 256), F32),
        ],
        [seg, seg, x0, x1, x2, x3, vecs, qkv0, qkv1],
        "first", ATT_SCRATCH, 2,
    )
    attp = hop(att1, PX)
    sy = after(sy, att1)
    sx = dhop(sy, 1)
    sz = dhop(sy, 2)
    e3 = hop(after(e1, att1), 1)
    p0, ot0, att0, invl0 = step(
        second_kernel,
        [sds((4, 1024, 256), BF16), sds((256, 256), BF16), sds((256, 256), BF16), sds((4, 8, 256), F32)],
        [seg, seg, qt0, k, vt],
        "second", ATT_SCRATCH, 2,
    )
    v, kt = step(prepare_kernel, [sds((1024, 256), BF16), sds((256, 1024), BF16)], [n, k, qkv0, qkv1], "prepare")
    n2, mid, branch, gate = step(
        out_kernel,
        [sds((256, 512), BF16), sds((256, 512), F32), sds((256, 512), F32), sds((256, 512), F32)],
        [x0, n, att0, attp, vecs, e0, e1, c2, e3],
        "out", [pltpu.VMEM((512, 512), BF16)],
    )
    n2p = hop(n2, PX)
    sxz = dhop(after(sz, n2), 1)
    total0, hid, slope0 = step(
        ffn_first_kernel,
        [sds((256, 512), F32), sds((256, 1024), BF16), sds((256, 1024), BF16)],
        [n2, vecs, w_in, w_back, c2],
        "ffn_first",
    )
    quarters = [sy, hop(sy, 1), sx, hop(sx, 1), sz, hop(sz, 1)]
    sxz = after(sxz, total0)
    quarters = quarters + [sxz, hop(sxz, 1)]
    result, fg, ltg, slope1 = step(
        ffn_kernel,
        [sds((256, 512), BF16), sds((256, 512), BF16), sds((256, 512), BF16), sds((256, 1024), BF16)],
        [n2, mid, cotangent, vecs, e0, e1, c2, e3, total0] + quarters,
        "ffn", [pltpu.VMEM((512, 512), BF16)],
    )
    fgp = hop(fg, PX)
    dot0, dotp, mg, bg, log, hg, sums = step(
        back_kernel,
        [
            sds((256, 256), BF16), sds((256, 256), BF16), sds((256, 512), F32), sds((256, 512), BF16),
            sds((256, 512), BF16), sds((256, 1024), BF16), sds((8, 512), F32),
        ],
        [fg, ltg, slope0, slope1, mid, branch, gate, cotangent, vecs, e0, e1, c2, e3, w_in, w_back] + quarters,
        "back", [pltpu.VMEM((512, 512), BF16)],
    )
    dot1 = hop(dotp, PX)
    back_scratch = [
        pltpu.VMEM((256, 256), F32), pltpu.VMEM((4, 128, 256), BF16), pltpu.VMEM((256, 256), BF16),
        pltpu.VMEM((4, 8, 256), F32),
    ]
    dk0, dv0, dq0 = step(
        back_first_kernel,
        [sds((256, 1024), F32), sds((256, 1024), F32), sds((256, 256), BF16)],
        [seg, p0, dot0, ot0, invl0, qt0, kt, v],
        "attn_back0", back_scratch, 2,
    )
    bkeep, bsend, slopep = step(
        ffn_back_weight_kernel,
        [sds((512, 512), F32), sds((512, 512), BF16), sds((256, 1024), BF16)],
        [n2p, fg, fgp, hid, vecs, w_in, c2],
        "ffn_back_weight",
    )
    brecv = hop(bsend, 1)
    ikeep, isend = step(
        ffn_in_weight_kernel,
        [sds((520, 512), F32), sds((520, 512), BF16)],
        [n2, n2p, fgp, hg, slopep, w_back, c2],
        "ffn_in_weight",
    )
    irecv = hop(isend, 1)
    skeep, ssend = step(
        small_weight_kernel,
        [sds((776, 512), F32), sds((776, 512), BF16)],
        [n, n2, ltg, log, att0, attp, bg, sums],
        "small_weight", [pltpu.VMEM((512, 512), F32), pltpu.VMEM((512, 512), F32)], then=(dot1,),
    )
    srecv = hop(ssend, 1)
    stages = stages_of(n_dp)

    def split(parts, rows, stage):
        shift, size = stage
        arrays = [a for _, addends in parts for a, _ in addends]
        static = tuple((r, tuple(start for _, start in addends)) for r, addends in parts)
        return step(
            functools.partial(split_kernel, parts=static, shift=shift, size=size),
            [sds((rows // size, 512), F32)] + [sds((rows // size, 512), BF16)] * (size - 1),
            arrays, "split", [pltpu.VMEM((rows, 512), F32)],
        )

    def send(pieces, stage):
        return [pieces[0]] + [dhop(p, k << stage[0]) for k, p in enumerate(pieces[1:], 1)]

    def resplit(pieces, i):
        rows = pieces[0].shape[0]
        return send(split([(rows, [(p, 0) for p in pieces])], rows, stages[i]), stages[i])

    def fold(pieces, small):
        rows = pieces[0].shape[0]
        static = tuple((f, m, tuple(start for _, start in group)) for f, m, group in small)
        arrays = [a for _, _, group in small for a, _ in group]
        return step(
            functools.partial(small_kernel, rows=rows, count=len(pieces), small=static),
            [sds((rows + (8 if small else 0), 512), BF16)], list(pieces) + arrays, "fold",
        )[0]

    def spread(held, i):
        shift, size = stages[i]
        return [held] + [dhop(held, k << shift) for k in range(1, size)]

    def join(blocks):
        shape = (len(blocks) * blocks[0].shape[0],) + blocks[0].shape[1:]
        return step(join_kernel, [sds(shape, BF16)], blocks, "join")[0]

    depth = len(stages)
    rows_f, rows_a = padded(1024, n_dp), padded(768, n_dp)
    f = send(split([(512, [(bkeep, 0), (brecv, 0)]), (512, [(ikeep, 0), (irecv, 0)])], rows_f, stages[0]), stages[0])
    (spar,) = step(half_rows_kernel, [sds((392, 512), BF16)], [skeep, srecv], "half_rows")
    sparr = hop(spar, PX)

    dqt, dkt, dvt, akeep, asend = step(
        back_second_kernel,
        [
            sds((256, 512), BF16), sds((256, 1024), BF16), sds((256, 1024), BF16), sds((392, 512), F32),
            sds((392, 512), BF16),
        ],
        [seg, p1, dot1, ot1, invl1, qt1, kt, v, dk0, dv0, dq0, n],
        "attn_back1", [pltpu.VMEM((256, 1024), F32), pltpu.VMEM((256, 1024), F32)] + back_scratch, 2,
    )
    arecv = hop(asend, 1)
    gown, gpar, gsend = step(
        input_kernel,
        [sds((512, 256), F32), sds((512, 256), F32), sds((512, 512), BF16)],
        [dqt, dkt, dvt, qkv0, qkv1],
        "input_grad",
    )
    gsib = hop(gsend, 1)
    f = resplit(f, 1)
    a = send(
        split([(384, [(akeep, 0), (arecv, 0)]), (384, [(skeep, 0), (srecv, 0), (sparr, 0)])], rows_a, stages[0]),
        stages[0],
    )
    (gsum,) = step(half_columns_kernel, [sds((512, 256), BF16)], [gpar, gsib], "half_columns")
    gp = hop(gsum, PX)
    f = resplit(f, 2)
    a = resplit(a, 1)
    input_grad, sums1 = step(
        last_kernel,
        [sds((256, 512), F32), sds((8, 512), F32)],
        [gown, gsib, gp, x0, mg, log, vecs, e0, e1, c2, e3],
        "last", [pltpu.VMEM((512, 512), BF16)],
    )
    sums1_b = hop(sums1, PX)
    sums1_a = hop(sums1, 1)
    for i in range(3, depth):
        f = resplit(f, i)
    for i in range(2, depth - 1):
        a = resplit(a, i)
    tail = [(skeep, 773), (srecv, 773), (sparr, 389)]
    f = fold(f, [(0, 1, [(ikeep, 512), (irecv, 512)]), (1, 1, tail)])[None]
    f = spread(f, depth - 1)
    a = resplit(a, depth - 1)
    sums1_c = hop(after(sums1_b, a[0]), 1)
    f = spread(join(f), depth - 2)
    group = [(skeep, 768), (srecv, 768), (sparr, 384)]
    a = fold(
        a,
        [(0, 2, [(sums1, 0), (sums1_a, 0), (sums1_b, 0), (sums1_c, 0)]), (2, 1, [(akeep, 384), (arecv, 384)]),
         (3, 5, group)],
    )[None]
    a = spread(a, depth - 1)
    for i in range(depth - 3, -1, -1):
        f = spread(join(f), i)
        a = spread(join(a), i + 1)
    a = spread(join(a), 0)
    g_wback, g_win, f_small = unpack_call(tb, f, stages, ((0, 512, False), (512, 512, False)), True)
    plan = ((0, 128, True), (128, 128, True), (256, 128, True), (384, 128, False), (512, 128, False), (640, 128, False))
    g_q, g_k, g_v, g_g2, g_g1, g_wo, a_small = unpack_call(tb, a, stages, plan, True)
    return (
        result,
        input_grad,
        a_small[0],
        a_small[1],
        g_q,
        a_small[2, 0:128],
        g_k,
        g_v,
        a_small[2, 128:256],
        g_wo,
        a_small[5],
        g_g1,
        a_small[6],
        a_small[7],
        f_small[1],
        g_win,
        f_small[0],
        g_wback,
        a_small[3],
        g_g2,
        a_small[4],
    )


def solution(mesh):
    tok = P(("dp", "tensor"), None)
    col = P(None, "tensor")
    row = P("tensor", None)
    vec = P("tensor")
    rep = P()
    return jax.shard_map(
        functools.partial(body, n_dp=mesh.shape["dp"]),
        mesh=mesh,
        in_specs=(
            tok, P("dp", None), rep, rep, col, vec, col, col, vec, row, rep, row, rep, rep, rep,
            col, vec, row, rep, row, rep, tok,
        ),
        out_specs=(
            tok, tok, rep, rep, col, vec, col, col, vec, row, rep, row, rep, rep, rep,
            col, vec, row, rep, row, rep,
        ),
        check_vma=False,
    )
```

```python
import functools
import math

import jax
import jax.numpy as jnp
from jax import lax
from jax.experimental import pallas as pl
from jax.experimental.pallas import tpu as pltpu
from jax.sharding import PartitionSpec as P

HD = 64
EPSILON = 1e-05
F32 = jnp.float32
BF16 = jnp.bfloat16
NEG = -1e30
PX = 2
LOCAL = (0, PX, 1, 1 ^ PX)
SPARE = 4 * 1024 * 1024
COST = 10**10


def nn(a, b):
    return lax.dot_general(a, b, (((1,), (0,)), ((), ())), preferred_element_type=F32)


def nt(a, b):
    return lax.dot_general(a, b, (((1,), (1,)), ((), ())), preferred_element_type=F32)


def tn(a, b):
    return lax.dot_general(a, b, (((0,), (0,)), ((), ())), preferred_element_type=F32)


VM = pl.BlockSpec(memory_space=pltpu.VMEM)
SM = pl.BlockSpec(memory_space=pltpu.SMEM)


def call(body, outs, args, smem=0, scratch=(), name=None, space=VM, limit=None):
    nbytes = sum(a.size * a.dtype.itemsize for a in args) + sum(o.size * o.dtype.itemsize for o in outs)
    held = sum(math.prod(s.shape) * 4 for s in scratch)
    limit = limit or nbytes + held + SPARE
    return pl.pallas_call(
        body,
        out_shape=tuple(outs),
        in_specs=[SM] * smem + [space] * (len(args) - smem),
        out_specs=tuple([VM] * len(outs)),
        scratch_shapes=list(scratch),
        compiler_params=pltpu.CompilerParams(vmem_limit_bytes=limit),
        cost_estimate=pl.CostEstimate(flops=COST, bytes_accessed=0, transcendentals=0),
        name=name,
    )(*args)


def sds(shape, dtype):
    return jax.ShapeDtypeStruct(shape, dtype)


def norm_unit(values):
    centred = values - jnp.mean(values, axis=-1, keepdims=True)
    spread = jnp.mean(centred * centred, axis=-1, keepdims=True)
    inverse = lax.rsqrt(spread + EPSILON)
    return centred * inverse, inverse


def sigmoid(v):
    return 1.0 / (1.0 + jnp.exp(-v))


C0 = 0.7978845608028654
C1 = 0.044715


def gelu_parts(u):
    square = u * u
    t = jnp.tanh(C0 * u * (1.0 + C1 * square))
    half = 0.5 * (1.0 + t)
    value = u * half
    slope = half + (0.5 * C0) * u * (1.0 - t * t) * (1.0 + (3.0 * C1) * square)
    return value, slope


def attend_query_block(qb, tb, segs, segv, qz, k, vt, p_ref, ot_ref, invl_ref, s_sc, m_sc, l_sc, o_sc, segc):
    rows = 256
    tq = tb[qb]
    m_sc[...] = jnp.full(m_sc.shape, NEG, F32)
    l_sc[...] = jnp.zeros(l_sc.shape, F32)
    o_sc[...] = jnp.zeros(o_sc.shape, F32)
    seg_q = segv[0:1, pl.ds(pl.multiple_of(tq * rows, rows), rows)].astype(F32)

    def active(kb):
        tk = tb[kb]
        return (tk <= tq) & (segs[0, tk * rows + rows - 1] >= segs[0, tq * rows])

    @pl.loop(0, 4)
    def _(kb):
        @pl.when(active(kb))
        def _():
            tk = tb[kb]
            krows = pl.ds(pl.multiple_of(kb * rows, rows), rows)
            kpos = tk * rows + lax.broadcasted_iota(jnp.int32, (rows, rows), 0)
            qpos = tq * rows + lax.broadcasted_iota(jnp.int32, (rows, rows), 1)
            seg_k = segc[pl.ds(pl.multiple_of(tk * rows, rows), rows), 0:1]
            bias = jnp.where((kpos <= qpos) & (seg_k == seg_q), 0.0, NEG)
            for h in range(4):
                pair = 128 * (h // 2)
                s = nn(k[krows, pair : pair + 128], qz[h]) + bias
                s_sc[h, krows, :] = s
                m_sc[h] = jnp.maximum(m_sc[h], jnp.max(s.reshape(rows // 8, 8, rows), axis=0))

    for h in range(4):
        m_sc[h] = jnp.broadcast_to(jnp.max(m_sc[h], axis=0, keepdims=True), (8, rows))

    @pl.loop(0, 4)
    def _(kb):
        @pl.when(active(kb))
        def _():
            krows = pl.ds(pl.multiple_of(kb * rows, rows), rows)
            for h in range(4):
                e = jnp.exp(s_sc[h, krows, :] - m_sc[h, 0:1, :])
                l_sc[h] = l_sc[h] + jnp.sum(e.reshape(rows // 8, 8, rows), axis=0)
                pb = e.astype(BF16)
                p_ref[h, krows, :] = pb
                o_sc[h] = o_sc[h] + nn(vt[64 * h : 64 * h + 64, krows], pb)

    for h in range(4):
        invl = 1.0 / jnp.sum(l_sc[h], axis=0, keepdims=True)
        invl_ref[h] = jnp.broadcast_to(invl, (8, rows))
        ot_ref[64 * h : 64 * h + 64, :] = (o_sc[h] * invl).astype(BF16)


def fill_qz(qz, qt):
    zero = jnp.zeros((64, 256), BF16)
    for h in range(4):
        mine = qt[64 * h : 64 * h + 64, :]
        qz[h] = jnp.concatenate([mine, zero] if h % 2 == 0 else [zero, mine], axis=0)


def fill_segc(segc, segv):
    for t in range(4):
        row = jnp.broadcast_to(segv[0:1, 256 * t : 256 * t + 256].astype(F32), (128, 256))
        segc[256 * t : 256 * t + 256, :] = row.T


def first_kernel(
    tb, segs, segv, x0, x1, x2, x3, vecs, qkv0, qkv1,
    n_ref, qt0_ref, qt1_ref, k_ref, vt_ref, p_ref, ot_ref, att_ref, invl_ref,
    qz, s_sc, m_sc, l_sc, o_sc, segc,
):
    for i, x in enumerate((x0, x1, x2, x3)):
        unit, _ = norm_unit(x[...].astype(F32))
        n_ref[256 * i : 256 * i + 256, :] = (unit * vecs[0:1, :] + vecs[1:2, :]).astype(BF16)
    n = n_ref[...]
    for c, w in enumerate((qkv0, qkv1)):
        cols = slice(128 * c, 128 * c + 128)
        q = nn(n[0:512], w[0:512, 0:128]) + w[512:513, 0:128].astype(F32)
        qt = (q.astype(BF16).astype(F32) * HD ** (-0.5)).T.astype(BF16)
        qt0_ref[cols, :] = qt[:, 0:256]
        qt1_ref[cols, :] = qt[:, 256:512]
        k_ref[:, cols] = nn(n, w[0:512, 128:256]).astype(BF16)
        v = nn(n, w[0:512, 256:384]) + w[512:513, 256:384].astype(F32)
        vt_ref[cols, :] = v.T.astype(BF16)
    fill_segc(segc, segv)
    fill_qz(qz, qt1_ref)
    attend_query_block(1, tb, segs, segv, qz, k_ref, vt_ref, p_ref, ot_ref, invl_ref, s_sc, m_sc, l_sc, o_sc, segc)
    att_ref[...] = ot_ref[...].astype(F32).T.astype(BF16)


def second_kernel(
    tb, segs, segv, qt0, k, vt,
    p_ref, ot_ref, att_ref, invl_ref,
    qz, s_sc, m_sc, l_sc, o_sc, segc,
):
    fill_segc(segc, segv)
    fill_qz(qz, qt0)
    attend_query_block(0, tb, segs, segv, qz, k, vt, p_ref, ot_ref, invl_ref, s_sc, m_sc, l_sc, o_sc, segc)
    att_ref[...] = ot_ref[...].astype(F32).T.astype(BF16)


ATT_SCRATCH = (
    pltpu.VMEM((4, 128, 256), BF16),
    pltpu.VMEM((4, 1024, 256), F32),
    pltpu.VMEM((4, 8, 256), F32),
    pltpu.VMEM((4, 8, 256), F32),
    pltpu.VMEM((4, 64, 256), F32),
    pltpu.VMEM((1024, 128), F32),
)


def gather_gate(tb, pieces, start, scratch):
    for i, piece in enumerate(pieces):
        scratch[pl.ds(pl.multiple_of(tb[i] * 128, 128), 128), :] = piece[start : start + 128, :]


def out_kernel(
    tb, x0, n, att, attp, vecs, e0, e1, e2, e3,
    n2_ref, mid_ref, branch_ref, gate_ref,
    gw,
):
    gather_gate(tb, (e0, e1, e2, e3), 128, gw)
    branch = nn(att[:, 0:128], e0[0:128, :]) + nn(att[:, 128:256], e2[0:128, :])
    branch = branch + nn(attp[:, 0:128], e1[0:128, :]) + nn(attp[:, 128:256], e3[0:128, :])
    branch = branch + vecs[2:3, :]
    gate = sigmoid(nn(n[0:256, :], gw[...]) + vecs[3:4, :])
    middle = x0[...].astype(F32) + gate * branch
    unit, _ = norm_unit(middle)
    n2_ref[...] = (unit * vecs[4:5, :] + vecs[5:6, :]).astype(BF16)
    mid_ref[...] = middle
    branch_ref[...] = branch
    gate_ref[...] = gate


def pair_up(a, b, start):
    return jnp.concatenate([a[start : start + 128, :], b[start : start + 128, :]], axis=0)


def pair_bias(a, b):
    return jnp.concatenate([a[256:257, 0:128], b[256:257, 0:128]], axis=1).astype(F32)


def ffn_first_kernel(
    tb, n2, vecs, win0, wback0, c2,
    total_ref, hid_ref, slope_ref,
):
    n2v = n2[...]
    total = jnp.zeros((256, 512), F32)
    for i, (b, w, wb) in enumerate(((vecs[8:9, :], win0[...], wback0[...]), (c2[384:385, :], c2[392:904, :], c2[904:1416, :]))):
        value, slope = gelu_parts(nn(n2v, w) + b.astype(F32))
        value = value.astype(BF16)
        hid_ref[:, 512 * i : 512 * i + 512] = value
        slope_ref[:, 512 * i : 512 * i + 512] = slope.astype(BF16)
        total = total + nn(value, wb)
    total_ref[...] = total


def ffn_kernel(
    tb, n2, mid, ct, vecs, e0, e1, e2, e3, total0, s0, s1, s2, s3, s4, s5, s6, s7,
    out_ref, fg_ref, ltg_ref, slope_ref,
    gw,
):
    gather_gate(tb, (e0, e1, e2, e3), 256, gw)
    n2v = n2[...]
    total = total0[...]
    for i, (a, b) in enumerate(((s0, s1), (s2, s3), (s4, s5), (s6, s7))):
        value, slope = gelu_parts(nt(n2v, pair_up(a, b, 0)) + pair_bias(a, b))
        slope_ref[:, 256 * i : 256 * i + 256] = slope.astype(BF16)
        total = total + nn(value.astype(BF16), pair_up(a, b, 128))
    ffn = total + vecs[6:7, :]
    gate = sigmoid(nn(n2v, gw[...]) + vecs[7:8, :])
    up = ct[...].astype(F32)
    out_ref[...] = (mid[...] + gate * ffn).astype(BF16)
    fg_ref[...] = (gate * up).astype(BF16)
    ltg_ref[...] = (up * ffn * (gate * (1.0 - gate))).astype(BF16)


def back_kernel(
    tb, fg, ltg, slope0, slope1, mid, branch, gate, ct, vecs, e0, e1, e2, e3,
    win0, wback0, s0, s1, s2, s3, s4, s5, s6, s7,
    dot_ref, dotp_ref, mg_ref, bg_ref, log_ref, hg_ref, sums_ref,
    gw,
):
    gather_gate(tb, (e0, e1, e2, e3), 256, gw)
    fgv = fg[...]
    ltgv = ltg[...]
    ng = nt(ltgv, gw[...])
    for i, (w, wb) in enumerate(((win0[...], wback0[...]), (e2[392:904, :], e2[904:1416, :]))):
        hg = (nt(fgv, wb) * slope0[:, 512 * i : 512 * i + 512].astype(F32)).astype(BF16)
        hg_ref[:, 512 * i : 512 * i + 512] = hg
        ng = ng + nt(hg, w)
    for i, (a, b) in enumerate(((s0, s1), (s2, s3), (s4, s5), (s6, s7))):
        hg = (nt(fgv, pair_up(a, b, 128)) * slope1[:, 256 * i : 256 * i + 256].astype(F32)).astype(BF16)
        ng = ng + nn(hg, pair_up(a, b, 0))
    unit, inverse = norm_unit(mid[...])
    g = ng * vecs[4:5, :]
    back = inverse * (g - jnp.mean(g, axis=-1, keepdims=True) - unit * jnp.mean(g * unit, axis=-1, keepdims=True))
    mg = ct[...].astype(F32) + back
    mg_ref[...] = mg
    gatev = gate[...]
    bg = (gatev * mg).astype(BF16)
    log = (mg * branch[...] * (gatev * (1.0 - gatev))).astype(BF16)
    bg_ref[...] = bg
    log_ref[...] = log
    dot_ref[0:128, :] = nt(e0[0:128, :], bg).astype(BF16)
    dot_ref[128:256, :] = nt(e2[0:128, :], bg).astype(BF16)
    dotp_ref[0:128, :] = nt(e1[0:128, :], bg).astype(BF16)
    dotp_ref[128:256, :] = nt(e3[0:128, :], bg).astype(BF16)
    rows = [fgv.astype(F32), ltgv.astype(F32), bg.astype(F32), log.astype(F32), ng * unit, ng]
    sums_ref[...] = jnp.zeros((8, 512), F32)
    for i, r in enumerate(rows):
        sums_ref[i : i + 1, :] = jnp.sum(r, axis=0, keepdims=True)


def ffn_back_weight_kernel(
    tb, n2p, fg, fgp, hid, vecs, win0, c2,
    keep_ref, send_ref, slope_ref,
):
    fgv, fgpv, n2pv = fg[...], fgp[...], n2p[...]
    for i, (b, w) in enumerate(((vecs[8:9, :], win0[...]), (c2[384:385, :], c2[392:904, :]))):
        cols = slice(512 * i, 512 * i + 512)
        value, slope = gelu_parts(nn(n2pv, w) + b.astype(F32))
        slope_ref[:, cols] = slope.astype(BF16)
        wback = tn(hid[:, cols], fgv) + tn(value.astype(BF16), fgpv)
        dst = keep_ref if i == 0 else send_ref
        dst[...] = wback.astype(dst.dtype)


def ffn_in_weight_kernel(
    tb, n2, n2p, fgp, hg, slope, wback0, c2,
    keep_ref, send_ref,
):
    n2v, n2pv, fgpv = n2[...], n2p[...], fgp[...]
    for i, wb in enumerate((wback0[...], c2[904:1416, :])):
        cols = slice(512 * i, 512 * i + 512)
        hgp = (nt(fgpv, wb) * slope[:, cols].astype(F32)).astype(BF16)
        hgo = hg[:, cols]
        win = tn(n2v, hgo) + tn(n2pv, hgp)
        bias = jnp.sum(hgo.astype(F32), axis=0, keepdims=True) + jnp.sum(hgp.astype(F32), axis=0, keepdims=True)
        dst = keep_ref if i == 0 else send_ref
        dst[0:512, :] = win.astype(dst.dtype)
        dst[512:520, :] = jnp.broadcast_to(bias, (8, 512)).astype(dst.dtype)


def small_weight_kernel(
    tb, n, n2, ltg, log, att, attp, bg, sums,
    keep_ref, send_ref,
    g1, g2,
):
    keep_ref[768:776, :] = sums[...]
    send_ref[768:776, :] = sums[...].astype(BF16)
    g2[...] = tn(n2[...], ltg[...])
    g1[...] = tn(n[0:256, :], log[...])
    bgv = bg[...]
    wo = (tn(att[:, 0:128], bgv), tn(attp[:, 0:128], bgv), tn(att[:, 128:256], bgv), tn(attp[:, 128:256], bgv))
    for i in range(4):
        src = pl.ds(pl.multiple_of(tb[i] * 128, 128), 128)
        dst = keep_ref if i < 2 else send_ref
        base = 384 * (i % 2)
        dst[base : base + 128, :] = g2[src, :].astype(dst.dtype)
        dst[base + 128 : base + 256, :] = g1[src, :].astype(dst.dtype)
        dst[base + 256 : base + 384, :] = wo[i].astype(dst.dtype)


def prepare_kernel(tb, n, k, qkv0, qkv1, v_ref, kt_ref):
    nv = n[...]
    for c, w in enumerate((qkv0, qkv1)):
        v = nn(nv, w[0:512, 256:384]) + w[512:513, 256:384].astype(F32)
        v_ref[:, 128 * c : 128 * c + 128] = v.astype(BF16)
    kt_ref[...] = k[...].astype(F32).T.astype(BF16)


def attend_back(qb, tb, segs, p, dot, ot, invl, qt, kt, v, dk, dv, dq, doz, dos, dlt):
    rows = 256
    tq = tb[qb]
    zero = jnp.zeros((64, rows), BF16)
    for h in range(4):
        hs = slice(64 * h, 64 * h + 64)
        scale = invl[h, 0:1, :]
        dv_h = dot[hs, :].astype(F32)
        delta = jnp.sum(dv_h * ot[hs, :].astype(F32), axis=0, keepdims=True) * scale
        dlt[h] = jnp.broadcast_to(delta, (8, rows))
        mine = (dv_h * scale).astype(BF16)
        dos[hs, :] = mine
        doz[h] = jnp.concatenate([mine, zero] if h % 2 == 0 else [zero, mine], axis=0)
    dq[...] = jnp.zeros(dq.shape, F32)

    @pl.loop(0, 4)
    def _(kb):
        tk = tb[kb]

        @pl.when((tk <= tq) & (segs[0, tk * rows + rows - 1] >= segs[0, tq * rows]))
        def _():
            ks = pl.ds(pl.multiple_of(kb * rows, rows), rows)
            for h in range(4):
                pair = 128 * (h // 2)
                hs = slice(64 * h, 64 * h + 64)
                ph = p[h, ks, :]
                dp = nn(v[ks, pair : pair + 128], doz[h])
                ds = (ph.astype(F32) * (dp - dlt[h, 0:1, :])).astype(BF16)
                dv[hs, ks] = dv[hs, ks] + nt(dos[hs, :], ph)
                dk[hs, ks] = dk[hs, ks] + nt(qt[hs, :], ds)
                dq[hs, :] = dq[hs, :] + nn(kt[hs, ks], ds)


def back_first_kernel(
    tb, segs, p, dot, ot, invl, qt, kt, v,
    dk_ref, dv_ref, dq_ref,
    dq, doz, dos, dlt,
):
    dk_ref[...] = jnp.zeros(dk_ref.shape, F32)
    dv_ref[...] = jnp.zeros(dv_ref.shape, F32)
    attend_back(0, tb, segs, p, dot, ot, invl, qt, kt, v, dk_ref, dv_ref, dq, doz, dos, dlt)
    dq_ref[...] = (dq[...] * HD ** (-0.5)).astype(BF16)


def back_second_kernel(
    tb, segs, p, dot, ot, invl, qt, kt, v, dk0, dv0, dq0, n,
    dqt_ref, dkt_ref, dvt_ref, keep_ref, send_ref,
    dk, dv, dq, doz, dos, dlt,
):
    dk[...] = dk0[...]
    dv[...] = dv0[...]
    attend_back(1, tb, segs, p, dot, ot, invl, qt, kt, v, dk, dv, dq, doz, dos, dlt)
    dqt_ref[:, 0:256] = dq0[...]
    dqt_ref[:, 256:512] = (dq[...] * HD ** (-0.5)).astype(BF16)
    dkt_ref[...] = dk[...].astype(BF16)
    dvt_ref[...] = dv[...].astype(BF16)
    nv = n[...]
    wq = nn(dqt_ref[...], nv[0:512, :])
    wk = nn(dkt_ref[...], nv)
    wv = nn(dvt_ref[...], nv)
    for i, w in enumerate((wq, wk, wv)):
        keep_ref[128 * i : 128 * i + 128, :] = w[0:128, :]
        send_ref[128 * i : 128 * i + 128, :] = w[128:256, :].astype(BF16)
    ones_q = jnp.ones((8, 512), BF16)
    ones_v = jnp.ones((8, 1024), BF16)
    bq = nt(ones_q, dqt_ref[...])
    bv = nt(ones_v, dvt_ref[...])
    empty = jnp.zeros((8, 256), F32)
    keep_ref[384:392, :] = jnp.concatenate([bq[:, 0:128], bv[:, 0:128], empty], axis=1)
    send_ref[384:392, :] = jnp.concatenate([bq[:, 128:256], bv[:, 128:256], empty], axis=1).astype(BF16)


def input_kernel(tb, dqt, dkt, dvt, qkv0, qkv1, own_ref, par_ref, send_ref):
    def weight(part):
        cols = slice(128 * part, 128 * part + 128)
        return jnp.concatenate([qkv0[0:512, cols], qkv1[0:512, cols]], axis=1)

    wk, wv = weight(1), weight(2)
    g = nn(wk, dkt[...]) + nn(wv, dvt[...])
    send_ref[...] = g[:, 512:1024].astype(BF16)
    g0 = g[:, 0:512] + nn(weight(0), dqt[...])
    own_ref[...] = g0[:, 0:256]
    par_ref[...] = g0[:, 256:512]


def last_kernel(tb, own, sib, par, x0, mg, log, vecs, e0, e1, e2, e3, grad_ref, sums_ref, gw):
    gather_gate(tb, (e0, e1, e2, e3), 128, gw)
    total = own[...] + sib[:, 0:256].astype(F32) + par[...].astype(F32)
    ng = total.T + nt(log[...], gw[...])
    unit, inverse = norm_unit(x0[...].astype(F32))
    g = ng * vecs[0:1, :]
    back = inverse * (g - jnp.mean(g, axis=-1, keepdims=True) - unit * jnp.mean(g * unit, axis=-1, keepdims=True))
    grad_ref[...] = mg[...] + back
    sums_ref[...] = jnp.zeros((8, 512), F32)
    sums_ref[0:1, :] = jnp.sum(ng * unit, axis=0, keepdims=True)
    sums_ref[1:2, :] = jnp.sum(ng, axis=0, keepdims=True)


def pack_kernel(
    pos, w_in, w_back, w_out, g1, g2, wq, wk, wv, *refs,
):
    vectors, (s_ref, e_ref, c_ref, qkv_ref, vecs), (sems, cut, *lines) = refs[:11], refs[11:16], refs[16:]
    start = pl.multiple_of((pos[4] & 3) * 128, 128)
    moves = [
        (w_in.at[:, pl.ds(start, 128)], cut),
        (w_back.at[pl.ds(start, 128), :], s_ref.at[128:256, :]),
        (w_out, e_ref.at[0:128, :]),
        (g1, e_ref.at[128:256, :]),
        (g2, e_ref.at[256:384, :]),
        (w_out, c_ref.at[0:128, :]),
        (g1, c_ref.at[128:256, :]),
        (g2, c_ref.at[256:384, :]),
        (w_in, c_ref.at[392:904, :]),
        (w_back, c_ref.at[904:1416, :]),
        (wq, qkv_ref.at[0:512, 0:128]),
        (wk, qkv_ref.at[0:512, 128:256]),
        (wv, qkv_ref.at[0:512, 256:384]),
    ] + list(zip(vectors, lines))
    copies = [pltpu.make_async_copy(src, dst, sems.at[i]) for i, (src, dst) in enumerate(moves)]
    for copy in copies:
        copy.start()
    for copy in copies:
        copy.wait()
    for i, v in enumerate(lines[:9]):
        vecs[i : i + 1, :] = v[...].astype(F32).reshape(1, 512)
    bq = lines[9][...].astype(F32).reshape(1, 128)
    bv = lines[10][...].astype(F32).reshape(1, 128)
    vecs[9:16, :] = jnp.zeros((7, 512), F32)
    s_ref[0:128, :] = cut[...].astype(F32).T.astype(BF16)
    bias = vecs[8:9, pl.ds(start, 128)]
    s_ref[256:264, :] = jnp.broadcast_to(jnp.concatenate([bias] * 4, axis=1), (8, 512)).astype(BF16)
    b_in = jnp.broadcast_to(vecs[8:9, :], (8, 512)).astype(BF16)
    e_ref[384:392, :] = b_in
    c_ref[384:392, :] = b_in
    for i, bias in enumerate((bq, jnp.zeros_like(bq), bv)):
        qkv_ref[512:520, 128 * i : 128 * i + 128] = jnp.broadcast_to(bias, (8, 128)).astype(BF16)


def half_rows_kernel(tb, keep, recv, out_ref):
    out_ref[...] = (keep[384:, :] + recv[384:, :].astype(F32)).astype(BF16)


def half_columns_kernel(tb, keep, recv, out_ref):
    half = keep.shape[1]
    out_ref[...] = (keep[...] + recv[:, half:].astype(F32)).astype(BF16)


def padded(rows, n_dp):
    unit = 8 * n_dp
    return -(-rows // unit) * unit


def bit_of(pos, b):
    return (pos[4] >> b) & 1


def sum_into(dst, at, addends, rows):
    value = None
    for ref, start in addends:
        block = ref[start : start + rows, :].astype(F32)
        value = block if value is None else value + block
    dst[at : at + rows, :] = value


def cut_rows(total, at, rows, bit, own, own_at, send, send_at):
    half = rows // 2
    mine = pl.multiple_of(at + bit * half, 8)
    other = pl.multiple_of(at + (1 - bit) * half, 8)
    own[own_at : own_at + half, :] = total[pl.ds(mine, half), :]
    send[send_at : send_at + half, :] = total[pl.ds(other, half), :].astype(BF16)


def pick(refs, groups):
    it = iter(refs)
    return [(rows, [(next(it), start) for start in starts]) for rows, starts in groups]


def halves_kernel(pos, *refs, parts, rows, bits):
    count = sum(len(starts) for groups in parts for _, starts in groups)
    ins, (own1, send1, own2, send2, total) = refs[:count], refs[count:]
    used = 0
    for groups, bit, own, send in zip(parts, bits, (own1, own2), (send1, send2)):
        need = sum(len(starts) for _, starts in groups)
        at = 0
        for size, addends in pick(ins[used : used + need], groups):
            sum_into(total, at, addends, size)
            at += size
        used += need
        if at < rows:
            total[at:, :] = jnp.zeros((rows - at, 512), F32)
        cut_rows(total, 0, rows, bit_of(pos, bit), own, 0, send, 0)


def merge_kernel(pos, own1, recv1, own2, recv2, own, send, total, *, bit):
    rows = own1.shape[0]
    for i, (o, r) in enumerate(((own1, recv1), (own2, recv2))):
        total[...] = o[...] + r[...].astype(F32)
        cut_rows(total, 0, rows, bit_of(pos, bit), own, i * rows // 2, send, i * rows // 2)


def both_kernel(pos, own0, recv0, own, send, total, *, bit):
    rows = own0.shape[0] // 2
    total[...] = own0[...] + recv0[...].astype(F32)
    for i in range(2):
        cut_rows(total, i * rows, rows, bit_of(pos, bit), own, i * rows // 2, send, i * rows // 2)


def fold_kernel(pos, own, recv, *refs, small):
    out = refs[-1]
    rows = own.shape[0]
    out[0:rows, :] = (own[...] + recv[...].astype(F32)).astype(BF16)
    out[rows : rows + 8, :] = jnp.zeros((8, 512), BF16)
    at = 0
    for first, size, starts in small:
        value = None
        for ref, start in zip(refs[at : at + len(starts)], starts):
            block = ref[start : start + size, :].astype(F32)
            value = block if value is None else value + block
        out[rows + first : rows + first + size, :] = value.astype(BF16)
        at += len(starts)


def stack_kernel(pos, held, recv, out):
    size = held.shape[0]
    out[0:size] = held[...]
    out[size:] = recv[...]


def part_kernel(pos, held, recv, out1, out2):
    size, rows = held.shape[0], (held.shape[1] - 8) // 2
    for i, r in enumerate((held, recv)):
        at = slice(i * size, i * size + size)
        out1[at, 0:rows, :] = r[:, 0:rows, :]
        out1[at, rows : rows + 8, :] = r[:, 2 * rows :, :]
        out2[at] = r[:, rows : 2 * rows, :]


def pair_kernel(pos, held1, recv1, held2, recv2, out1, out2):
    for out, h, r in ((out1, held1, recv1), (out2, held2, recv2)):
        size = h.shape[0]
        out[0:size] = h[...]
        out[size:] = r[...]


def unpack_kernel(pos, held1, recv1, held2, recv2, *refs, plans, orders):
    outs, scratch = refs[:-1], refs[-1]
    rows = held2.shape[1]
    used = 0
    for plan, order, blocks in zip(plans, orders, ((held1, recv1), (held2, recv2))):
        place = 0
        for b in order:
            place = place * 2 + bit_of(pos, b)
        each = blocks[0].shape[0]
        for i in range(2 * each):
            at = pl.multiple_of((place ^ i) * rows, 8)
            scratch[pl.ds(at, rows), :] = blocks[i // each][i % each, 0:rows, :].astype(F32)
        for start, size, flip in plan:
            block = scratch[start : start + size, :]
            outs[used][...] = block.T if flip else block
            used += 1
    total = jnp.zeros((8, 512), F32)
    for r in (held1, recv1):
        total = total + jnp.sum(r[:, rows:, :].astype(F32), axis=0)
    outs[used][...] = total


def body(
    layer_input, segments, norm1_gain, norm1_bias, w_query, b_query, w_key, w_value, b_value,
    w_out, b_out, gate1_w, gate1_b, norm2_gain, norm2_bias, w_in, b_in, w_back, b_back,
    gate2_w, gate2_b, cotangent, *, n_dp,
):
    def hop(value, mask):
        return lax.ppermute(value, "tensor", [(i, i ^ mask) for i in range(4)])

    def dhop(value, mask):
        return lax.ppermute(value, "dp", [(i, i ^ mask) for i in range(n_dp)])

    def after(value, *deps):
        return lax.optimization_barrier((value,) + deps)[0]

    t = lax.axis_index("tensor").astype(jnp.int32)
    me = lax.axis_index("dp").astype(jnp.int32)
    tb = jnp.where(jnp.arange(8) < 4, t ^ jnp.array(LOCAL + (0,) * 4, jnp.int32), me)
    seg = segments
    x0 = layer_input
    last = [None]

    def step(kernel, outs, args, name, scratch=(), smem=1, space=VM, then=(), limit=None):
        pos = tb if last[0] is None else after(tb, last[0], *then)
        got = call(kernel, outs, [pos] + args, smem=smem, scratch=scratch, name=name, space=space, limit=limit)
        last[0] = got[0]
        return got

    x1 = hop(x0, PX)
    x2 = hop(x0, 1)
    s0, e0, c0, qkv0, vecs = step(
        pack_kernel,
        [sds((264, 512), BF16), sds((392, 512), BF16), sds((1416, 512), BF16), sds((520, 384), BF16), sds((16, 512), F32)],
        [w_in, w_back, w_out, gate1_w, gate2_w, w_query, w_key, w_value, norm1_gain, norm1_bias, b_out, gate1_b,
         norm2_gain, norm2_bias, b_back, gate2_b, b_in, b_query, b_value],
        "pack",
        [pltpu.SemaphoreType.DMA((24,)), pltpu.VMEM((512, 128), BF16)]
        + [pltpu.VMEM((512,), BF16)] * 9 + [pltpu.VMEM((128,), BF16)] * 2,
        space=pl.BlockSpec(memory_space=pltpu.MemorySpace.HBM), limit=60 * 1024 * 1024,
    )
    qkv1 = hop(qkv0, 1)
    sy = hop(s0, PX)
    x3 = hop(x1, 1)
    e1 = hop(after(e0, x1), PX)
    c2 = hop(after(c0, qkv1), 1)

    n, qt0, qt1, k, vt, p1, ot1, att1, invl1 = step(
        first_kernel,
        [
            sds((1024, 512), BF16), sds((256, 256), BF16), sds((256, 256), BF16), sds((1024, 256), BF16),
            sds((256, 1024), BF16), sds((4, 1024, 256), BF16), sds((256, 256), BF16), sds((256, 256), BF16),
            sds((4, 8, 256), F32),
        ],
        [seg, seg, x0, x1, x2, x3, vecs, qkv0, qkv1],
        "first", ATT_SCRATCH, 2,
    )
    attp = hop(att1, PX)
    sy = after(sy, att1)
    sx = dhop(sy, 1)
    sz = dhop(sy, 2)
    e3 = hop(after(e1, att1), 1)
    p0, ot0, att0, invl0 = step(
        second_kernel,
        [sds((4, 1024, 256), BF16), sds((256, 256), BF16), sds((256, 256), BF16), sds((4, 8, 256), F32)],
        [seg, seg, qt0, k, vt],
        "second", ATT_SCRATCH, 2,
    )
    v, kt = step(prepare_kernel, [sds((1024, 256), BF16), sds((256, 1024), BF16)], [n, k, qkv0, qkv1], "prepare")
    n2, mid, branch, gate = step(
        out_kernel,
        [sds((256, 512), BF16), sds((256, 512), F32), sds((256, 512), F32), sds((256, 512), F32)],
        [x0, n, att0, attp, vecs, e0, e1, c2, e3],
        "out", [pltpu.VMEM((512, 512), BF16)],
    )
    n2p = hop(n2, PX)
    sxz = dhop(after(sz, n2), 1)
    total0, hid, slope0 = step(
        ffn_first_kernel,
        [sds((256, 512), F32), sds((256, 1024), BF16), sds((256, 1024), BF16)],
        [n2, vecs, w_in, w_back, c2],
        "ffn_first",
    )
    quarters = [sy, hop(sy, 1), sx, hop(sx, 1), sz, hop(sz, 1)]
    sxz = after(sxz, total0)
    quarters = quarters + [sxz, hop(sxz, 1)]
    result, fg, ltg, slope1 = step(
        ffn_kernel,
        [sds((256, 512), BF16), sds((256, 512), BF16), sds((256, 512), BF16), sds((256, 1024), BF16)],
        [n2, mid, cotangent, vecs, e0, e1, c2, e3, total0] + quarters,
        "ffn", [pltpu.VMEM((512, 512), BF16)],
    )
    fgp = hop(fg, PX)
    dot0, dotp, mg, bg, log, hg, sums = step(
        back_kernel,
        [
            sds((256, 256), BF16), sds((256, 256), BF16), sds((256, 512), F32), sds((256, 512), BF16),
            sds((256, 512), BF16), sds((256, 1024), BF16), sds((8, 512), F32),
        ],
        [fg, ltg, slope0, slope1, mid, branch, gate, cotangent, vecs, e0, e1, c2, e3, w_in, w_back] + quarters,
        "back", [pltpu.VMEM((512, 512), BF16)],
    )
    dot1 = hop(dotp, PX)
    back_scratch = [
        pltpu.VMEM((256, 256), F32), pltpu.VMEM((4, 128, 256), BF16), pltpu.VMEM((256, 256), BF16),
        pltpu.VMEM((4, 8, 256), F32),
    ]
    dk0, dv0, dq0 = step(
        back_first_kernel,
        [sds((256, 1024), F32), sds((256, 1024), F32), sds((256, 256), BF16)],
        [seg, p0, dot0, ot0, invl0, qt0, kt, v],
        "attn_back0", back_scratch, 2,
    )
    bkeep, bsend, slopep = step(
        ffn_back_weight_kernel,
        [sds((512, 512), F32), sds((512, 512), BF16), sds((256, 1024), BF16)],
        [n2p, fg, fgp, hid, vecs, w_in, c2],
        "ffn_back_weight",
    )
    brecv = hop(bsend, 1)
    ikeep, isend = step(
        ffn_in_weight_kernel,
        [sds((520, 512), F32), sds((520, 512), BF16)],
        [n2, n2p, fgp, hg, slopep, w_back, c2],
        "ffn_in_weight",
    )
    irecv = hop(isend, 1)
    skeep, ssend = step(
        small_weight_kernel,
        [sds((776, 512), F32), sds((776, 512), BF16)],
        [n, n2, ltg, log, att0, attp, bg, sums],
        "small_weight", [pltpu.VMEM((512, 512), F32), pltpu.VMEM((512, 512), F32)], then=(dot1,),
    )
    srecv = hop(ssend, 1)
    bits = n_dp.bit_length() - 1

    def halves(parts1, parts2, rows):
        arrays = [a for parts in (parts1, parts2) for _, group in parts for a, _ in group]
        static = tuple(
            tuple((m, tuple(start for _, start in group)) for m, group in parts) for parts in (parts1, parts2)
        )
        shapes = [sds((rows // 2, 512), F32), sds((rows // 2, 512), BF16)] * 2
        o1, s1, o2, s2 = step(
            functools.partial(halves_kernel, parts=static, rows=rows, bits=(0, 1)),
            shapes, arrays, "halves", [pltpu.VMEM((rows, 512), F32)],
        )
        return o1, dhop(s1, 1), o2, dhop(s2, 2)

    def quarter_step(o1, r1, o2, r2):
        rows = o1.shape[0]
        shapes = [sds((rows // 2, 512), F32), sds((rows // 2, 512), BF16)] * 2
        o1, s1, o2, s2 = step(
            functools.partial(halves_kernel, parts=(((rows, (0, 0)),),) * 2, rows=rows, bits=(1, 0)),
            shapes, [o1, r1, o2, r2], "quarters", [pltpu.VMEM((rows, 512), F32)],
        )
        return o1, dhop(s1, 2), o2, dhop(s2, 1)

    def merge_step(o1, r1, o2, r2):
        rows = o1.shape[0]
        own, sent = step(
            functools.partial(merge_kernel, bit=2), [sds((rows, 512), F32), sds((rows, 512), BF16)],
            [o1, r1, o2, r2], "merge", [pltpu.VMEM((rows, 512), F32)],
        )
        pair = own, dhop(sent, 4)
        for b in range(3, bits):
            rows = rows // 2
            own, sent = step(
                functools.partial(both_kernel, bit=b), [sds((rows, 512), F32), sds((rows, 512), BF16)],
                list(pair), "both", [pltpu.VMEM((2 * rows, 512), F32)],
            )
            pair = own, dhop(sent, 1 << b)
        return pair

    def fold_step(own, recv, small):
        rows = own.shape[0]
        static = tuple((f, m, tuple(start for _, start in group)) for f, m, group in small)
        arrays = [a for _, _, group in small for a, _ in group]
        held = step(
            functools.partial(fold_kernel, small=static), [sds((rows + 8, 512), BF16)], [own, recv] + arrays, "fold"
        )[0][None]
        for b in range(bits - 1, 2, -1):
            shape = (2 * held.shape[0],) + held.shape[1:]
            held = step(stack_kernel, [sds(shape, BF16)], [held, dhop(held, 1 << b)], "stack")[0]
        return held, dhop(held, 4)

    def part_step(held, recv):
        size, rows = 2 * held.shape[0], (held.shape[1] - 8) // 2
        h1, h2 = step(part_kernel, [sds((size, rows + 8, 512), BF16), sds((size, rows, 512), BF16)], [held, recv], "part")
        return h1, dhop(h1, 2), h2, dhop(h2, 1)

    def pair_step(h1, r1, h2, r2):
        shapes = [sds((2 * h.shape[0],) + h.shape[1:], BF16) for h in (h1, h2)]
        h1, h2 = step(pair_kernel, shapes, [h1, r1, h2, r2], "pair")
        return h1, dhop(h1, 1), h2, dhop(h2, 2)

    def unpack_step(h1, r1, h2, r2, plans):
        shapes = [sds((512, size) if flip else (size, 512), F32) for plan in plans for _, size, flip in plan]
        rest = tuple(range(2, bits))
        rows = 2 * h2.shape[0] * h2.shape[1]
        return step(
            functools.partial(unpack_kernel, plans=plans, orders=((0, 1) + rest, (1, 0) + rest)),
            shapes + [sds((8, 512), F32)], [h1, r1, h2, r2], "unpack", [pltpu.VMEM((rows, 512), F32)],
        )

    f = halves([(512, [(bkeep, 0), (brecv, 0)])], [(512, [(ikeep, 0), (irecv, 0)])], padded(512, n_dp))
    (spar,) = step(half_rows_kernel, [sds((392, 512), BF16)], [skeep, srecv], "half_rows")
    sparr = hop(spar, PX)

    dqt, dkt, dvt, akeep, asend = step(
        back_second_kernel,
        [
            sds((256, 512), BF16), sds((256, 1024), BF16), sds((256, 1024), BF16), sds((392, 512), F32),
            sds((392, 512), BF16),
        ],
        [seg, p1, dot1, ot1, invl1, qt1, kt, v, dk0, dv0, dq0, n],
        "attn_back1", [pltpu.VMEM((256, 1024), F32), pltpu.VMEM((256, 1024), F32)] + back_scratch, 2,
    )
    arecv = hop(asend, 1)
    gown, gpar, gsend = step(
        input_kernel,
        [sds((512, 256), F32), sds((512, 256), F32), sds((512, 512), BF16)],
        [dqt, dkt, dvt, qkv0, qkv1],
        "input_grad",
    )
    gsib = hop(gsend, 1)
    f = quarter_step(*f)
    a = halves(
        [(384, [(akeep, 0), (arecv, 0)])], [(384, [(skeep, 0), (srecv, 0), (sparr, 0)])], padded(384, n_dp)
    )
    (gsum,) = step(half_columns_kernel, [sds((512, 256), BF16)], [gpar, gsib], "half_columns")
    gp = hop(gsum, PX)
    f = merge_step(*f)
    a = quarter_step(*a)
    input_grad, sums1 = step(
        last_kernel,
        [sds((256, 512), F32), sds((8, 512), F32)],
        [gown, gsib, gp, x0, mg, log, vecs, e0, e1, c2, e3],
        "last", [pltpu.VMEM((512, 512), BF16)],
    )
    sums1_b = hop(sums1, PX)
    sums1_a = hop(sums1, 1)
    tail = [(skeep, 773), (srecv, 773), (sparr, 389)]
    f = fold_step(*f, [(0, 1, [(ikeep, 512), (irecv, 512)]), (1, 1, tail)])
    a = merge_step(*a)
    sums1_c = hop(after(sums1_b, a[0]), 1)
    f = part_step(*f)
    group = [(skeep, 768), (srecv, 768), (sparr, 384)]
    a = fold_step(
        *a,
        [(0, 2, [(sums1, 0), (sums1_a, 0), (sums1_b, 0), (sums1_c, 0)]), (2, 1, [(akeep, 384), (arecv, 384)]),
         (3, 5, group)],
    )
    f = pair_step(*f)
    a = part_step(*a)
    g_wback, g_win, f_small = unpack_step(*f, (((0, 512, False),), ((0, 512, False),)))
    a = pair_step(*a)
    plans = (
        ((0, 128, True), (128, 128, True), (256, 128, True)),
        ((0, 128, False), (128, 128, False), (256, 128, False)),
    )
    g_q, g_k, g_v, g_g2, g_g1, g_wo, a_small = unpack_step(*a, plans)
    return (
        result,
        input_grad,
        a_small[0],
        a_small[1],
        g_q,
        a_small[2, 0:128],
        g_k,
        g_v,
        a_small[2, 128:256],
        g_wo,
        a_small[5],
        g_g1,
        a_small[6],
        a_small[7],
        f_small[1],
        g_win,
        f_small[0],
        g_wback,
        a_small[3],
        g_g2,
        a_small[4],
    )


def solution(mesh):
    tok = P(("dp", "tensor"), None)
    col = P(None, "tensor")
    row = P("tensor", None)
    vec = P("tensor")
    rep = P()
    return jax.shard_map(
        functools.partial(body, n_dp=mesh.shape["dp"]),
        mesh=mesh,
        in_specs=(
            tok, P("dp", None), rep, rep, col, vec, col, col, vec, row, rep, row, rep, rep, rep,
            col, vec, row, rep, row, rep, tok,
        ),
        out_specs=(
            tok, tok, rep, rep, col, vec, col, col, vec, row, rep, row, rep, rep, rep,
            col, vec, row, rep, row, rep,
        ),
        check_vma=False,
    )
```

```python
import functools
import math

import jax
import jax.numpy as jnp
from jax import lax
from jax.experimental import pallas as pl
from jax.experimental.pallas import tpu as pltpu
from jax.sharding import PartitionSpec as P

HD = 64
EPSILON = 1e-05
F32 = jnp.float32
BF16 = jnp.bfloat16
NEG = -1e30
PX = 2
LOCAL = (0, PX, 1, 1 ^ PX)
SPARE = 4 * 1024 * 1024
HEAVY = 10**10
LIGHT = 0
EASY = ("pair_a", "part_f", "halves_f", "halves_a", "input_grad")


def nn(a, b):
    return lax.dot_general(a, b, (((1,), (0,)), ((), ())), preferred_element_type=F32)


def nt(a, b):
    return lax.dot_general(a, b, (((1,), (1,)), ((), ())), preferred_element_type=F32)


def tn(a, b):
    return lax.dot_general(a, b, (((0,), (0,)), ((), ())), preferred_element_type=F32)


VM = pl.BlockSpec(memory_space=pltpu.VMEM)
SM = pl.BlockSpec(memory_space=pltpu.SMEM)


def call(body, outs, args, smem=0, scratch=(), name=None, space=VM, limit=None, cost=0):
    nbytes = sum(a.size * a.dtype.itemsize for a in args) + sum(o.size * o.dtype.itemsize for o in outs)
    held = sum(math.prod(s.shape) * 4 for s in scratch)
    limit = limit or nbytes + held + SPARE
    return pl.pallas_call(
        body,
        out_shape=tuple(outs),
        in_specs=[SM] * smem + [space] * (len(args) - smem),
        out_specs=tuple([VM] * len(outs)),
        scratch_shapes=list(scratch),
        compiler_params=pltpu.CompilerParams(vmem_limit_bytes=limit),
        cost_estimate=pl.CostEstimate(flops=cost, bytes_accessed=0, transcendentals=0),
        name=name,
    )(*args)


def sds(shape, dtype):
    return jax.ShapeDtypeStruct(shape, dtype)


def norm_unit(values):
    centred = values - jnp.mean(values, axis=-1, keepdims=True)
    spread = jnp.mean(centred * centred, axis=-1, keepdims=True)
    inverse = lax.rsqrt(spread + EPSILON)
    return centred * inverse, inverse


def sigmoid(v):
    return 1.0 / (1.0 + jnp.exp(-v))


C0 = 0.7978845608028654
C1 = 0.044715


def gelu_parts(u):
    square = u * u
    t = jnp.tanh(C0 * u * (1.0 + C1 * square))
    half = 0.5 * (1.0 + t)
    value = u * half
    slope = half + (0.5 * C0) * u * (1.0 - t * t) * (1.0 + (3.0 * C1) * square)
    return value, slope


def attend_query_block(qb, tb, segs, segv, qz, k, vt, p_ref, ot_ref, invl_ref, s_sc, m_sc, l_sc, o_sc, segc):
    rows = 256
    tq = tb[qb]
    m_sc[...] = jnp.full(m_sc.shape, NEG, F32)
    l_sc[...] = jnp.zeros(l_sc.shape, F32)
    o_sc[...] = jnp.zeros(o_sc.shape, F32)
    seg_q = segv[0:1, pl.ds(pl.multiple_of(tq * rows, rows), rows)].astype(F32)

    def active(kb):
        tk = tb[kb]
        return (tk <= tq) & (segs[0, tk * rows + rows - 1] >= segs[0, tq * rows])

    @pl.loop(0, 4)
    def _(kb):
        @pl.when(active(kb))
        def _():
            tk = tb[kb]
            krows = pl.ds(pl.multiple_of(kb * rows, rows), rows)
            kpos = tk * rows + lax.broadcasted_iota(jnp.int32, (rows, rows), 0)
            qpos = tq * rows + lax.broadcasted_iota(jnp.int32, (rows, rows), 1)
            seg_k = segc[pl.ds(pl.multiple_of(tk * rows, rows), rows), 0:1]
            bias = jnp.where((kpos <= qpos) & (seg_k == seg_q), 0.0, NEG)
            for h in range(4):
                pair = 128 * (h // 2)
                s = nn(k[krows, pair : pair + 128], qz[h]) + bias
                s_sc[h, krows, :] = s
                m_sc[h] = jnp.maximum(m_sc[h], jnp.max(s.reshape(rows // 8, 8, rows), axis=0))

    for h in range(4):
        m_sc[h] = jnp.broadcast_to(jnp.max(m_sc[h], axis=0, keepdims=True), (8, rows))

    @pl.loop(0, 4)
    def _(kb):
        @pl.when(active(kb))
        def _():
            krows = pl.ds(pl.multiple_of(kb * rows, rows), rows)
            for h in range(4):
                e = jnp.exp(s_sc[h, krows, :] - m_sc[h, 0:1, :])
                l_sc[h] = l_sc[h] + jnp.sum(e.reshape(rows // 8, 8, rows), axis=0)
                pb = e.astype(BF16)
                p_ref[h, krows, :] = pb
                o_sc[h] = o_sc[h] + nn(vt[64 * h : 64 * h + 64, krows], pb)

    for h in range(4):
        invl = 1.0 / jnp.sum(l_sc[h], axis=0, keepdims=True)
        invl_ref[h] = jnp.broadcast_to(invl, (8, rows))
        ot_ref[64 * h : 64 * h + 64, :] = (o_sc[h] * invl).astype(BF16)


def fill_qz(qz, qt):
    zero = jnp.zeros((64, 256), BF16)
    for h in range(4):
        mine = qt[64 * h : 64 * h + 64, :]
        qz[h] = jnp.concatenate([mine, zero] if h % 2 == 0 else [zero, mine], axis=0)


def fill_segc(segc, segv):
    for t in range(4):
        row = jnp.broadcast_to(segv[0:1, 256 * t : 256 * t + 256].astype(F32), (128, 256))
        segc[256 * t : 256 * t + 256, :] = row.T


def weight_of(w, part):
    cols = slice(128 * part, 128 * part + 128)
    return jnp.concatenate([w[0][:, cols], w[1][0:256, cols]], axis=0)


def bias_of(w, part):
    return w[1][256:257, 128 * part : 128 * part + 128].astype(F32)


def project(n, w, c, k_ref, vt_ref, blocks):
    cols = slice(128 * c, 128 * c + 128)
    k = nn(n, weight_of(w, 1)).astype(BF16)
    vt = (nn(n, weight_of(w, 2)) + bias_of(w, 2)).T.astype(BF16)
    for i, at in enumerate(blocks):
        k_ref[at : at + 256, cols] = k[256 * i : 256 * i + 256]
        vt_ref[cols, at : at + 256] = vt[:, 256 * i : 256 * i + 256]


def query_of(n, w):
    q = nn(n, weight_of(w, 0)) + bias_of(w, 0)
    return (q.astype(BF16).astype(F32) * HD ** (-0.5)).T.astype(BF16)


def chip_kernel(pos, x0, x2, vecs, qa0, qb0, qa1, qb1, n_ref, qt_ref, k_ref, vt_ref):
    for i, x in enumerate((x0, x2)):
        unit, _ = norm_unit(x[...].astype(F32))
        n_ref[256 * i : 256 * i + 256, :] = (unit * vecs[0:1, :] + vecs[1:2, :]).astype(BF16)
    n = n_ref[...]
    for c, w in enumerate(((qa0, qb0), (qa1, qb1))):
        qt_ref[128 * c : 128 * c + 128, :] = query_of(n[0:256], w)
        project(n, w, c, k_ref, vt_ref, (0, 256))


def first_kernel(
    tb, segs, segv, x1, x3, vecs, qa0, qb0, qa1, qb1, na, ka, vta,
    n_ref, qt1_ref, k_ref, vt_ref, p_ref, ot_ref, att_ref, invl_ref,
    qz, s_sc, m_sc, l_sc, o_sc, segc,
):
    for i, x in enumerate((x1, x3)):
        unit, _ = norm_unit(x[...].astype(F32))
        n_ref[512 * i + 256 : 512 * i + 512, :] = (unit * vecs[0:1, :] + vecs[1:2, :]).astype(BF16)
    n = jnp.concatenate([n_ref[256:512, :], n_ref[768:1024, :]], axis=0)
    for c, w in enumerate(((qa0, qb0), (qa1, qb1))):
        qt1_ref[128 * c : 128 * c + 128, :] = query_of(n[0:256], w)
        project(n, w, c, k_ref, vt_ref, (256, 768))
    for i in range(2):
        src, dst = slice(256 * i, 256 * i + 256), slice(512 * i, 512 * i + 256)
        n_ref[dst, :] = na[src, :]
        k_ref[dst, :] = ka[src, :]
        vt_ref[:, dst] = vta[:, src]
    fill_segc(segc, segv)
    fill_qz(qz, qt1_ref)
    attend_query_block(1, tb, segs, segv, qz, k_ref, vt_ref, p_ref, ot_ref, invl_ref, s_sc, m_sc, l_sc, o_sc, segc)
    att_ref[...] = ot_ref[...].astype(F32).T.astype(BF16)


def second_kernel(
    tb, segs, segv, qt0, k, vt,
    p_ref, ot_ref, att_ref, invl_ref,
    qz, s_sc, m_sc, l_sc, o_sc, segc,
):
    fill_segc(segc, segv)
    fill_qz(qz, qt0)
    attend_query_block(0, tb, segs, segv, qz, k, vt, p_ref, ot_ref, invl_ref, s_sc, m_sc, l_sc, o_sc, segc)
    att_ref[...] = ot_ref[...].astype(F32).T.astype(BF16)


ATT_SCRATCH = (
    pltpu.VMEM((4, 128, 256), BF16),
    pltpu.VMEM((4, 1024, 256), F32),
    pltpu.VMEM((4, 8, 256), F32),
    pltpu.VMEM((4, 8, 256), F32),
    pltpu.VMEM((4, 64, 256), F32),
    pltpu.VMEM((1024, 128), F32),
)


def gather_gate(tb, pieces, start, scratch):
    for i, piece in enumerate(pieces):
        scratch[pl.ds(pl.multiple_of(tb[i] * 128, 128), 128), :] = piece[start : start + 128, :]


def gather_gate_two(pos, g2, c2, pieces, scratch):
    scratch[pl.ds(pl.multiple_of(pos[0] * 128, 128), 128), :] = g2[...]
    scratch[pl.ds(pl.multiple_of(pos[2] * 128, 128), 128), :] = c2[256:384, :]
    for i, piece in enumerate(pieces):
        quarter = (pos[4] ^ (i // 2)) & 3
        at = pos[1 + 2 * (i % 2)] * 128 + quarter * 32
        rows = piece.shape[0]
        scratch[pl.ds(pl.multiple_of(at, 32), 32), :] = piece[rows - 32 : rows, :]


def out_kernel(
    tb, x0, n, att, attp, vecs, e0, e1, e2, e3,
    n2_ref, mid_ref, branch_ref, gate_ref,
    gw,
):
    gather_gate(tb, (e0, e1, e2, e3), 128, gw)
    branch = nn(att[:, 0:128], e0[0:128, :]) + nn(att[:, 128:256], e2[0:128, :])
    branch = branch + nn(attp[:, 0:128], e1[0:128, :]) + nn(attp[:, 128:256], e3[0:128, :])
    branch = branch + vecs[2:3, :]
    gate = sigmoid(nn(n[0:256, :], gw[...]) + vecs[3:4, :])
    middle = x0[...].astype(F32) + gate * branch
    unit, _ = norm_unit(middle)
    n2_ref[...] = (unit * vecs[4:5, :] + vecs[5:6, :]).astype(BF16)
    mid_ref[...] = middle
    branch_ref[...] = branch
    gate_ref[...] = gate


def pair_up(a, b, start):
    return jnp.concatenate([a[start : start + 128, :], b[start : start + 128, :]], axis=0)


def pair_bias(a, b, row=256):
    return jnp.concatenate([a[row : row + 1, 0:128], b[row : row + 1, 0:128]], axis=1).astype(F32)


def cut_kernel(pos, sx, sz, a_ref, b_ref):
    a_ref[...] = sz[0:128, :]
    b_ref[...] = sx[128:296, :]


def ffn_first_kernel(
    tb, n2, vecs, win0, wback0, c2, s0, s1, s2, s3, s4, s5,
    total_ref, hid_ref, slope_ref, slope1_ref,
):
    n2v = n2[...]
    total = jnp.zeros((256, 512), F32)
    for i, (b, w, wb) in enumerate(((vecs[8:9, :], win0[...], wback0[...]), (c2[384:385, :], c2[392:904, :], c2[904:1416, :]))):
        value, slope = gelu_parts(nn(n2v, w) + b.astype(F32))
        value = value.astype(BF16)
        hid_ref[:, 512 * i : 512 * i + 512] = value
        slope_ref[:, 512 * i : 512 * i + 512] = slope.astype(BF16)
        total = total + nn(value, wb)
    for i, (a, b) in enumerate(((s0, s1), (s2, s3), (s4, s5))):
        value, slope = gelu_parts(nt(n2v, pair_up(a, b, 0)) + pair_bias(a, b))
        slope1_ref[:, 256 * i : 256 * i + 256] = slope.astype(BF16)
        total = total + nn(value.astype(BF16), pair_up(a, b, 128))
    total_ref[...] = total


def ffn_kernel(
    tb, n2, mid, ct, vecs, g2, c2, total0, s0, s1, s2, s3, s4, s5, a6, a7, b6, b7,
    out_ref, fg_ref, ltg_ref, slope_ref, gw,
):
    gather_gate_two(tb, g2, c2, (s0, s1, s2, s3, s4, s5, b6, b7), gw)
    n2v = n2[...]
    value, slope = gelu_parts(nt(n2v, pair_up(a6, a7, 0)) + pair_bias(b6, b7, 128))
    slope_ref[...] = slope.astype(BF16)
    ffn = total0[...] + nn(value.astype(BF16), pair_up(b6, b7, 0)) + vecs[6:7, :]
    gate = sigmoid(nn(n2v, gw[...]) + vecs[7:8, :])
    up = ct[...].astype(F32)
    out_ref[...] = (mid[...] + gate * ffn).astype(BF16)
    fg_ref[...] = (gate * up).astype(BF16)
    ltg_ref[...] = (up * ffn * (gate * (1.0 - gate))).astype(BF16)


def back_kernel(
    tb, fg, ltg, slope0, slope1, slope2, mid, branch, gate, ct, vecs, e0, e1, e2, e3, g2,
    win0, wback0, s0, s1, s2, s3, s4, s5, a6, a7, b6, b7,
    dot_ref, dotp_ref, mg_ref, bg_ref, log_ref, hg_ref, sums_ref,
    gw,
):
    gather_gate_two(tb, g2, e2, (s0, s1, s2, s3, s4, s5, b6, b7), gw)
    fgv = fg[...]
    ltgv = ltg[...]
    ng = nt(ltgv, gw[...])
    for i, (w, wb) in enumerate(((win0[...], wback0[...]), (e2[392:904, :], e2[904:1416, :]))):
        hg = (nt(fgv, wb) * slope0[:, 512 * i : 512 * i + 512].astype(F32)).astype(BF16)
        hg_ref[:, 512 * i : 512 * i + 512] = hg
        ng = ng + nt(hg, w)
    for i, (a, b) in enumerate(((s0, s1), (s2, s3), (s4, s5))):
        part = slope1[:, 256 * i : 256 * i + 256]
        hg = (nt(fgv, pair_up(a, b, 128)) * part.astype(F32)).astype(BF16)
        ng = ng + nn(hg, pair_up(a, b, 0))
    hg = (nt(fgv, pair_up(b6, b7, 0)) * slope2[...].astype(F32)).astype(BF16)
    ng = ng + nn(hg, pair_up(a6, a7, 0))
    unit, inverse = norm_unit(mid[...])
    g = ng * vecs[4:5, :]
    back = inverse * (g - jnp.mean(g, axis=-1, keepdims=True) - unit * jnp.mean(g * unit, axis=-1, keepdims=True))
    mg = ct[...].astype(F32) + back
    mg_ref[...] = mg
    gatev = gate[...]
    bg = (gatev * mg).astype(BF16)
    log = (mg * branch[...] * (gatev * (1.0 - gatev))).astype(BF16)
    bg_ref[...] = bg
    log_ref[...] = log
    dot_ref[0:128, :] = nt(e0[0:128, :], bg).astype(BF16)
    dot_ref[128:256, :] = nt(e2[0:128, :], bg).astype(BF16)
    dotp_ref[0:128, :] = nt(e1[0:128, :], bg).astype(BF16)
    dotp_ref[128:256, :] = nt(e3[0:128, :], bg).astype(BF16)
    rows = [fgv.astype(F32), ltgv.astype(F32), bg.astype(F32), log.astype(F32), ng * unit, ng]
    sums_ref[...] = jnp.zeros((8, 512), F32)
    for i, r in enumerate(rows):
        sums_ref[i : i + 1, :] = jnp.sum(r, axis=0, keepdims=True)


def ffn_back_weight_kernel(
    tb, n2p, fg, fgp, hid, vecs, win0, c2,
    keep_ref, send_ref, slope_ref,
):
    fgv, fgpv, n2pv = fg[...], fgp[...], n2p[...]
    for i, (b, w) in enumerate(((vecs[8:9, :], win0[...]), (c2[384:385, :], c2[392:904, :]))):
        cols = slice(512 * i, 512 * i + 512)
        value, slope = gelu_parts(nn(n2pv, w) + b.astype(F32))
        slope_ref[:, cols] = slope.astype(BF16)
        wback = tn(hid[:, cols], fgv) + tn(value.astype(BF16), fgpv)
        dst = keep_ref if i == 0 else send_ref
        dst[...] = wback.astype(dst.dtype)


def ffn_in_weight_kernel(
    tb, n2, n2p, fgp, hg, slope, wback0, c2,
    keep_ref, send_ref,
):
    n2v, n2pv, fgpv = n2[...], n2p[...], fgp[...]
    for i, wb in enumerate((wback0[...], c2[904:1416, :])):
        cols = slice(512 * i, 512 * i + 512)
        hgp = (nt(fgpv, wb) * slope[:, cols].astype(F32)).astype(BF16)
        hgo = hg[:, cols]
        win = tn(n2v, hgo) + tn(n2pv, hgp)
        bias = jnp.sum(hgo.astype(F32), axis=0, keepdims=True) + jnp.sum(hgp.astype(F32), axis=0, keepdims=True)
        dst = keep_ref if i == 0 else send_ref
        dst[0:512, :] = win.astype(dst.dtype)
        dst[512:520, :] = jnp.broadcast_to(bias, (8, 512)).astype(dst.dtype)


def small_weight_kernel(
    tb, n, n2, ltg, log, att, attp, bg, sums,
    keep_ref, send_ref,
    g1, g2,
):
    keep_ref[768:776, :] = sums[...]
    send_ref[768:776, :] = sums[...].astype(BF16)
    g2[...] = tn(n2[...], ltg[...])
    g1[...] = tn(n[0:256, :], log[...])
    bgv = bg[...]
    wo = (tn(att[:, 0:128], bgv), tn(attp[:, 0:128], bgv), tn(att[:, 128:256], bgv), tn(attp[:, 128:256], bgv))
    for i in range(4):
        src = pl.ds(pl.multiple_of(tb[i] * 128, 128), 128)
        dst = keep_ref if i < 2 else send_ref
        base = 384 * (i % 2)
        dst[base : base + 128, :] = g2[src, :].astype(dst.dtype)
        dst[base + 128 : base + 256, :] = g1[src, :].astype(dst.dtype)
        dst[base + 256 : base + 384, :] = wo[i].astype(dst.dtype)


def prepare_kernel(tb, n, k, qa0, qb0, qa1, qb1, v_ref, kt_ref):
    nv = n[...]
    for c, w in enumerate(((qa0, qb0), (qa1, qb1))):
        v = nn(nv, weight_of(w, 2)) + bias_of(w, 2)
        v_ref[:, 128 * c : 128 * c + 128] = v.astype(BF16)
    kt_ref[...] = k[...].astype(F32).T.astype(BF16)


def attend_back(qb, tb, segs, p, dot, ot, invl, qt, kt, v, dk, dv, dq, doz, dos, dlt):
    rows = 256
    tq = tb[qb]
    zero = jnp.zeros((64, rows), BF16)
    for h in range(4):
        hs = slice(64 * h, 64 * h + 64)
        scale = invl[h, 0:1, :]
        dv_h = dot[hs, :].astype(F32)
        delta = jnp.sum(dv_h * ot[hs, :].astype(F32), axis=0, keepdims=True) * scale
        dlt[h] = jnp.broadcast_to(delta, (8, rows))
        mine = (dv_h * scale).astype(BF16)
        dos[hs, :] = mine
        doz[h] = jnp.concatenate([mine, zero] if h % 2 == 0 else [zero, mine], axis=0)
    dq[...] = jnp.zeros(dq.shape, F32)

    @pl.loop(0, 4)
    def _(kb):
        tk = tb[kb]

        @pl.when((tk <= tq) & (segs[0, tk * rows + rows - 1] >= segs[0, tq * rows]))
        def _():
            ks = pl.ds(pl.multiple_of(kb * rows, rows), rows)
            for h in range(4):
                pair = 128 * (h // 2)
                hs = slice(64 * h, 64 * h + 64)
                ph = p[h, ks, :]
                dp = nn(v[ks, pair : pair + 128], doz[h])
                ds = (ph.astype(F32) * (dp - dlt[h, 0:1, :])).astype(BF16)
                dv[hs, ks] = dv[hs, ks] + nt(dos[hs, :], ph)
                dk[hs, ks] = dk[hs, ks] + nt(qt[hs, :], ds)
                dq[hs, :] = dq[hs, :] + nn(kt[hs, ks], ds)


def back_first_kernel(
    tb, segs, p, dot, ot, invl, qt, kt, v,
    dk_ref, dv_ref, dq_ref,
    dq, doz, dos, dlt,
):
    dk_ref[...] = jnp.zeros(dk_ref.shape, F32)
    dv_ref[...] = jnp.zeros(dv_ref.shape, F32)
    attend_back(0, tb, segs, p, dot, ot, invl, qt, kt, v, dk_ref, dv_ref, dq, doz, dos, dlt)
    dq_ref[...] = (dq[...] * HD ** (-0.5)).astype(BF16)


def back_second_kernel(
    tb, segs, p, dot, ot, invl, qt, kt, v, dk0, dv0, dq0, n,
    dqt_ref, dkt_ref, dvt_ref, keep_ref, send_ref,
    dk, dv, dq, doz, dos, dlt,
):
    dk[...] = dk0[...]
    dv[...] = dv0[...]
    attend_back(1, tb, segs, p, dot, ot, invl, qt, kt, v, dk, dv, dq, doz, dos, dlt)
    dqt_ref[:, 0:256] = dq0[...]
    dqt_ref[:, 256:512] = (dq[...] * HD ** (-0.5)).astype(BF16)
    dkt_ref[...] = dk[...].astype(BF16)
    dvt_ref[...] = dv[...].astype(BF16)
    nv = n[...]
    wq = nn(dqt_ref[...], nv[0:512, :])
    wk = nn(dkt_ref[...], nv)
    wv = nn(dvt_ref[...], nv)
    for i, w in enumerate((wq, wk, wv)):
        keep_ref[128 * i : 128 * i + 128, :] = w[0:128, :]
        send_ref[128 * i : 128 * i + 128, :] = w[128:256, :].astype(BF16)
    ones_q = jnp.ones((8, 512), BF16)
    ones_v = jnp.ones((8, 1024), BF16)
    bq = nt(ones_q, dqt_ref[...])
    bv = nt(ones_v, dvt_ref[...])
    empty = jnp.zeros((8, 256), F32)
    keep_ref[384:392, :] = jnp.concatenate([bq[:, 0:128], bv[:, 0:128], empty], axis=1)
    send_ref[384:392, :] = jnp.concatenate([bq[:, 128:256], bv[:, 128:256], empty], axis=1).astype(BF16)


def input_kernel(tb, dqt, dkt, dvt, qa0, qb0, qa1, qb1, own_ref, par_ref, send_ref):
    def weight(part):
        return jnp.concatenate([weight_of((qa0, qb0), part), weight_of((qa1, qb1), part)], axis=1)

    wk, wv = weight(1), weight(2)
    g = nn(wk, dkt[...]) + nn(wv, dvt[...])
    send_ref[...] = g[:, 512:1024].astype(BF16)
    g0 = g[:, 0:512] + nn(weight(0), dqt[...])
    own_ref[...] = g0[:, 0:256]
    par_ref[...] = g0[:, 256:512]


def last_kernel(tb, own, sib, par, x0, mg, log, vecs, e0, e1, e2, e3, grad_ref, sums_ref, gw):
    gather_gate(tb, (e0, e1, e2, e3), 128, gw)
    total = own[...] + sib[:, 0:256].astype(F32) + par[...].astype(F32)
    ng = total.T + nt(log[...], gw[...])
    unit, inverse = norm_unit(x0[...].astype(F32))
    g = ng * vecs[0:1, :]
    back = inverse * (g - jnp.mean(g, axis=-1, keepdims=True) - unit * jnp.mean(g * unit, axis=-1, keepdims=True))
    grad_ref[...] = mg[...] + back
    sums_ref[...] = jnp.zeros((8, 512), F32)
    sums_ref[0:1, :] = jnp.sum(ng * unit, axis=0, keepdims=True)
    sums_ref[1:2, :] = jnp.sum(ng, axis=0, keepdims=True)


def run_copies(moves, sems):
    copies = [pltpu.make_async_copy(src, dst, sems.at[i]) for i, (src, dst) in enumerate(moves)]
    for copy in copies:
        copy.start()
    for copy in copies:
        copy.wait()


def pack_kernel(pos, w_in, w_back, w_out, g1, g2, wq, wk, wv, *refs):
    vectors, (s_ref, e_ref, c_ref, qa_ref, qb_ref, vecs), (sems, cut, *lines) = refs[:11], refs[11:17], refs[17:]
    start = pl.multiple_of((pos[4] & 3) * 128, 128)
    gate = pl.multiple_of((pos[4] & 3) * 32, 32)
    moves = [
        (w_in.at[:, pl.ds(start, 128)], cut),
        (w_back.at[pl.ds(start, 128), :], s_ref.at[128:256, :]),
        (g2.at[pl.ds(gate, 32), :], s_ref.at[264:296, :]),
    ]
    for i, w in enumerate((wq, wk, wv)):
        cols = slice(128 * i, 128 * i + 128)
        moves.append((w.at[0:256, :], qa_ref.at[:, cols]))
        moves.append((w.at[256:512, :], qb_ref.at[0:256, cols]))
    late = [
        (w_out, e_ref.at[0:128, :]),
        (g1, e_ref.at[128:256, :]),
        (w_out, c_ref.at[0:128, :]),
        (g1, c_ref.at[128:256, :]),
        (g2, c_ref.at[256:384, :]),
        (w_in, c_ref.at[392:904, :]),
        (w_back, c_ref.at[904:1416, :]),
    ]
    moves = moves + list(zip(vectors, lines)) + late
    copies = [pltpu.make_async_copy(src, dst, sems.at[i]) for i, (src, dst) in enumerate(moves)]
    for copy in copies:
        copy.start()
    for copy in copies[: len(moves) - len(late)]:
        copy.wait()
    for i, v in enumerate(lines[:9]):
        vecs[i : i + 1, :] = v[...].astype(F32).reshape(1, 512)
    bq = lines[9][...].astype(F32).reshape(1, 128)
    bv = lines[10][...].astype(F32).reshape(1, 128)
    vecs[9:16, :] = jnp.zeros((7, 512), F32)
    s_ref[0:128, :] = cut[...].astype(F32).T.astype(BF16)
    bias = vecs[8:9, pl.ds(start, 128)]
    s_ref[256:264, :] = jnp.broadcast_to(jnp.concatenate([bias] * 4, axis=1), (8, 512)).astype(BF16)
    c_ref[384:392, :] = jnp.broadcast_to(vecs[8:9, :], (8, 512)).astype(BF16)
    for i, bias in enumerate((bq, jnp.zeros_like(bq), bv)):
        qb_ref[256:264, 128 * i : 128 * i + 128] = jnp.broadcast_to(bias, (8, 128)).astype(BF16)
    for copy in copies[len(moves) - len(late) :]:
        copy.wait()


def half_rows_kernel(tb, keep, recv, out_ref):
    out_ref[...] = (keep[384:, :] + recv[384:, :].astype(F32)).astype(BF16)


def half_columns_kernel(tb, keep, recv, out_ref):
    half = keep.shape[1]
    out_ref[...] = (keep[...] + recv[:, half:].astype(F32)).astype(BF16)


def padded(rows, n_dp):
    unit = 8 * n_dp
    return -(-rows // unit) * unit


def bit_of(pos, b):
    return (pos[4] >> b) & 1


def sum_into(dst, at, addends, rows):
    value = None
    for ref, start in addends:
        block = ref[start : start + rows, :].astype(F32)
        value = block if value is None else value + block
    dst[at : at + rows, :] = value


def cut_rows(total, at, rows, bit, own, own_at, send, send_at):
    half = rows // 2
    mine = pl.multiple_of(at + bit * half, 8)
    other = pl.multiple_of(at + (1 - bit) * half, 8)
    own[own_at : own_at + half, :] = total[pl.ds(mine, half), :]
    send[send_at : send_at + half, :] = total[pl.ds(other, half), :].astype(BF16)


def pick(refs, groups):
    it = iter(refs)
    return [(rows, [(next(it), start) for start in starts]) for rows, starts in groups]


def halves_kernel(pos, *refs, parts, rows, bits):
    count = sum(len(starts) for groups in parts for _, starts in groups)
    ins, (own1, send1, own2, send2, total) = refs[:count], refs[count:]
    used = 0
    for groups, bit, own, send in zip(parts, bits, (own1, own2), (send1, send2)):
        need = sum(len(starts) for _, starts in groups)
        at = 0
        for size, addends in pick(ins[used : used + need], groups):
            sum_into(total, at, addends, size)
            at += size
        used += need
        if at < rows:
            total[at:, :] = jnp.zeros((rows - at, 512), F32)
        cut_rows(total, 0, rows, bit_of(pos, bit), own, 0, send, 0)


def merge_kernel(pos, own1, recv1, own2, recv2, own, send, total, *, bit):
    rows = own1.shape[0]
    for i, (o, r) in enumerate(((own1, recv1), (own2, recv2))):
        total[...] = o[...] + r[...].astype(F32)
        cut_rows(total, 0, rows, bit_of(pos, bit), own, i * rows // 2, send, i * rows // 2)


def round_kernel(pos, *refs, count, small):
    out = refs[-1]
    at = 0
    for i in range(0, count, 2):
        rows = refs[i].shape[0]
        out[at : at + rows, :] = (refs[i][...] + refs[i + 1][...].astype(F32)).astype(BF16)
        at += rows
    out[at : at + 8, :] = jnp.zeros((8, 512), BF16)
    used = count
    for first, size, starts in small:
        value = None
        for ref, start in zip(refs[used : used + len(starts)], starts):
            block = ref[start : start + size, :].astype(F32)
            value = block if value is None else value + block
        out[at + first : at + first + size, :] = value.astype(BF16)
        used += len(starts)


def both_kernel(pos, own0, recv0, own, send, total, *, bit):
    rows = own0.shape[0] // 2
    total[...] = own0[...] + recv0[...].astype(F32)
    for i in range(2):
        cut_rows(total, i * rows, rows, bit_of(pos, bit), own, i * rows // 2, send, i * rows // 2)


def settle_kernel(pos, own, recv, out):
    out[...] = (own[...].astype(F32) + recv[...].astype(F32)).astype(BF16)


def stack_kernel(pos, held, recv, out):
    size = held.shape[0]
    out[0:size] = held[...]
    out[size:] = recv[...]


def part_rows(value, at, rows, out1, out2):
    out1[at, 0:rows, :] = value[0:rows]
    out1[at, rows : rows + 8, :] = value[2 * rows :]
    out2[at] = value[rows : 2 * rows]


def settle_part_kernel(pos, own, recv, out1, out2):
    rows = (own.shape[0] - 8) // 2
    value = (own[...].astype(F32) + recv[...].astype(F32)).astype(BF16)
    part_rows(value, 0, rows, out1, out2)


def part_kernel(pos, held, recv, out1, out2):
    size, rows = held.shape[0], (held.shape[1] - 8) // 2
    for i, r in enumerate((held, recv)):
        for j in range(size):
            part_rows(r[j], i * size + j, rows, out1, out2)


def pair_kernel(pos, held1, recv1, held2, recv2, out1, out2):
    for out, h, r in ((out1, held1, recv1), (out2, held2, recv2)):
        size = h.shape[0]
        out[0:size] = h[...]
        out[size:] = r[...]


def unpack_kernel(pos, held1, recv1, held2, recv2, *refs, plans, orders, small):
    outs, scratch, sums = refs[:-2], refs[-2], refs[-1]
    rows = held2.shape[1]
    used = 0
    for plan, order, blocks in zip(plans, orders, ((held1, recv1), (held2, recv2))):
        place = 0
        for b in order:
            place = place * 2 + bit_of(pos, b)
        each = blocks[0].shape[0]
        for i in range(2 * each):
            at = pl.multiple_of((place ^ i) * rows, 8)
            scratch[pl.ds(at, rows), :] = blocks[i // each][i % each, 0:rows, :].astype(F32)
        for start, size, flip in plan:
            block = scratch[start : start + size, :]
            outs[used][...] = block.T if flip else block
            used += 1
    total = jnp.zeros((8, 512), F32)
    for r in (held1, recv1):
        total = total + jnp.sum(r[:, rows:, :].astype(F32), axis=0)
    sums[...] = total
    for i, (row, start, size) in enumerate(small):
        outs[used + i][...] = sums[row : row + 1, start : start + size].reshape(size)


def body(
    layer_input, segments, norm1_gain, norm1_bias, w_query, b_query, w_key, w_value, b_value,
    w_out, b_out, gate1_w, gate1_b, norm2_gain, norm2_bias, w_in, b_in, w_back, b_back,
    gate2_w, gate2_b, cotangent, *, n_dp,
):
    def hop(value, mask):
        return lax.ppermute(value, "tensor", [(i, i ^ mask) for i in range(4)])

    def dhop(value, mask):
        return lax.ppermute(value, "dp", [(i, i ^ mask) for i in range(n_dp)])

    def after(value, *deps):
        return lax.optimization_barrier((value,) + deps)[0]

    t = lax.axis_index("tensor").astype(jnp.int32)
    me = lax.axis_index("dp").astype(jnp.int32)
    tb = jnp.where(jnp.arange(8) < 4, t ^ jnp.array(LOCAL + (0,) * 4, jnp.int32), me)
    seg = segments
    x0 = layer_input
    last = [None]

    def step(kernel, outs, args, name, scratch=(), smem=1, space=VM, then=(), limit=None, cost=HEAVY):
        pos = tb if last[0] is None else after(tb, last[0], *then)
        got = call(kernel, outs, [pos] + args, smem=smem, scratch=scratch, name=name, space=space, limit=limit, cost=LIGHT if name in EASY else cost)
        last[0] = got[0]
        return got

    x1 = hop(x0, PX)
    x2 = hop(x0, 1)
    hbm = dict(space=pl.BlockSpec(memory_space=pltpu.MemorySpace.HBM), cost=LIGHT)
    s0, e0, c0, qa0, qb0, vecs = step(
        pack_kernel,
        [sds((296, 512), BF16), sds((256, 512), BF16), sds((1416, 512), BF16), sds((256, 384), BF16),
         sds((264, 384), BF16), sds((16, 512), F32)],
        [pltpu.with_memory_space_constraint(w, pltpu.MemorySpace.HBM) for w in
         (w_in, w_back, w_out, gate1_w, gate2_w, w_query, w_key, w_value, norm1_gain, norm1_bias, b_out, gate1_b,
          norm2_gain, norm2_bias, b_back, gate2_b, b_in, b_query, b_value)],
        "pack",
        [pltpu.SemaphoreType.DMA((27,)), pltpu.VMEM((512, 128), BF16)]
        + [pltpu.VMEM((512,), BF16)] * 9 + [pltpu.VMEM((128,), BF16)] * 2, **hbm,
    )
    qkv = [qa0, qb0, hop(qa0, 1), hop(qb0, 1)]
    sy = hop(s0, PX)
    c2 = hop(c0, 1)
    na, qt0, ka, vta = step(
        chip_kernel,
        [sds((512, 512), BF16), sds((256, 256), BF16), sds((512, 256), BF16), sds((256, 512), BF16)],
        [x0, x2, vecs] + qkv, "chip", cost=LIGHT,
    )
    x3 = hop(after(x1, na), 1)
    e1 = hop(after(e0, x3), PX)
    n, qt1, k, vt, p1, ot1, att1, invl1 = step(
        first_kernel,
        [
            sds((1024, 512), BF16), sds((256, 256), BF16), sds((1024, 256), BF16),
            sds((256, 1024), BF16), sds((4, 1024, 256), BF16), sds((256, 256), BF16), sds((256, 256), BF16),
            sds((4, 8, 256), F32),
        ],
        [seg, seg, x1, x3, vecs] + qkv + [na, ka, vta],
        "first", ATT_SCRATCH, 2,
    )
    attp = hop(att1, PX)
    sy = after(sy, att1)
    sx = dhop(sy, 1)
    sz = dhop(sy, 2)
    p0, ot0, att0, invl0 = step(
        second_kernel,
        [sds((4, 1024, 256), BF16), sds((256, 256), BF16), sds((256, 256), BF16), sds((4, 8, 256), F32)],
        [seg, seg, qt0, k, vt],
        "second", ATT_SCRATCH, 2,
    )
    e3 = hop(after(e1, att0), 1)
    v, kt = step(prepare_kernel, [sds((1024, 256), BF16), sds((256, 1024), BF16)], [n, k] + qkv, "prepare")
    cut_a, cut_b = step(cut_kernel, [sds((128, 512), BF16), sds((168, 512), BF16)], [sx, sz], "cut")
    sxz_a, sxz_b = dhop(cut_a, 1), dhop(cut_b, 2)
    n2, mid, branch, gate = step(
        out_kernel,
        [sds((256, 512), BF16), sds((256, 512), F32), sds((256, 512), F32), sds((256, 512), F32)],
        [x0, n, att0, attp, vecs, e0, e1, c2, e3],
        "out", [pltpu.VMEM((512, 512), BF16)],
    )
    n2p = hop(n2, PX)
    quarters = [sy, hop(sy, 1), sx, hop(sx, 1), sz, hop(sz, 1)]
    total0, hid, slope0, slope1 = step(
        ffn_first_kernel,
        [sds((256, 512), F32), sds((256, 1024), BF16), sds((256, 1024), BF16), sds((256, 768), BF16)],
        [n2, vecs, w_in, w_back, c2] + quarters,
        "ffn_first", cost=LIGHT,
    )
    sxz_a, sxz_b = lax.optimization_barrier((sxz_a, sxz_b, total0))[0:2]
    quarters = quarters + [sxz_a, hop(sxz_a, 1), sxz_b, hop(sxz_b, 1)]
    result, fg, ltg, slope2 = step(
        ffn_kernel,
        [sds((256, 512), BF16), sds((256, 512), BF16), sds((256, 512), BF16), sds((256, 256), BF16)],
        [n2, mid, cotangent, vecs, gate2_w, c2, total0] + quarters,
        "ffn", [pltpu.VMEM((512, 512), BF16)],
    )
    fgp = hop(fg, PX)
    dot0, dotp, mg, bg, log, hg, sums = step(
        back_kernel,
        [
            sds((256, 256), BF16), sds((256, 256), BF16), sds((256, 512), F32), sds((256, 512), BF16),
            sds((256, 512), BF16), sds((256, 1024), BF16), sds((8, 512), F32),
        ],
        [fg, ltg, slope0, slope1, slope2, mid, branch, gate, cotangent, vecs, e0, e1, c2, e3, gate2_w, w_in, w_back]
        + quarters,
        "back", [pltpu.VMEM((512, 512), BF16)],
    )
    dot1 = hop(dotp, PX)
    skeep, ssend = step(
        small_weight_kernel,
        [sds((776, 512), F32), sds((776, 512), BF16)],
        [n, n2, ltg, log, att0, attp, bg, sums],
        "small_weight", [pltpu.VMEM((512, 512), F32), pltpu.VMEM((512, 512), F32)],
    )
    srecv = hop(ssend, 1)
    back_scratch = [
        pltpu.VMEM((256, 256), F32), pltpu.VMEM((4, 128, 256), BF16), pltpu.VMEM((256, 256), BF16),
        pltpu.VMEM((4, 8, 256), F32),
    ]
    dk0, dv0, dq0 = step(
        back_first_kernel,
        [sds((256, 1024), F32), sds((256, 1024), F32), sds((256, 256), BF16)],
        [seg, p0, dot0, ot0, invl0, qt0, kt, v],
        "attn_back0", back_scratch, 2,
    )
    (spar,) = step(half_rows_kernel, [sds((392, 512), BF16)], [skeep, srecv], "half_rows")
    sparr = hop(spar, PX)
    bkeep, bsend, slopep = step(
        ffn_back_weight_kernel,
        [sds((512, 512), F32), sds((512, 512), BF16), sds((256, 1024), BF16)],
        [n2p, fg, fgp, hid, vecs, w_in, c2],
        "ffn_back_weight",
    )
    brecv = hop(bsend, 1)
    ikeep, isend = step(
        ffn_in_weight_kernel,
        [sds((520, 512), F32), sds((520, 512), BF16)],
        [n2, n2p, fgp, hg, slopep, w_back, c2],
        "ffn_in_weight",
    )
    irecv = hop(isend, 1)
    bits = n_dp.bit_length() - 1

    def halves(tag, parts1, parts2, rows):
        arrays = [a for parts in (parts1, parts2) for _, group in parts for a, _ in group]
        static = tuple(
            tuple((m, tuple(start for _, start in group)) for m, group in parts) for parts in (parts1, parts2)
        )
        shapes = [sds((rows // 2, 512), F32), sds((rows // 2, 512), BF16)] * 2
        o1, s1, o2, s2 = step(
            functools.partial(halves_kernel, parts=static, rows=rows, bits=(0, 1)),
            shapes, arrays, "halves_" + tag, [pltpu.VMEM((rows, 512), F32)],
        )
        return o1, dhop(s1, 1), o2, dhop(s2, 2)

    def quarter_step(tag, o1, r1, o2, r2):
        rows = o1.shape[0]
        shapes = [sds((rows // 2, 512), F32), sds((rows // 2, 512), BF16)] * 2
        o1, s1, o2, s2 = step(
            functools.partial(halves_kernel, parts=(((rows, (0, 0)),),) * 2, rows=rows, bits=(1, 0)),
            shapes, [o1, r1, o2, r2], "quarters_" + tag, [pltpu.VMEM((rows, 512), F32)],
        )
        return o1, dhop(s1, 2), o2, dhop(s2, 1)

    def merge_step(tag, o1, r1, o2, r2, small):
        rows = o1.shape[0]
        pairs = [o1, r1, o2, r2]
        for b in range(2, bits - 1):
            kernel = merge_kernel if b == 2 else both_kernel
            own, sent = step(
                functools.partial(kernel, bit=b), [sds((rows, 512), F32), sds((rows, 512), BF16)],
                pairs, "cut_" + tag, [pltpu.VMEM((rows if b == 2 else 2 * rows, 512), F32)],
            )
            pairs, rows = [own, dhop(sent, 1 << b)], rows // 2
        static = tuple((f, m, tuple(start for _, start in group)) for f, m, group in small)
        arrays = [a for _, _, group in small for a, _ in group]
        own = step(
            functools.partial(round_kernel, count=len(pairs), small=static), [sds((2 * rows + 8, 512), BF16)],
            pairs + arrays, "merge_" + tag,
        )[0]
        return own, dhop(own, 1 << (bits - 1))

    def part_step(tag, own, recv):
        rows = (own.shape[0] - 8) // 2
        if bits > 3:
            held = step(settle_kernel, [sds(own.shape, BF16)], [own, recv], "settle")[0][None]
            for b in range(bits - 2, 2, -1):
                shape = (2 * held.shape[0],) + held.shape[1:]
                held = step(stack_kernel, [sds(shape, BF16)], [held, dhop(held, 1 << b)], "stack")[0]
            size = 2 * held.shape[0]
            kernel, args = part_kernel, [held, dhop(held, 4)]
        else:
            size, kernel, args = 1, settle_part_kernel, [own, recv]
        h1, h2 = step(kernel, [sds((size, rows + 8, 512), BF16), sds((size, rows, 512), BF16)], args, "part_" + tag)
        return h1, dhop(h1, 2), h2, dhop(h2, 1)

    def pair_step(tag, h1, r1, h2, r2):
        shapes = [sds((2 * h.shape[0],) + h.shape[1:], BF16) for h in (h1, h2)]
        h1, h2 = step(pair_kernel, shapes, [h1, r1, h2, r2], "pair_" + tag)
        return h1, dhop(h1, 1), h2, dhop(h2, 2)

    def unpack_step(tag, h1, r1, h2, r2, plans, small):
        shapes = [sds((512, size) if flip else (size, 512), F32) for plan in plans for _, size, flip in plan]
        rest = tuple(range(2, bits - 1))
        rows = 2 * h2.shape[0] * h2.shape[1]
        return step(
            functools.partial(unpack_kernel, plans=plans, orders=((0, 1) + rest, (1, 0) + rest), small=small),
            shapes + [sds((size,), F32) for _, _, size in small], [h1, r1, h2, r2], "unpack_" + tag,
            [pltpu.VMEM((rows, 512), F32), pltpu.VMEM((8, 512), F32)],
        )

    f = halves("f", [(512, [(bkeep, 0), (brecv, 0)])], [(512, [(ikeep, 0), (irecv, 0)])], padded(512, n_dp))

    dqt, dkt, dvt, akeep, asend = step(
        back_second_kernel,
        [
            sds((256, 512), BF16), sds((256, 1024), BF16), sds((256, 1024), BF16), sds((392, 512), F32),
            sds((392, 512), BF16),
        ],
        [seg, p1, dot1, ot1, invl1, qt1, kt, v, dk0, dv0, dq0, n],
        "attn_back1", [pltpu.VMEM((256, 1024), F32), pltpu.VMEM((256, 1024), F32)] + back_scratch, 2,
    )
    arecv = hop(asend, 1)
    gown, gpar, gsend = step(
        input_kernel,
        [sds((512, 256), F32), sds((512, 256), F32), sds((512, 512), BF16)],
        [dqt, dkt, dvt] + qkv,
        "input_grad",
    )
    gsib = hop(gsend, 1)
    f = quarter_step("f", *f)
    a = halves(
        "a", [(384, [(akeep, 0), (arecv, 0)])], [(384, [(skeep, 0), (srecv, 0), (sparr, 0)])], padded(384, n_dp)
    )
    (gsum,) = step(half_columns_kernel, [sds((512, 256), BF16)], [gpar, gsib], "half_columns")
    gp = hop(gsum, PX)
    tail = [(skeep, 773), (srecv, 773), (sparr, 389)]
    f = merge_step("f", *f, [(0, 1, [(ikeep, 512), (irecv, 512)]), (1, 1, tail)])
    a = quarter_step("a", *a)
    input_grad, sums1 = step(
        last_kernel,
        [sds((256, 512), F32), sds((8, 512), F32)],
        [gown, gsib, gp, x0, mg, log, vecs, e0, e1, c2, e3],
        "last", [pltpu.VMEM((512, 512), BF16)],
    )
    sums1_b = hop(sums1, PX)
    sums1_a = hop(sums1, 1)
    sums1_c = hop(sums1, PX ^ 1)
    f = part_step("f", *f)
    group = [(skeep, 768), (srecv, 768), (sparr, 384)]
    a = merge_step(
        "a", *a,
        [(0, 2, [(sums1, 0), (sums1_a, 0), (sums1_b, 0), (sums1_c, 0)]), (2, 1, [(akeep, 384), (arecv, 384)]),
         (3, 5, group)],
    )
    f = pair_step("f", *f)
    a = part_step("a", *a)
    a = pair_step("a", *a)
    g_wback, g_win, d_b_in, d_n2b = unpack_step(
        "f", *f, (((0, 512, False),), ((0, 512, False),)), ((0, 0, 512), (1, 0, 512))
    )
    plans = (
        ((0, 128, True), (128, 128, True), (256, 128, True)),
        ((0, 128, False), (128, 128, False), (256, 128, False)),
    )
    small = ((0, 0, 512), (1, 0, 512), (2, 0, 128), (2, 128, 128)) + tuple((i, 0, 512) for i in range(3, 8))
    g_q, g_k, g_v, g_g2, g_g1, g_wo, d_n1g, d_n1b, d_bq, d_bv, d_b_back, d_g2b, d_b_out, d_g1b, d_n2g = unpack_step(
        "a", *a, plans, small
    )
    return (
        result, input_grad, d_n1g, d_n1b, g_q, d_bq, g_k, g_v, d_bv, g_wo, d_b_out, g_g1, d_g1b, d_n2g, d_n2b,
        g_win, d_b_in, g_wback, d_b_back, g_g2, d_g2b,
    )


def solution(mesh):
    tok = P(("dp", "tensor"), None)
    col = P(None, "tensor")
    row = P("tensor", None)
    vec = P("tensor")
    rep = P()
    return jax.shard_map(
        functools.partial(body, n_dp=mesh.shape["dp"]),
        mesh=mesh,
        in_specs=(
            tok, P("dp", None), rep, rep, col, vec, col, col, vec, row, rep, row, rep, rep, rep,
            col, vec, row, rep, row, rep, tok,
        ),
        out_specs=(
            tok, tok, rep, rep, col, vec, col, col, vec, row, rep, row, rep, rep, rep,
            col, vec, row, rep, row, rep,
        ),
        check_vma=False,
    )
```

```python
import functools
import math

import jax
import jax.numpy as jnp
from jax import lax
from jax.experimental import pallas as pl
from jax.experimental.pallas import tpu as pltpu
from jax.sharding import PartitionSpec as P

HD = 64
EPSILON = 1e-05
F32 = jnp.float32
BF16 = jnp.bfloat16
NEG = -1e30
PX = 2
LOCAL = (0, PX, 1, 1 ^ PX)
SPARE = 4 * 1024 * 1024
HEAVY = 10**10
LIGHT = 0
COSTS = {"halves_f": 0, "halves_a": 0, "input_grad": 0, "pair_a": 2*10**10, "part_f": 0, "merge_a": 0, "last": 0, "pair_f": 0, "part_a": 0,"unpack_f":0, "first": 0, "ffn": 0}


def nn(a, b):
    return lax.dot_general(a, b, (((1,), (0,)), ((), ())), preferred_element_type=F32)


def nt(a, b):
    return lax.dot_general(a, b, (((1,), (1,)), ((), ())), preferred_element_type=F32)


def tn(a, b):
    return lax.dot_general(a, b, (((0,), (0,)), ((), ())), preferred_element_type=F32)


VM = pl.BlockSpec(memory_space=pltpu.VMEM)
SM = pl.BlockSpec(memory_space=pltpu.SMEM)


def call(body, outs, args, smem=0, scratch=(), name=None, space=VM, limit=None, cost=0):
    nbytes = sum(a.size * a.dtype.itemsize for a in args) + sum(o.size * o.dtype.itemsize for o in outs)
    held = sum(math.prod(s.shape) * 4 for s in scratch)
    limit = limit or nbytes + held + SPARE
    return pl.pallas_call(
        body,
        out_shape=tuple(outs),
        in_specs=[SM] * smem + [space] * (len(args) - smem),
        out_specs=tuple([VM] * len(outs)),
        scratch_shapes=list(scratch),
        compiler_params=pltpu.CompilerParams(vmem_limit_bytes=limit),
        cost_estimate=pl.CostEstimate(flops=cost, bytes_accessed=0, transcendentals=0),
        name=name,
    )(*args)


def sds(shape, dtype):
    return jax.ShapeDtypeStruct(shape, dtype)


def norm_unit(values):
    centred = values - jnp.mean(values, axis=-1, keepdims=True)
    spread = jnp.mean(centred * centred, axis=-1, keepdims=True)
    inverse = lax.rsqrt(spread + EPSILON)
    return centred * inverse, inverse


def sigmoid(v):
    return 1.0 / (1.0 + jnp.exp(-v))


C0 = 0.7978845608028654
C1 = 0.044715


def gelu_parts(u):
    square = u * u
    t = jnp.tanh(C0 * u * (1.0 + C1 * square))
    half = 0.5 * (1.0 + t)
    value = u * half
    slope = half + (0.5 * C0) * u * (1.0 - t * t) * (1.0 + (3.0 * C1) * square)
    return value, slope


def attend_query_block(qb, tb, segs, segv, qz, k, vt, p_ref, ot_ref, invl_ref, s_sc, m_sc, l_sc, o_sc, segc):
    rows = 256
    tq = tb[qb]
    m_sc[...] = jnp.full(m_sc.shape, NEG, F32)
    l_sc[...] = jnp.zeros(l_sc.shape, F32)
    o_sc[...] = jnp.zeros(o_sc.shape, F32)
    seg_q = segv[0:1, pl.ds(pl.multiple_of(tq * rows, rows), rows)].astype(F32)

    def active(kb):
        tk = tb[kb]
        return (tk <= tq) & (segs[0, tk * rows + rows - 1] >= segs[0, tq * rows])

    @pl.loop(0, 4)
    def _(kb):
        @pl.when(active(kb))
        def _():
            tk = tb[kb]
            krows = pl.ds(pl.multiple_of(kb * rows, rows), rows)
            kpos = tk * rows + lax.broadcasted_iota(jnp.int32, (rows, rows), 0)
            qpos = tq * rows + lax.broadcasted_iota(jnp.int32, (rows, rows), 1)
            seg_k = segc[pl.ds(pl.multiple_of(tk * rows, rows), rows), 0:1]
            bias = jnp.where((kpos <= qpos) & (seg_k == seg_q), 0.0, NEG)
            for h in range(4):
                pair = 128 * (h // 2)
                s = nn(k[krows, pair : pair + 128], qz[h]) + bias
                s_sc[h, krows, :] = s
                m_sc[h] = jnp.maximum(m_sc[h], jnp.max(s.reshape(rows // 8, 8, rows), axis=0))

    for h in range(4):
        m_sc[h] = jnp.broadcast_to(jnp.max(m_sc[h], axis=0, keepdims=True), (8, rows))

    @pl.loop(0, 4)
    def _(kb):
        @pl.when(active(kb))
        def _():
            krows = pl.ds(pl.multiple_of(kb * rows, rows), rows)
            for h in range(4):
                e = jnp.exp(s_sc[h, krows, :] - m_sc[h, 0:1, :])
                l_sc[h] = l_sc[h] + jnp.sum(e.reshape(rows // 8, 8, rows), axis=0)
                pb = e.astype(BF16)
                p_ref[h, krows, :] = pb
                o_sc[h] = o_sc[h] + nn(vt[64 * h : 64 * h + 64, krows], pb)

    for h in range(4):
        invl = 1.0 / jnp.sum(l_sc[h], axis=0, keepdims=True)
        invl_ref[h] = jnp.broadcast_to(invl, (8, rows))
        ot_ref[64 * h : 64 * h + 64, :] = (o_sc[h] * invl).astype(BF16)


def fill_qz(qz, qt):
    zero = jnp.zeros((64, 256), BF16)
    for h in range(4):
        mine = qt[64 * h : 64 * h + 64, :]
        qz[h] = jnp.concatenate([mine, zero] if h % 2 == 0 else [zero, mine], axis=0)


def fill_segc(segc, segv):
    for t in range(4):
        row = jnp.broadcast_to(segv[0:1, 256 * t : 256 * t + 256].astype(F32), (128, 256))
        segc[256 * t : 256 * t + 256, :] = row.T


def weight_of(w, part):
    cols = slice(128 * part, 128 * part + 128)
    return jnp.concatenate([w[0][:, cols], w[1][0:256, cols]], axis=0)


def bias_of(w, part):
    return w[1][256:257, 128 * part : 128 * part + 128].astype(F32)


def project(n, w, c, k_ref, vt_ref, blocks):
    cols = slice(128 * c, 128 * c + 128)
    k = nn(n, weight_of(w, 1)).astype(BF16)
    vt = (nn(n, weight_of(w, 2)) + bias_of(w, 2)).T.astype(BF16)
    for i, at in enumerate(blocks):
        k_ref[at : at + 256, cols] = k[256 * i : 256 * i + 256]
        vt_ref[cols, at : at + 256] = vt[:, 256 * i : 256 * i + 256]


def query_of(n, w):
    q = nn(n, weight_of(w, 0)) + bias_of(w, 0)
    return (q.astype(BF16).astype(F32) * HD ** (-0.5)).T.astype(BF16)


def chip_kernel(pos, x0, x2, vecs, qa0, qb0, qa1, qb1, n_ref, qt_ref, k_ref, vt_ref):
    for i, x in enumerate((x0, x2)):
        unit, _ = norm_unit(x[...].astype(F32))
        n_ref[256 * i : 256 * i + 256, :] = (unit * vecs[0:1, :] + vecs[1:2, :]).astype(BF16)
    n = n_ref[...]
    for c, w in enumerate(((qa0, qb0), (qa1, qb1))):
        qt_ref[128 * c : 128 * c + 128, :] = query_of(n[0:256], w)
        project(n, w, c, k_ref, vt_ref, (0, 256))


def first_kernel(
    tb, segs, segv, x1, x3, vecs, qa0, qb0, qa1, qb1, na, ka, vta,
    n_ref, qt1_ref, k_ref, vt_ref, p_ref, ot_ref, att_ref, invl_ref,
    qz, s_sc, m_sc, l_sc, o_sc, segc,
):
    for i, x in enumerate((x1, x3)):
        unit, _ = norm_unit(x[...].astype(F32))
        n_ref[512 * i + 256 : 512 * i + 512, :] = (unit * vecs[0:1, :] + vecs[1:2, :]).astype(BF16)
    n = jnp.concatenate([n_ref[256:512, :], n_ref[768:1024, :]], axis=0)
    for c, w in enumerate(((qa0, qb0), (qa1, qb1))):
        qt1_ref[128 * c : 128 * c + 128, :] = query_of(n[0:256], w)
        project(n, w, c, k_ref, vt_ref, (256, 768))
    for i in range(2):
        src, dst = slice(256 * i, 256 * i + 256), slice(512 * i, 512 * i + 256)
        n_ref[dst, :] = na[src, :]
        k_ref[dst, :] = ka[src, :]
        vt_ref[:, dst] = vta[:, src]
    fill_segc(segc, segv)
    fill_qz(qz, qt1_ref)
    attend_query_block(1, tb, segs, segv, qz, k_ref, vt_ref, p_ref, ot_ref, invl_ref, s_sc, m_sc, l_sc, o_sc, segc)
    att_ref[...] = ot_ref[...].astype(F32).T.astype(BF16)


def second_kernel(
    tb, segs, segv, qt0, k, vt,
    p_ref, ot_ref, att_ref, invl_ref,
    qz, s_sc, m_sc, l_sc, o_sc, segc,
):
    fill_segc(segc, segv)
    fill_qz(qz, qt0)
    attend_query_block(0, tb, segs, segv, qz, k, vt, p_ref, ot_ref, invl_ref, s_sc, m_sc, l_sc, o_sc, segc)
    att_ref[...] = ot_ref[...].astype(F32).T.astype(BF16)


ATT_SCRATCH = (
    pltpu.VMEM((4, 128, 256), BF16),
    pltpu.VMEM((4, 1024, 256), F32),
    pltpu.VMEM((4, 8, 256), F32),
    pltpu.VMEM((4, 8, 256), F32),
    pltpu.VMEM((4, 64, 256), F32),
    pltpu.VMEM((1024, 128), F32),
)


def gather_gate(tb, pieces, start, scratch):
    for i, piece in enumerate(pieces):
        scratch[pl.ds(pl.multiple_of(tb[i] * 128, 128), 128), :] = piece[start : start + 128, :]


def gather_gate_two(pos, g2, c2, pieces, scratch):
    scratch[pl.ds(pl.multiple_of(pos[0] * 128, 128), 128), :] = g2[...]
    scratch[pl.ds(pl.multiple_of(pos[2] * 128, 128), 128), :] = c2[256:384, :]
    for i, piece in enumerate(pieces):
        quarter = (pos[4] ^ (i // 2)) & 3
        at = pos[1 + 2 * (i % 2)] * 128 + quarter * 32
        rows = piece.shape[0]
        scratch[pl.ds(pl.multiple_of(at, 32), 32), :] = piece[rows - 32 : rows, :]


def out_kernel(
    tb, x0, n, att, attp, vecs, e0, e1, e2, e3,
    n2_ref, mid_ref, branch_ref, gate_ref,
    gw,
):
    gather_gate(tb, (e0, e1, e2, e3), 128, gw)
    branch = nn(att[:, 0:128], e0[0:128, :]) + nn(att[:, 128:256], e2[0:128, :])
    branch = branch + nn(attp[:, 0:128], e1[0:128, :]) + nn(attp[:, 128:256], e3[0:128, :])
    branch = branch + vecs[2:3, :]
    gate = sigmoid(nn(n[0:256, :], gw[...]) + vecs[3:4, :])
    middle = x0[...].astype(F32) + gate * branch
    unit, _ = norm_unit(middle)
    n2_ref[...] = (unit * vecs[4:5, :] + vecs[5:6, :]).astype(BF16)
    mid_ref[...] = middle
    branch_ref[...] = branch
    gate_ref[...] = gate


def pair_up(a, b, start):
    return jnp.concatenate([a[start : start + 128, :], b[start : start + 128, :]], axis=0)


def pair_bias(a, b, row=256):
    return jnp.concatenate([a[row : row + 1, 0:128], b[row : row + 1, 0:128]], axis=1).astype(F32)


def cut_kernel(pos, sx, sz, a_ref, b_ref):
    a_ref[...] = sz[0:128, :]
    b_ref[...] = sx[128:296, :]


def ffn_first_kernel(
    tb, n2, vecs, win0, wback0, c2, s0, s1, s2, s3, s4, s5,
    total_ref, hid_ref, slope_ref, slope1_ref,
):
    n2v = n2[...]
    total = jnp.zeros((256, 512), F32)
    for i, (b, w, wb) in enumerate(((vecs[8:9, :], win0[...], wback0[...]), (c2[384:385, :], c2[392:904, :], c2[904:1416, :]))):
        value, slope = gelu_parts(nn(n2v, w) + b.astype(F32))
        value = value.astype(BF16)
        hid_ref[:, 512 * i : 512 * i + 512] = value
        slope_ref[:, 512 * i : 512 * i + 512] = slope.astype(BF16)
        total = total + nn(value, wb)
    for i, (a, b) in enumerate(((s0, s1), (s2, s3), (s4, s5))):
        value, slope = gelu_parts(nt(n2v, pair_up(a, b, 0)) + pair_bias(a, b))
        slope1_ref[:, 256 * i : 256 * i + 256] = slope.astype(BF16)
        total = total + nn(value.astype(BF16), pair_up(a, b, 128))
    total_ref[...] = total


def ffn_kernel(
    tb, n2, mid, ct, vecs, g2, c2, total0, s0, s1, s2, s3, s4, s5, a6, a7, b6, b7,
    out_ref, fg_ref, ltg_ref, slope_ref, gw,
):
    gather_gate_two(tb, g2, c2, (s0, s1, s2, s3, s4, s5, b6, b7), gw)
    n2v = n2[...]
    value, slope = gelu_parts(nt(n2v, pair_up(a6, a7, 0)) + pair_bias(b6, b7, 128))
    slope_ref[...] = slope.astype(BF16)
    ffn = total0[...] + nn(value.astype(BF16), pair_up(b6, b7, 0)) + vecs[6:7, :]
    gate = sigmoid(nn(n2v, gw[...]) + vecs[7:8, :])
    up = ct[...].astype(F32)
    out_ref[...] = (mid[...] + gate * ffn).astype(BF16)
    fg_ref[...] = (gate * up).astype(BF16)
    ltg_ref[...] = (up * ffn * (gate * (1.0 - gate))).astype(BF16)


def back_kernel(
    tb, fg, ltg, slope0, slope1, slope2, mid, branch, gate, ct, vecs, e0, e1, e2, e3, g2,
    win0, wback0, s0, s1, s2, s3, s4, s5, a6, a7, b6, b7,
    dot_ref, dotp_ref, mg_ref, bg_ref, log_ref, hg_ref, sums_ref,
    gw,
):
    gather_gate_two(tb, g2, e2, (s0, s1, s2, s3, s4, s5, b6, b7), gw)
    fgv = fg[...]
    ltgv = ltg[...]
    ng = nt(ltgv, gw[...])
    for i, (w, wb) in enumerate(((win0[...], wback0[...]), (e2[392:904, :], e2[904:1416, :]))):
        hg = (nt(fgv, wb) * slope0[:, 512 * i : 512 * i + 512].astype(F32)).astype(BF16)
        hg_ref[:, 512 * i : 512 * i + 512] = hg
        ng = ng + nt(hg, w)
    for i, (a, b) in enumerate(((s0, s1), (s2, s3), (s4, s5))):
        part = slope1[:, 256 * i : 256 * i + 256]
        hg = (nt(fgv, pair_up(a, b, 128)) * part.astype(F32)).astype(BF16)
        ng = ng + nn(hg, pair_up(a, b, 0))
    hg = (nt(fgv, pair_up(b6, b7, 0)) * slope2[...].astype(F32)).astype(BF16)
    ng = ng + nn(hg, pair_up(a6, a7, 0))
    unit, inverse = norm_unit(mid[...])
    g = ng * vecs[4:5, :]
    back = inverse * (g - jnp.mean(g, axis=-1, keepdims=True) - unit * jnp.mean(g * unit, axis=-1, keepdims=True))
    mg = ct[...].astype(F32) + back
    mg_ref[...] = mg
    gatev = gate[...]
    bg = (gatev * mg).astype(BF16)
    log = (mg * branch[...] * (gatev * (1.0 - gatev))).astype(BF16)
    bg_ref[...] = bg
    log_ref[...] = log
    dot_ref[0:128, :] = nt(e0[0:128, :], bg).astype(BF16)
    dot_ref[128:256, :] = nt(e2[0:128, :], bg).astype(BF16)
    dotp_ref[0:128, :] = nt(e1[0:128, :], bg).astype(BF16)
    dotp_ref[128:256, :] = nt(e3[0:128, :], bg).astype(BF16)
    rows = [fgv.astype(F32), ltgv.astype(F32), bg.astype(F32), log.astype(F32), ng * unit, ng]
    sums_ref[...] = jnp.zeros((8, 512), F32)
    for i, r in enumerate(rows):
        sums_ref[i : i + 1, :] = jnp.sum(r, axis=0, keepdims=True)


def ffn_back_weight_kernel(
    tb, n2p, fg, fgp, hid, vecs, win0, c2,
    keep_ref, send_ref, slope_ref,
):
    fgv, fgpv, n2pv = fg[...], fgp[...], n2p[...]
    for i, (b, w) in enumerate(((vecs[8:9, :], win0[...]), (c2[384:385, :], c2[392:904, :]))):
        cols = slice(512 * i, 512 * i + 512)
        value, slope = gelu_parts(nn(n2pv, w) + b.astype(F32))
        slope_ref[:, cols] = slope.astype(BF16)
        wback = tn(hid[:, cols], fgv) + tn(value.astype(BF16), fgpv)
        dst = keep_ref if i == 0 else send_ref
        dst[...] = wback.astype(dst.dtype)


def ffn_in_weight_kernel(
    tb, n2, n2p, fgp, hg, slope, wback0, c2,
    keep_ref, send_ref,
):
    n2v, n2pv, fgpv = n2[...], n2p[...], fgp[...]
    for i, wb in enumerate((wback0[...], c2[904:1416, :])):
        cols = slice(512 * i, 512 * i + 512)
        hgp = (nt(fgpv, wb) * slope[:, cols].astype(F32)).astype(BF16)
        hgo = hg[:, cols]
        win = tn(n2v, hgo) + tn(n2pv, hgp)
        bias = jnp.sum(hgo.astype(F32), axis=0, keepdims=True) + jnp.sum(hgp.astype(F32), axis=0, keepdims=True)
        dst = keep_ref if i == 0 else send_ref
        dst[0:512, :] = win.astype(dst.dtype)
        dst[512:520, :] = jnp.broadcast_to(bias, (8, 512)).astype(dst.dtype)


def small_weight_kernel(
    tb, n, n2, ltg, log, att, attp, bg, sums,
    keep_ref, send_ref,
    g1, g2,
):
    keep_ref[768:776, :] = sums[...]
    send_ref[768:776, :] = sums[...].astype(BF16)
    g2[...] = tn(n2[...], ltg[...])
    g1[...] = tn(n[0:256, :], log[...])
    bgv = bg[...]
    wo = (tn(att[:, 0:128], bgv), tn(attp[:, 0:128], bgv), tn(att[:, 128:256], bgv), tn(attp[:, 128:256], bgv))
    for i in range(4):
        src = pl.ds(pl.multiple_of(tb[i] * 128, 128), 128)
        dst = keep_ref if i < 2 else send_ref
        base = 384 * (i % 2)
        dst[base : base + 128, :] = g2[src, :].astype(dst.dtype)
        dst[base + 128 : base + 256, :] = g1[src, :].astype(dst.dtype)
        dst[base + 256 : base + 384, :] = wo[i].astype(dst.dtype)


def prepare_kernel(tb, n, k, qa0, qb0, qa1, qb1, v_ref, kt_ref):
    nv = n[...]
    for c, w in enumerate(((qa0, qb0), (qa1, qb1))):
        v = nn(nv, weight_of(w, 2)) + bias_of(w, 2)
        v_ref[:, 128 * c : 128 * c + 128] = v.astype(BF16)
    kt_ref[...] = k[...].astype(F32).T.astype(BF16)


def attend_back(qb, tb, segs, p, dot, ot, invl, qt, kt, v, dk, dv, dq, doz, dos, dlt):
    rows = 256
    tq = tb[qb]
    zero = jnp.zeros((64, rows), BF16)
    for h in range(4):
        hs = slice(64 * h, 64 * h + 64)
        scale = invl[h, 0:1, :]
        dv_h = dot[hs, :].astype(F32)
        delta = jnp.sum(dv_h * ot[hs, :].astype(F32), axis=0, keepdims=True) * scale
        dlt[h] = jnp.broadcast_to(delta, (8, rows))
        mine = (dv_h * scale).astype(BF16)
        dos[hs, :] = mine
        doz[h] = jnp.concatenate([mine, zero] if h % 2 == 0 else [zero, mine], axis=0)
    dq[...] = jnp.zeros(dq.shape, F32)

    @pl.loop(0, 4)
    def _(kb):
        tk = tb[kb]

        @pl.when((tk <= tq) & (segs[0, tk * rows + rows - 1] >= segs[0, tq * rows]))
        def _():
            ks = pl.ds(pl.multiple_of(kb * rows, rows), rows)
            for h in range(4):
                pair = 128 * (h // 2)
                hs = slice(64 * h, 64 * h + 64)
                ph = p[h, ks, :]
                dp = nn(v[ks, pair : pair + 128], doz[h])
                ds = (ph.astype(F32) * (dp - dlt[h, 0:1, :])).astype(BF16)
                dv[hs, ks] = dv[hs, ks] + nt(dos[hs, :], ph)
                dk[hs, ks] = dk[hs, ks] + nt(qt[hs, :], ds)
                dq[hs, :] = dq[hs, :] + nn(kt[hs, ks], ds)


def back_first_kernel(
    tb, segs, p, dot, ot, invl, qt, kt, v,
    dk_ref, dv_ref, dq_ref,
    dq, doz, dos, dlt,
):
    dk_ref[...] = jnp.zeros(dk_ref.shape, F32)
    dv_ref[...] = jnp.zeros(dv_ref.shape, F32)
    attend_back(0, tb, segs, p, dot, ot, invl, qt, kt, v, dk_ref, dv_ref, dq, doz, dos, dlt)
    dq_ref[...] = (dq[...] * HD ** (-0.5)).astype(BF16)


def back_second_kernel(
    tb, segs, p, dot, ot, invl, qt, kt, v, dk0, dv0, dq0, n,
    dqt_ref, dkt_ref, dvt_ref, keep_ref, send_ref,
    dk, dv, dq, doz, dos, dlt,
):
    dk[...] = dk0[...]
    dv[...] = dv0[...]
    attend_back(1, tb, segs, p, dot, ot, invl, qt, kt, v, dk, dv, dq, doz, dos, dlt)
    dqt_ref[:, 0:256] = dq0[...]
    dqt_ref[:, 256:512] = (dq[...] * HD ** (-0.5)).astype(BF16)
    dkt_ref[...] = dk[...].astype(BF16)
    dvt_ref[...] = dv[...].astype(BF16)
    nv = n[...]
    wq = nn(dqt_ref[...], nv[0:512, :])
    wk = nn(dkt_ref[...], nv)
    wv = nn(dvt_ref[...], nv)
    for i, w in enumerate((wq, wk, wv)):
        keep_ref[128 * i : 128 * i + 128, :] = w[0:128, :]
        send_ref[128 * i : 128 * i + 128, :] = w[128:256, :].astype(BF16)
    ones_q = jnp.ones((8, 512), BF16)
    ones_v = jnp.ones((8, 1024), BF16)
    bq = nt(ones_q, dqt_ref[...])
    bv = nt(ones_v, dvt_ref[...])
    empty = jnp.zeros((8, 256), F32)
    keep_ref[384:392, :] = jnp.concatenate([bq[:, 0:128], bv[:, 0:128], empty], axis=1)
    send_ref[384:392, :] = jnp.concatenate([bq[:, 128:256], bv[:, 128:256], empty], axis=1).astype(BF16)


def input_kernel(tb, dqt, dkt, dvt, qa0, qb0, qa1, qb1, own_ref, par_ref, send_ref):
    def weight(part):
        return jnp.concatenate([weight_of((qa0, qb0), part), weight_of((qa1, qb1), part)], axis=1)

    wk, wv = weight(1), weight(2)
    g = nn(wk, dkt[...]) + nn(wv, dvt[...])
    send_ref[...] = g[:, 512:1024].astype(BF16)
    g0 = g[:, 0:512] + nn(weight(0), dqt[...])
    own_ref[...] = g0[:, 0:256]
    par_ref[...] = g0[:, 256:512]


def last_kernel(tb, own, sib, par, x0, mg, log, vecs, e0, e1, e2, e3, grad_ref, sums_ref, gw):
    gather_gate(tb, (e0, e1, e2, e3), 128, gw)
    total = own[...] + sib[:, 0:256].astype(F32) + par[...].astype(F32)
    ng = total.T + nt(log[...], gw[...])
    unit, inverse = norm_unit(x0[...].astype(F32))
    g = ng * vecs[0:1, :]
    back = inverse * (g - jnp.mean(g, axis=-1, keepdims=True) - unit * jnp.mean(g * unit, axis=-1, keepdims=True))
    grad_ref[...] = mg[...] + back
    sums_ref[...] = jnp.zeros((8, 512), F32)
    sums_ref[0:1, :] = jnp.sum(ng * unit, axis=0, keepdims=True)
    sums_ref[1:2, :] = jnp.sum(ng, axis=0, keepdims=True)


def run_copies(moves, sems):
    copies = [pltpu.make_async_copy(src, dst, sems.at[i]) for i, (src, dst) in enumerate(moves)]
    for copy in copies:
        copy.start()
    for copy in copies:
        copy.wait()


def pack_kernel(pos, w_in, w_back, w_out, g1, g2, wq, wk, wv, *refs):
    vectors, (s_ref, e_ref, c_ref, qa_ref, qb_ref, vecs), (sems, cut, *lines) = refs[:11], refs[11:17], refs[17:]
    start = pl.multiple_of((pos[4] & 3) * 128, 128)
    gate = pl.multiple_of((pos[4] & 3) * 32, 32)
    moves = [
        (w_in.at[:, pl.ds(start, 128)], cut),
        (w_back.at[pl.ds(start, 128), :], s_ref.at[128:256, :]),
        (g2.at[pl.ds(gate, 32), :], s_ref.at[264:296, :]),
    ]
    for i, w in enumerate((wq, wk, wv)):
        cols = slice(128 * i, 128 * i + 128)
        moves.append((w.at[0:256, :], qa_ref.at[:, cols]))
        moves.append((w.at[256:512, :], qb_ref.at[0:256, cols]))
    late = [
        (w_out, e_ref.at[0:128, :]),
        (g1, e_ref.at[128:256, :]),
        (w_out, c_ref.at[0:128, :]),
        (g1, c_ref.at[128:256, :]),
        (g2, c_ref.at[256:384, :]),
        (w_in, c_ref.at[392:904, :]),
        (w_back, c_ref.at[904:1416, :]),
    ]
    moves = moves + list(zip(vectors, lines)) + late
    copies = [pltpu.make_async_copy(src, dst, sems.at[i]) for i, (src, dst) in enumerate(moves)]
    for copy in copies:
        copy.start()
    for copy in copies[: len(moves) - len(late)]:
        copy.wait()
    for i, v in enumerate(lines[:9]):
        vecs[i : i + 1, :] = v[...].astype(F32).reshape(1, 512)
    bq = lines[9][...].astype(F32).reshape(1, 128)
    bv = lines[10][...].astype(F32).reshape(1, 128)
    vecs[9:16, :] = jnp.zeros((7, 512), F32)
    s_ref[0:128, :] = cut[...].astype(F32).T.astype(BF16)
    bias = vecs[8:9, pl.ds(start, 128)]
    s_ref[256:264, :] = jnp.broadcast_to(jnp.concatenate([bias] * 4, axis=1), (8, 512)).astype(BF16)
    c_ref[384:392, :] = jnp.broadcast_to(vecs[8:9, :], (8, 512)).astype(BF16)
    for i, bias in enumerate((bq, jnp.zeros_like(bq), bv)):
        qb_ref[256:264, 128 * i : 128 * i + 128] = jnp.broadcast_to(bias, (8, 128)).astype(BF16)
    for copy in copies[len(moves) - len(late) :]:
        copy.wait()


def half_rows_kernel(tb, keep, recv, out_ref):
    out_ref[...] = (keep[384:, :] + recv[384:, :].astype(F32)).astype(BF16)


def half_columns_kernel(tb, keep, recv, out_ref):
    half = keep.shape[1]
    out_ref[...] = (keep[...] + recv[:, half:].astype(F32)).astype(BF16)


def padded(rows, n_dp):
    unit = 8 * n_dp
    return -(-rows // unit) * unit


def bit_of(pos, b):
    return (pos[4] >> b) & 1


def sum_into(dst, at, addends, rows):
    value = None
    for ref, start in addends:
        block = ref[start : start + rows, :].astype(F32)
        value = block if value is None else value + block
    dst[at : at + rows, :] = value


def cut_rows(total, at, rows, bit, own, own_at, send, send_at):
    half = rows // 2
    mine = pl.multiple_of(at + bit * half, 8)
    other = pl.multiple_of(at + (1 - bit) * half, 8)
    own[own_at : own_at + half, :] = total[pl.ds(mine, half), :]
    send[send_at : send_at + half, :] = total[pl.ds(other, half), :].astype(BF16)


def pick(refs, groups):
    it = iter(refs)
    return [(rows, [(next(it), start) for start in starts]) for rows, starts in groups]


def halves_kernel(pos, *refs, parts, rows, bits):
    count = sum(len(starts) for groups in parts for _, starts in groups)
    ins, (own1, send1, own2, send2, total) = refs[:count], refs[count:]
    used = 0
    for groups, bit, own, send in zip(parts, bits, (own1, own2), (send1, send2)):
        need = sum(len(starts) for _, starts in groups)
        at = 0
        for size, addends in pick(ins[used : used + need], groups):
            sum_into(total, at, addends, size)
            at += size
        used += need
        if at < rows:
            total[at:, :] = jnp.zeros((rows - at, 512), F32)
        cut_rows(total, 0, rows, bit_of(pos, bit), own, 0, send, 0)


def merge_kernel(pos, own1, recv1, own2, recv2, own, send, total, *, bit):
    rows = own1.shape[0]
    for i, (o, r) in enumerate(((own1, recv1), (own2, recv2))):
        total[...] = o[...] + r[...].astype(F32)
        cut_rows(total, 0, rows, bit_of(pos, bit), own, i * rows // 2, send, i * rows // 2)


def round_kernel(pos, *refs, count, small):
    out = refs[-1]
    at = 0
    for i in range(0, count, 2):
        rows = refs[i].shape[0]
        out[at : at + rows, :] = (refs[i][...] + refs[i + 1][...].astype(F32)).astype(BF16)
        at += rows
    out[at : at + 8, :] = jnp.zeros((8, 512), BF16)
    used = count
    for first, size, starts in small:
        value = None
        for ref, start in zip(refs[used : used + len(starts)], starts):
            block = ref[start : start + size, :].astype(F32)
            value = block if value is None else value + block
        out[at + first : at + first + size, :] = value.astype(BF16)
        used += len(starts)


def both_kernel(pos, own0, recv0, own, send, total, *, bit):
    rows = own0.shape[0] // 2
    total[...] = own0[...] + recv0[...].astype(F32)
    for i in range(2):
        cut_rows(total, i * rows, rows, bit_of(pos, bit), own, i * rows // 2, send, i * rows // 2)


def settle_kernel(pos, own, recv, out):
    out[...] = (own[...].astype(F32) + recv[...].astype(F32)).astype(BF16)


def stack_kernel(pos, held, recv, out):
    size = held.shape[0]
    out[0:size] = held[...]
    out[size:] = recv[...]


def part_rows(value, at, rows, out1, out2):
    out1[at, 0:rows, :] = value[0:rows]
    out1[at, rows : rows + 8, :] = value[2 * rows :]
    out2[at] = value[rows : 2 * rows]


def settle_part_kernel(pos, own, recv, out1, out2):
    rows = (own.shape[0] - 8) // 2
    value = (own[...].astype(F32) + recv[...].astype(F32)).astype(BF16)
    part_rows(value, 0, rows, out1, out2)


def part_kernel(pos, held, recv, out1, out2):
    size, rows = held.shape[0], (held.shape[1] - 8) // 2
    for i, r in enumerate((held, recv)):
        for j in range(size):
            part_rows(r[j], i * size + j, rows, out1, out2)


def pair_kernel(pos, held1, recv1, held2, recv2, out1, out2):
    for out, h, r in ((out1, held1, recv1), (out2, held2, recv2)):
        size = h.shape[0]
        out[0:size] = h[...]
        out[size:] = r[...]


def unpack_kernel(pos, held1, recv1, held2, recv2, *refs, plans, orders, small):
    outs, scratch, sums = refs[:-2], refs[-2], refs[-1]
    rows = held2.shape[1]
    used = 0
    for plan, order, blocks in zip(plans, orders, ((held1, recv1), (held2, recv2))):
        place = 0
        for b in order:
            place = place * 2 + bit_of(pos, b)
        each = blocks[0].shape[0]
        for i in range(2 * each):
            at = pl.multiple_of((place ^ i) * rows, 8)
            scratch[pl.ds(at, rows), :] = blocks[i // each][i % each, 0:rows, :].astype(F32)
        for start, size, flip in plan:
            block = scratch[start : start + size, :]
            outs[used][...] = block.T if flip else block
            used += 1
    total = jnp.zeros((8, 512), F32)
    for r in (held1, recv1):
        total = total + jnp.sum(r[:, rows:, :].astype(F32), axis=0)
    sums[...] = total
    for i, (row, start, size) in enumerate(small):
        outs[used + i][...] = sums[row : row + 1, start : start + size].reshape(size)


def body(
    layer_input, segments, norm1_gain, norm1_bias, w_query, b_query, w_key, w_value, b_value,
    w_out, b_out, gate1_w, gate1_b, norm2_gain, norm2_bias, w_in, b_in, w_back, b_back,
    gate2_w, gate2_b, cotangent, *, n_dp,
):
    def hop(value, mask):
        return lax.ppermute(value, "tensor", [(i, i ^ mask) for i in range(4)])

    def dhop(value, mask):
        return lax.ppermute(value, "dp", [(i, i ^ mask) for i in range(n_dp)])

    def after(value, *deps):
        return lax.optimization_barrier((value,) + deps)[0]

    t = lax.axis_index("tensor").astype(jnp.int32)
    me = lax.axis_index("dp").astype(jnp.int32)
    tb = jnp.where(jnp.arange(8) < 4, t ^ jnp.array(LOCAL + (0,) * 4, jnp.int32), me)
    seg = segments
    x0 = layer_input
    last = [None]

    def step(kernel, outs, args, name, scratch=(), smem=1, space=VM, then=(), limit=None, cost=HEAVY):
        pos = tb if last[0] is None else after(tb, last[0], *then)
        got = call(kernel, outs, [pos] + args, smem=smem, scratch=scratch, name=name, space=space, limit=limit, cost=COSTS.get(name, cost))
        last[0] = got[0]
        return got

    x1 = hop(x0, PX)
    x2 = hop(x0, 1)
    hbm = dict(space=pl.BlockSpec(memory_space=pltpu.MemorySpace.HBM), cost=LIGHT)
    s0, e0, c0, qa0, qb0, vecs = step(
        pack_kernel,
        [sds((296, 512), BF16), sds((256, 512), BF16), sds((1416, 512), BF16), sds((256, 384), BF16),
         sds((264, 384), BF16), sds((16, 512), F32)],
        [pltpu.with_memory_space_constraint(w, pltpu.MemorySpace.HBM) for w in
         (w_in, w_back, w_out, gate1_w, gate2_w, w_query, w_key, w_value, norm1_gain, norm1_bias, b_out, gate1_b,
          norm2_gain, norm2_bias, b_back, gate2_b, b_in, b_query, b_value)],
        "pack",
        [pltpu.SemaphoreType.DMA((27,)), pltpu.VMEM((512, 128), BF16)]
        + [pltpu.VMEM((512,), BF16)] * 9 + [pltpu.VMEM((128,), BF16)] * 2, **hbm,
    )
    qkv = [qa0, qb0, hop(qa0, 1), hop(qb0, 1)]
    sy = hop(s0, PX)
    c2 = hop(c0, 1)
    na, qt0, ka, vta = step(
        chip_kernel,
        [sds((512, 512), BF16), sds((256, 256), BF16), sds((512, 256), BF16), sds((256, 512), BF16)],
        [x0, x2, vecs] + qkv, "chip", cost=LIGHT,
    )
    x3 = hop(after(x1, na), 1)
    e1 = hop(after(e0, na), PX)
    n, qt1, k, vt, p1, ot1, att1, invl1 = step(
        first_kernel,
        [
            sds((1024, 512), BF16), sds((256, 256), BF16), sds((1024, 256), BF16),
            sds((256, 1024), BF16), sds((4, 1024, 256), BF16), sds((256, 256), BF16), sds((256, 256), BF16),
            sds((4, 8, 256), F32),
        ],
        [seg, seg, x1, x3, vecs] + qkv + [na, ka, vta],
        "first", ATT_SCRATCH, 2,
    )
    attp = hop(att1, PX)
    sy = after(sy, att1)
    sx = dhop(sy, 1)
    sz = dhop(sy, 2)
    p0, ot0, att0, invl0 = step(
        second_kernel,
        [sds((4, 1024, 256), BF16), sds((256, 256), BF16), sds((256, 256), BF16), sds((4, 8, 256), F32)],
        [seg, seg, qt0, k, vt],
        "second", ATT_SCRATCH, 2,
    )
    e3 = hop(after(e1, att0), 1)
    v, kt = step(prepare_kernel, [sds((1024, 256), BF16), sds((256, 1024), BF16)], [n, k] + qkv, "prepare")
    n2, mid, branch, gate = step(
        out_kernel,
        [sds((256, 512), BF16), sds((256, 512), F32), sds((256, 512), F32), sds((256, 512), F32)],
        [x0, n, att0, attp, vecs, e0, e1, c2, e3],
        "out", [pltpu.VMEM((512, 512), BF16)],
    )
    cut_a, cut_b = step(cut_kernel, [sds((128, 512), BF16), sds((168, 512), BF16)], [sx, sz], "cut")
    sxz_a, sxz_b = dhop(cut_a, 1), dhop(cut_b, 2)
    n2p = hop(after(n2, cut_a), PX)
    quarters = [sy, hop(after(sy, cut_a), 1), sx, hop(after(sx, cut_a), 1), sz, hop(after(sz, cut_a), 1)]
    total0, hid, slope0, slope1 = step(
        ffn_first_kernel,
        [sds((256, 512), F32), sds((256, 1024), BF16), sds((256, 1024), BF16), sds((256, 768), BF16)],
        [n2, vecs, w_in, w_back, c2] + quarters,
        "ffn_first", cost=LIGHT,
    )
    sxz_a, sxz_b = lax.optimization_barrier((sxz_a, sxz_b, total0))[0:2]
    quarters = quarters + [sxz_a, hop(sxz_a, 1), sxz_b, hop(sxz_b, 1)]
    result, fg, ltg, slope2 = step(
        ffn_kernel,
        [sds((256, 512), BF16), sds((256, 512), BF16), sds((256, 512), BF16), sds((256, 256), BF16)],
        [n2, mid, cotangent, vecs, gate2_w, c2, total0] + quarters,
        "ffn", [pltpu.VMEM((512, 512), BF16)],
    )
    fgp = hop(fg, PX)
    dot0, dotp, mg, bg, log, hg, sums = step(
        back_kernel,
        [
            sds((256, 256), BF16), sds((256, 256), BF16), sds((256, 512), F32), sds((256, 512), BF16),
            sds((256, 512), BF16), sds((256, 1024), BF16), sds((8, 512), F32),
        ],
        [fg, ltg, slope0, slope1, slope2, mid, branch, gate, cotangent, vecs, e0, e1, c2, e3, gate2_w, w_in, w_back]
        + quarters,
        "back", [pltpu.VMEM((512, 512), BF16)], then=(n2p,),
    )
    dot1 = hop(dotp, PX)
    skeep, ssend = step(
        small_weight_kernel,
        [sds((776, 512), F32), sds((776, 512), BF16)],
        [n, n2, ltg, log, att0, attp, bg, sums],
        "small_weight", [pltpu.VMEM((512, 512), F32), pltpu.VMEM((512, 512), F32)],
    )
    srecv = hop(ssend, 1)
    back_scratch = [
        pltpu.VMEM((256, 256), F32), pltpu.VMEM((4, 128, 256), BF16), pltpu.VMEM((256, 256), BF16),
        pltpu.VMEM((4, 8, 256), F32),
    ]
    dk0, dv0, dq0 = step(
        back_first_kernel,
        [sds((256, 1024), F32), sds((256, 1024), F32), sds((256, 256), BF16)],
        [seg, p0, dot0, ot0, invl0, qt0, kt, v],
        "attn_back0", back_scratch, 2,
    )
    (spar,) = step(half_rows_kernel, [sds((392, 512), BF16)], [skeep, srecv], "half_rows")
    sparr = hop(spar, PX)
    bkeep, bsend, slopep = step(
        ffn_back_weight_kernel,
        [sds((512, 512), F32), sds((512, 512), BF16), sds((256, 1024), BF16)],
        [n2p, fg, fgp, hid, vecs, w_in, c2],
        "ffn_back_weight",
    )
    brecv = hop(bsend, 1)
    ikeep, isend = step(
        ffn_in_weight_kernel,
        [sds((520, 512), F32), sds((520, 512), BF16)],
        [n2, n2p, fgp, hg, slopep, w_back, c2],
        "ffn_in_weight",
    )
    irecv = hop(isend, 1)
    bits = n_dp.bit_length() - 1

    def halves(tag, parts1, parts2, rows):
        arrays = [a for parts in (parts1, parts2) for _, group in parts for a, _ in group]
        static = tuple(
            tuple((m, tuple(start for _, start in group)) for m, group in parts) for parts in (parts1, parts2)
        )
        shapes = [sds((rows // 2, 512), F32), sds((rows // 2, 512), BF16)] * 2
        o1, s1, o2, s2 = step(
            functools.partial(halves_kernel, parts=static, rows=rows, bits=(0, 1)),
            shapes, arrays, "halves_" + tag, [pltpu.VMEM((rows, 512), F32)],
        )
        return o1, dhop(s1, 1), o2, dhop(s2, 2)

    def quarter_step(tag, o1, r1, o2, r2):
        rows = o1.shape[0]
        shapes = [sds((rows // 2, 512), F32), sds((rows // 2, 512), BF16)] * 2
        o1, s1, o2, s2 = step(
            functools.partial(halves_kernel, parts=(((rows, (0, 0)),),) * 2, rows=rows, bits=(1, 0)),
            shapes, [o1, r1, o2, r2], "quarters_" + tag, [pltpu.VMEM((rows, 512), F32)],
        )
        return o1, dhop(s1, 2), o2, dhop(s2, 1)

    def merge_step(tag, o1, r1, o2, r2, small):
        rows = o1.shape[0]
        pairs = [o1, r1, o2, r2]
        for b in range(2, bits - 1):
            kernel = merge_kernel if b == 2 else both_kernel
            own, sent = step(
                functools.partial(kernel, bit=b), [sds((rows, 512), F32), sds((rows, 512), BF16)],
                pairs, "cut_" + tag, [pltpu.VMEM((rows if b == 2 else 2 * rows, 512), F32)],
            )
            pairs, rows = [own, dhop(sent, 1 << b)], rows // 2
        static = tuple((f, m, tuple(start for _, start in group)) for f, m, group in small)
        arrays = [a for _, _, group in small for a, _ in group]
        own = step(
            functools.partial(round_kernel, count=len(pairs), small=static), [sds((2 * rows + 8, 512), BF16)],
            pairs + arrays, "merge_" + tag,
        )[0]
        return own, dhop(own, 1 << (bits - 1))

    def part_step(tag, own, recv):
        rows = (own.shape[0] - 8) // 2
        if bits > 3:
            held = step(settle_kernel, [sds(own.shape, BF16)], [own, recv], "settle")[0][None]
            for b in range(bits - 2, 2, -1):
                shape = (2 * held.shape[0],) + held.shape[1:]
                held = step(stack_kernel, [sds(shape, BF16)], [held, dhop(held, 1 << b)], "stack")[0]
            size = 2 * held.shape[0]
            kernel, args = part_kernel, [held, dhop(held, 4)]
        else:
            size, kernel, args = 1, settle_part_kernel, [own, recv]
        h1, h2 = step(kernel, [sds((size, rows + 8, 512), BF16), sds((size, rows, 512), BF16)], args, "part_" + tag)
        return h1, dhop(h1, 2), h2, dhop(h2, 1)

    def pair_step(tag, h1, r1, h2, r2):
        shapes = [sds((2 * h.shape[0],) + h.shape[1:], BF16) for h in (h1, h2)]
        h1, h2 = step(pair_kernel, shapes, [h1, r1, h2, r2], "pair_" + tag)
        return h1, dhop(h1, 1), h2, dhop(h2, 2)

    def unpack_step(tag, h1, r1, h2, r2, plans, small):
        shapes = [sds((512, size) if flip else (size, 512), F32) for plan in plans for _, size, flip in plan]
        rest = tuple(range(2, bits - 1))
        rows = 2 * h2.shape[0] * h2.shape[1]
        return step(
            functools.partial(unpack_kernel, plans=plans, orders=((0, 1) + rest, (1, 0) + rest), small=small),
            shapes + [sds((size,), F32) for _, _, size in small], [h1, r1, h2, r2], "unpack_" + tag,
            [pltpu.VMEM((rows, 512), F32), pltpu.VMEM((8, 512), F32)],
        )

    f = halves("f", [(512, [(bkeep, 0), (brecv, 0)])], [(512, [(ikeep, 0), (irecv, 0)])], padded(512, n_dp))

    dqt, dkt, dvt, akeep, asend = step(
        back_second_kernel,
        [
            sds((256, 512), BF16), sds((256, 1024), BF16), sds((256, 1024), BF16), sds((392, 512), F32),
            sds((392, 512), BF16),
        ],
        [seg, p1, dot1, ot1, invl1, qt1, kt, v, dk0, dv0, dq0, n],
        "attn_back1", [pltpu.VMEM((256, 1024), F32), pltpu.VMEM((256, 1024), F32)] + back_scratch, 2,
    )
    arecv = hop(asend, 1)
    gown, gpar, gsend = step(
        input_kernel,
        [sds((512, 256), F32), sds((512, 256), F32), sds((512, 512), BF16)],
        [dqt, dkt, dvt] + qkv,
        "input_grad",
    )
    gsib = hop(gsend, 1)
    f = quarter_step("f", *f)
    a = halves(
        "a", [(384, [(akeep, 0), (arecv, 0)])], [(384, [(skeep, 0), (srecv, 0), (sparr, 0)])], padded(384, n_dp)
    )
    (gsum,) = step(half_columns_kernel, [sds((512, 256), BF16)], [gpar, gsib], "half_columns")
    gp = hop(gsum, PX)
    tail = [(skeep, 773), (srecv, 773), (sparr, 389)]
    f = merge_step("f", *f, [(0, 1, [(ikeep, 512), (irecv, 512)]), (1, 1, tail)])
    a = quarter_step("a", *a)
    input_grad, sums1 = step(
        last_kernel,
        [sds((256, 512), F32), sds((8, 512), F32)],
        [gown, gsib, gp, x0, mg, log, vecs, e0, e1, c2, e3],
        "last", [pltpu.VMEM((512, 512), BF16)],
    )
    sums1_b = hop(sums1, PX)
    sums1_a = hop(sums1, 1)
    sums1_c = hop(sums1, PX ^ 1)
    group = [(skeep, 768), (srecv, 768), (sparr, 384)]
    a = merge_step(
        "a", *a,
        [(0, 2, [(sums1, 0), (sums1_a, 0), (sums1_b, 0), (sums1_c, 0)]), (2, 1, [(akeep, 384), (arecv, 384)]),
         (3, 5, group)],
    )
    f = part_step("f", *f)
    f = pair_step("f", *f)
    a = part_step("a", *a)
    a = pair_step("a", *a)
    g_wback, g_win, d_b_in, d_n2b = unpack_step(
        "f", *f, (((0, 512, False),), ((0, 512, False),)), ((0, 0, 512), (1, 0, 512))
    )
    plans = (
        ((0, 128, True), (128, 128, True), (256, 128, True)),
        ((0, 128, False), (128, 128, False), (256, 128, False)),
    )
    small = ((0, 0, 512), (1, 0, 512), (2, 0, 128), (2, 128, 128)) + tuple((i, 0, 512) for i in range(3, 8))
    g_q, g_k, g_v, g_g2, g_g1, g_wo, d_n1g, d_n1b, d_bq, d_bv, d_b_back, d_g2b, d_b_out, d_g1b, d_n2g = unpack_step(
        "a", *a, plans, small
    )
    return (
        result, input_grad, d_n1g, d_n1b, g_q, d_bq, g_k, g_v, d_bv, g_wo, d_b_out, g_g1, d_g1b, d_n2g, d_n2b,
        g_win, d_b_in, g_wback, d_b_back, g_g2, d_g2b,
    )


def solution(mesh):
    tok = P(("dp", "tensor"), None)
    col = P(None, "tensor")
    row = P("tensor", None)
    vec = P("tensor")
    rep = P()
    return jax.shard_map(
        functools.partial(body, n_dp=mesh.shape["dp"]),
        mesh=mesh,
        in_specs=(
            tok, P("dp", None), rep, rep, col, vec, col, col, vec, row, rep, row, rep, rep, rep,
            col, vec, row, rep, row, rep, tok,
        ),
        out_specs=(
            tok, tok, rep, rep, col, vec, col, col, vec, row, rep, row, rep, rep, rep,
            col, vec, row, rep, row, rep,
        ),
        check_vma=False,
    )
```

```python
import functools
import math

import jax
import jax.numpy as jnp
from jax import lax
from jax.experimental import pallas as pl
from jax.experimental.pallas import tpu as pltpu
from jax.sharding import PartitionSpec as P

HD = 64
EPSILON = 1e-05
F32 = jnp.float32
BF16 = jnp.bfloat16
NEG = -1e30
PX = 2
LOCAL = (0, PX, 1, 1 ^ PX)
SPARE = 4 * 1024 * 1024
HEAVY = 10**10
LIGHT = 0
AHEAD = ("a", "f")
COSTS = {"halves_f": 0, "halves_a": 0, "input_grad": 0, "part_f": 0, "merge_a": 0, "last": 0, "first": 0, "ffn": 0, "part_a": 0, "unpack_f": 2*10**10}


def nn(a, b):
    return lax.dot_general(a, b, (((1,), (0,)), ((), ())), preferred_element_type=F32)


def nt(a, b):
    return lax.dot_general(a, b, (((1,), (1,)), ((), ())), preferred_element_type=F32)


def tn(a, b):
    return lax.dot_general(a, b, (((0,), (0,)), ((), ())), preferred_element_type=F32)


VM = pl.BlockSpec(memory_space=pltpu.VMEM)
SM = pl.BlockSpec(memory_space=pltpu.SMEM)


def call(body, outs, args, smem=0, scratch=(), name=None, space=VM, limit=None, cost=0):
    nbytes = sum(a.size * a.dtype.itemsize for a in args) + sum(o.size * o.dtype.itemsize for o in outs)
    held = sum(math.prod(s.shape) * 4 for s in scratch)
    limit = limit or nbytes + held + SPARE
    return pl.pallas_call(
        body,
        out_shape=tuple(outs),
        in_specs=[SM] * smem + [space] * (len(args) - smem),
        out_specs=tuple([VM] * len(outs)),
        scratch_shapes=list(scratch),
        compiler_params=pltpu.CompilerParams(vmem_limit_bytes=limit),
        cost_estimate=pl.CostEstimate(flops=cost, bytes_accessed=0, transcendentals=0),
        name=name,
    )(*args)


def sds(shape, dtype):
    return jax.ShapeDtypeStruct(shape, dtype)


def norm_unit(values):
    centred = values - jnp.mean(values, axis=-1, keepdims=True)
    spread = jnp.mean(centred * centred, axis=-1, keepdims=True)
    inverse = lax.rsqrt(spread + EPSILON)
    return centred * inverse, inverse


def sigmoid(v):
    return 1.0 / (1.0 + jnp.exp(-v))


C0 = 0.7978845608028654
C1 = 0.044715


def gelu_parts(u):
    square = u * u
    t = jnp.tanh(C0 * u * (1.0 + C1 * square))
    half = 0.5 * (1.0 + t)
    value = u * half
    slope = half + (0.5 * C0) * u * (1.0 - t * t) * (1.0 + (3.0 * C1) * square)
    return value, slope


def attend_query_block(qb, tb, segs, segv, qz, k, vt, p_ref, ot_ref, invl_ref, s_sc, m_sc, l_sc, o_sc, segc):
    rows = 256
    tq = tb[qb]
    m_sc[...] = jnp.full(m_sc.shape, NEG, F32)
    l_sc[...] = jnp.zeros(l_sc.shape, F32)
    o_sc[...] = jnp.zeros(o_sc.shape, F32)
    seg_q = segv[0:1, pl.ds(pl.multiple_of(tq * rows, rows), rows)].astype(F32)

    def active(kb):
        tk = tb[kb]
        return (tk <= tq) & (segs[0, tk * rows + rows - 1] >= segs[0, tq * rows])

    @pl.loop(0, 4)
    def _(kb):
        @pl.when(active(kb))
        def _():
            tk = tb[kb]
            krows = pl.ds(pl.multiple_of(kb * rows, rows), rows)
            kpos = tk * rows + lax.broadcasted_iota(jnp.int32, (rows, rows), 0)
            qpos = tq * rows + lax.broadcasted_iota(jnp.int32, (rows, rows), 1)
            seg_k = segc[pl.ds(pl.multiple_of(tk * rows, rows), rows), 0:1]
            bias = jnp.where((kpos <= qpos) & (seg_k == seg_q), 0.0, NEG)
            for h in range(4):
                pair = 128 * (h // 2)
                s = nn(k[krows, pair : pair + 128], qz[h]) + bias
                s_sc[h, krows, :] = s
                m_sc[h] = jnp.maximum(m_sc[h], jnp.max(s.reshape(rows // 8, 8, rows), axis=0))

    for h in range(4):
        m_sc[h] = jnp.broadcast_to(jnp.max(m_sc[h], axis=0, keepdims=True), (8, rows))

    @pl.loop(0, 4)
    def _(kb):
        @pl.when(active(kb))
        def _():
            krows = pl.ds(pl.multiple_of(kb * rows, rows), rows)
            for h in range(4):
                e = jnp.exp(s_sc[h, krows, :] - m_sc[h, 0:1, :])
                l_sc[h] = l_sc[h] + jnp.sum(e.reshape(rows // 8, 8, rows), axis=0)
                pb = e.astype(BF16)
                p_ref[h, krows, :] = pb
                o_sc[h] = o_sc[h] + nn(vt[64 * h : 64 * h + 64, krows], pb)

    for h in range(4):
        invl = 1.0 / jnp.sum(l_sc[h], axis=0, keepdims=True)
        invl_ref[h] = jnp.broadcast_to(invl, (8, rows))
        ot_ref[64 * h : 64 * h + 64, :] = (o_sc[h] * invl).astype(BF16)


def fill_qz(qz, qt):
    zero = jnp.zeros((64, 256), BF16)
    for h in range(4):
        mine = qt[64 * h : 64 * h + 64, :]
        qz[h] = jnp.concatenate([mine, zero] if h % 2 == 0 else [zero, mine], axis=0)


def fill_segc(segc, segv):
    for t in range(4):
        row = jnp.broadcast_to(segv[0:1, 256 * t : 256 * t + 256].astype(F32), (128, 256))
        segc[256 * t : 256 * t + 256, :] = row.T


def weight_of(w, part):
    cols = slice(128 * part, 128 * part + 128)
    return jnp.concatenate([w[0][:, cols], w[1][0:256, cols]], axis=0)


def bias_of(w, part):
    return w[1][256:257, 128 * part : 128 * part + 128].astype(F32)


def project(n, w, c, k_ref, vt_ref, blocks):
    cols = slice(128 * c, 128 * c + 128)
    k = nn(n, weight_of(w, 1)).astype(BF16)
    vt = (nn(n, weight_of(w, 2)) + bias_of(w, 2)).T.astype(BF16)
    for i, at in enumerate(blocks):
        k_ref[at : at + 256, cols] = k[256 * i : 256 * i + 256]
        vt_ref[cols, at : at + 256] = vt[:, 256 * i : 256 * i + 256]


def query_of(n, w):
    q = nn(n, weight_of(w, 0)) + bias_of(w, 0)
    return (q.astype(BF16).astype(F32) * HD ** (-0.5)).T.astype(BF16)


def chip_kernel(pos, x0, x2, vecs, qa0, qb0, qa1, qb1, n_ref, qt_ref, k_ref, vt_ref):
    for i, x in enumerate((x0, x2)):
        unit, _ = norm_unit(x[...].astype(F32))
        n_ref[256 * i : 256 * i + 256, :] = (unit * vecs[0:1, :] + vecs[1:2, :]).astype(BF16)
    n = n_ref[...]
    for c, w in enumerate(((qa0, qb0), (qa1, qb1))):
        qt_ref[128 * c : 128 * c + 128, :] = query_of(n[0:256], w)
        project(n, w, c, k_ref, vt_ref, (0, 256))


def first_kernel(
    tb, segs, segv, x1, x3, vecs, qa0, qb0, qa1, qb1, na, ka, vta,
    n_ref, qt1_ref, k_ref, vt_ref, p_ref, ot_ref, att_ref, invl_ref,
    qz, s_sc, m_sc, l_sc, o_sc, segc,
):
    for i, x in enumerate((x1, x3)):
        unit, _ = norm_unit(x[...].astype(F32))
        n_ref[512 * i + 256 : 512 * i + 512, :] = (unit * vecs[0:1, :] + vecs[1:2, :]).astype(BF16)
    n = jnp.concatenate([n_ref[256:512, :], n_ref[768:1024, :]], axis=0)
    for c, w in enumerate(((qa0, qb0), (qa1, qb1))):
        qt1_ref[128 * c : 128 * c + 128, :] = query_of(n[0:256], w)
        project(n, w, c, k_ref, vt_ref, (256, 768))
    for i in range(2):
        src, dst = slice(256 * i, 256 * i + 256), slice(512 * i, 512 * i + 256)
        n_ref[dst, :] = na[src, :]
        k_ref[dst, :] = ka[src, :]
        vt_ref[:, dst] = vta[:, src]
    fill_segc(segc, segv)
    fill_qz(qz, qt1_ref)
    attend_query_block(1, tb, segs, segv, qz, k_ref, vt_ref, p_ref, ot_ref, invl_ref, s_sc, m_sc, l_sc, o_sc, segc)
    att_ref[...] = ot_ref[...].astype(F32).T.astype(BF16)


def second_kernel(
    tb, segs, segv, qt0, k, vt,
    p_ref, ot_ref, att_ref, invl_ref,
    qz, s_sc, m_sc, l_sc, o_sc, segc,
):
    fill_segc(segc, segv)
    fill_qz(qz, qt0)
    attend_query_block(0, tb, segs, segv, qz, k, vt, p_ref, ot_ref, invl_ref, s_sc, m_sc, l_sc, o_sc, segc)
    att_ref[...] = ot_ref[...].astype(F32).T.astype(BF16)


ATT_SCRATCH = (
    pltpu.VMEM((4, 128, 256), BF16),
    pltpu.VMEM((4, 1024, 256), F32),
    pltpu.VMEM((4, 8, 256), F32),
    pltpu.VMEM((4, 8, 256), F32),
    pltpu.VMEM((4, 64, 256), F32),
    pltpu.VMEM((1024, 128), F32),
)


def gather_gate(tb, pieces, start, scratch):
    for i, piece in enumerate(pieces):
        scratch[pl.ds(pl.multiple_of(tb[i] * 128, 128), 128), :] = piece[start : start + 128, :]


def gather_gate_two(pos, g2, c2, pieces, scratch):
    scratch[pl.ds(pl.multiple_of(pos[0] * 128, 128), 128), :] = g2[...]
    scratch[pl.ds(pl.multiple_of(pos[2] * 128, 128), 128), :] = c2[256:384, :]
    for i, piece in enumerate(pieces):
        quarter = (pos[4] ^ (i // 2)) & 3
        at = pos[1 + 2 * (i % 2)] * 128 + quarter * 32
        rows = piece.shape[0]
        scratch[pl.ds(pl.multiple_of(at, 32), 32), :] = piece[rows - 32 : rows, :]


def out_kernel(
    tb, x0, n, att, attp, vecs, e0, e1, e2, e3,
    n2_ref, mid_ref, branch_ref, gate_ref,
    gw,
):
    gather_gate(tb, (e0, e1, e2, e3), 128, gw)
    branch = nn(att[:, 0:128], e0[0:128, :]) + nn(att[:, 128:256], e2[0:128, :])
    branch = branch + nn(attp[:, 0:128], e1[0:128, :]) + nn(attp[:, 128:256], e3[0:128, :])
    branch = branch + vecs[2:3, :]
    gate = sigmoid(nn(n[0:256, :], gw[...]) + vecs[3:4, :])
    middle = x0[...].astype(F32) + gate * branch
    unit, _ = norm_unit(middle)
    n2_ref[...] = (unit * vecs[4:5, :] + vecs[5:6, :]).astype(BF16)
    mid_ref[...] = middle
    branch_ref[...] = branch
    gate_ref[...] = gate


def pair_up(a, b, start):
    return jnp.concatenate([a[start : start + 128, :], b[start : start + 128, :]], axis=0)


def pair_bias(a, b, row=256):
    return jnp.concatenate([a[row : row + 1, 0:128], b[row : row + 1, 0:128]], axis=1).astype(F32)


def cut_kernel(pos, sx, sz, a_ref, b_ref):
    a_ref[...] = sz[0:128, :]
    b_ref[...] = sx[128:296, :]


def ffn_first_kernel(
    tb, n2, vecs, win0, wback0, c2, s0, s1, s2, s3, s4, s5,
    total_ref, hid_ref, slope_ref, slope1_ref,
):
    n2v = n2[...]
    total = jnp.zeros((256, 512), F32)
    for i, (b, w, wb) in enumerate(((vecs[8:9, :], win0[...], wback0[...]), (c2[384:385, :], c2[392:904, :], c2[904:1416, :]))):
        value, slope = gelu_parts(nn(n2v, w) + b.astype(F32))
        value = value.astype(BF16)
        hid_ref[:, 512 * i : 512 * i + 512] = value
        slope_ref[:, 512 * i : 512 * i + 512] = slope.astype(BF16)
        total = total + nn(value, wb)
    for i, (a, b) in enumerate(((s0, s1), (s2, s3), (s4, s5))):
        value, slope = gelu_parts(nt(n2v, pair_up(a, b, 0)) + pair_bias(a, b))
        slope1_ref[:, 256 * i : 256 * i + 256] = slope.astype(BF16)
        total = total + nn(value.astype(BF16), pair_up(a, b, 128))
    total_ref[...] = total


def ffn_kernel(
    tb, n2, mid, ct, vecs, g2, c2, total0, s0, s1, s2, s3, s4, s5, a6, a7, b6, b7,
    out_ref, fg_ref, ltg_ref, slope_ref, gw,
):
    gather_gate_two(tb, g2, c2, (s0, s1, s2, s3, s4, s5, b6, b7), gw)
    n2v = n2[...]
    value, slope = gelu_parts(nt(n2v, pair_up(a6, a7, 0)) + pair_bias(b6, b7, 128))
    slope_ref[...] = slope.astype(BF16)
    ffn = total0[...] + nn(value.astype(BF16), pair_up(b6, b7, 0)) + vecs[6:7, :]
    gate = sigmoid(nn(n2v, gw[...]) + vecs[7:8, :])
    up = ct[...].astype(F32)
    out_ref[...] = (mid[...] + gate * ffn).astype(BF16)
    fg_ref[...] = (gate * up).astype(BF16)
    ltg_ref[...] = (up * ffn * (gate * (1.0 - gate))).astype(BF16)


def back_kernel(
    tb, fg, ltg, slope0, slope1, slope2, mid, branch, gate, ct, vecs, e0, e1, e2, e3, g2,
    win0, wback0, s0, s1, s2, s3, s4, s5, a6, a7, b6, b7,
    dot_ref, dotp_ref, mg_ref, bg_ref, log_ref, hg_ref, sums_ref,
    gw,
):
    gather_gate_two(tb, g2, e2, (s0, s1, s2, s3, s4, s5, b6, b7), gw)
    fgv = fg[...]
    ltgv = ltg[...]
    ng = nt(ltgv, gw[...])
    for i, (w, wb) in enumerate(((win0[...], wback0[...]), (e2[392:904, :], e2[904:1416, :]))):
        hg = (nt(fgv, wb) * slope0[:, 512 * i : 512 * i + 512].astype(F32)).astype(BF16)
        hg_ref[:, 512 * i : 512 * i + 512] = hg
        ng = ng + nt(hg, w)
    for i, (a, b) in enumerate(((s0, s1), (s2, s3), (s4, s5))):
        part = slope1[:, 256 * i : 256 * i + 256]
        hg = (nt(fgv, pair_up(a, b, 128)) * part.astype(F32)).astype(BF16)
        ng = ng + nn(hg, pair_up(a, b, 0))
    hg = (nt(fgv, pair_up(b6, b7, 0)) * slope2[...].astype(F32)).astype(BF16)
    ng = ng + nn(hg, pair_up(a6, a7, 0))
    unit, inverse = norm_unit(mid[...])
    g = ng * vecs[4:5, :]
    back = inverse * (g - jnp.mean(g, axis=-1, keepdims=True) - unit * jnp.mean(g * unit, axis=-1, keepdims=True))
    mg = ct[...].astype(F32) + back
    mg_ref[...] = mg
    gatev = gate[...]
    bg = (gatev * mg).astype(BF16)
    log = (mg * branch[...] * (gatev * (1.0 - gatev))).astype(BF16)
    bg_ref[...] = bg
    log_ref[...] = log
    dot_ref[0:128, :] = nt(e0[0:128, :], bg).astype(BF16)
    dot_ref[128:256, :] = nt(e2[0:128, :], bg).astype(BF16)
    dotp_ref[0:128, :] = nt(e1[0:128, :], bg).astype(BF16)
    dotp_ref[128:256, :] = nt(e3[0:128, :], bg).astype(BF16)
    rows = [fgv.astype(F32), ltgv.astype(F32), bg.astype(F32), log.astype(F32), ng * unit, ng]
    sums_ref[...] = jnp.zeros((8, 512), F32)
    for i, r in enumerate(rows):
        sums_ref[i : i + 1, :] = jnp.sum(r, axis=0, keepdims=True)


def ffn_back_weight_kernel(
    tb, n2p, fg, fgp, hid, vecs, win0, c2,
    keep_ref, send_ref, slope_ref,
):
    fgv, fgpv, n2pv = fg[...], fgp[...], n2p[...]
    for i, (b, w) in enumerate(((vecs[8:9, :], win0[...]), (c2[384:385, :], c2[392:904, :]))):
        cols = slice(512 * i, 512 * i + 512)
        value, slope = gelu_parts(nn(n2pv, w) + b.astype(F32))
        slope_ref[:, cols] = slope.astype(BF16)
        wback = tn(hid[:, cols], fgv) + tn(value.astype(BF16), fgpv)
        dst = keep_ref if i == 0 else send_ref
        dst[...] = wback.astype(dst.dtype)


def ffn_in_weight_kernel(
    tb, n2, n2p, fgp, hg, slope, wback0, c2,
    keep_ref, send_ref,
):
    n2v, n2pv, fgpv = n2[...], n2p[...], fgp[...]
    for i, wb in enumerate((wback0[...], c2[904:1416, :])):
        cols = slice(512 * i, 512 * i + 512)
        hgp = (nt(fgpv, wb) * slope[:, cols].astype(F32)).astype(BF16)
        hgo = hg[:, cols]
        win = tn(n2v, hgo) + tn(n2pv, hgp)
        bias = jnp.sum(hgo.astype(F32), axis=0, keepdims=True) + jnp.sum(hgp.astype(F32), axis=0, keepdims=True)
        dst = keep_ref if i == 0 else send_ref
        dst[0:512, :] = win.astype(dst.dtype)
        dst[512:520, :] = jnp.broadcast_to(bias, (8, 512)).astype(dst.dtype)


def small_weight_kernel(
    tb, n, n2, ltg, log, att, attp, bg, sums,
    keep_ref, send_ref,
    g1, g2,
):
    keep_ref[768:776, :] = sums[...]
    send_ref[768:776, :] = sums[...].astype(BF16)
    g2[...] = tn(n2[...], ltg[...])
    g1[...] = tn(n[0:256, :], log[...])
    bgv = bg[...]
    wo = (tn(att[:, 0:128], bgv), tn(attp[:, 0:128], bgv), tn(att[:, 128:256], bgv), tn(attp[:, 128:256], bgv))
    for i in range(4):
        src = pl.ds(pl.multiple_of(tb[i] * 128, 128), 128)
        dst = keep_ref if i < 2 else send_ref
        base = 384 * (i % 2)
        dst[base : base + 128, :] = g2[src, :].astype(dst.dtype)
        dst[base + 128 : base + 256, :] = g1[src, :].astype(dst.dtype)
        dst[base + 256 : base + 384, :] = wo[i].astype(dst.dtype)


def prepare_kernel(tb, n, k, qa0, qb0, qa1, qb1, v_ref, kt_ref):
    nv = n[...]
    for c, w in enumerate(((qa0, qb0), (qa1, qb1))):
        v = nn(nv, weight_of(w, 2)) + bias_of(w, 2)
        v_ref[:, 128 * c : 128 * c + 128] = v.astype(BF16)
    kt_ref[...] = k[...].astype(F32).T.astype(BF16)


def attend_back(qb, tb, segs, p, dot, ot, invl, qt, kt, v, dk, dv, dq, doz, dos, dlt):
    rows = 256
    tq = tb[qb]
    zero = jnp.zeros((64, rows), BF16)
    for h in range(4):
        hs = slice(64 * h, 64 * h + 64)
        scale = invl[h, 0:1, :]
        dv_h = dot[hs, :].astype(F32)
        delta = jnp.sum(dv_h * ot[hs, :].astype(F32), axis=0, keepdims=True) * scale
        dlt[h] = jnp.broadcast_to(delta, (8, rows))
        mine = (dv_h * scale).astype(BF16)
        dos[hs, :] = mine
        doz[h] = jnp.concatenate([mine, zero] if h % 2 == 0 else [zero, mine], axis=0)
    dq[...] = jnp.zeros(dq.shape, F32)

    @pl.loop(0, 4)
    def _(kb):
        tk = tb[kb]

        @pl.when((tk <= tq) & (segs[0, tk * rows + rows - 1] >= segs[0, tq * rows]))
        def _():
            ks = pl.ds(pl.multiple_of(kb * rows, rows), rows)
            for h in range(4):
                pair = 128 * (h // 2)
                hs = slice(64 * h, 64 * h + 64)
                ph = p[h, ks, :]
                dp = nn(v[ks, pair : pair + 128], doz[h])
                ds = (ph.astype(F32) * (dp - dlt[h, 0:1, :])).astype(BF16)
                dv[hs, ks] = dv[hs, ks] + nt(dos[hs, :], ph)
                dk[hs, ks] = dk[hs, ks] + nt(qt[hs, :], ds)
                dq[hs, :] = dq[hs, :] + nn(kt[hs, ks], ds)


def back_first_kernel(
    tb, segs, p, dot, ot, invl, qt, kt, v,
    dk_ref, dv_ref, dq_ref,
    dq, doz, dos, dlt,
):
    dk_ref[...] = jnp.zeros(dk_ref.shape, F32)
    dv_ref[...] = jnp.zeros(dv_ref.shape, F32)
    attend_back(0, tb, segs, p, dot, ot, invl, qt, kt, v, dk_ref, dv_ref, dq, doz, dos, dlt)
    dq_ref[...] = (dq[...] * HD ** (-0.5)).astype(BF16)


def back_second_kernel(
    tb, segs, p, dot, ot, invl, qt, kt, v, dk0, dv0, dq0, n,
    dqt_ref, dkt_ref, dvt_ref, keep_ref, send_ref,
    dk, dv, dq, doz, dos, dlt,
):
    dk[...] = dk0[...]
    dv[...] = dv0[...]
    attend_back(1, tb, segs, p, dot, ot, invl, qt, kt, v, dk, dv, dq, doz, dos, dlt)
    dqt_ref[:, 0:256] = dq0[...]
    dqt_ref[:, 256:512] = (dq[...] * HD ** (-0.5)).astype(BF16)
    dkt_ref[...] = dk[...].astype(BF16)
    dvt_ref[...] = dv[...].astype(BF16)
    nv = n[...]
    wq = nn(dqt_ref[...], nv[0:512, :])
    wk = nn(dkt_ref[...], nv)
    wv = nn(dvt_ref[...], nv)
    for i, w in enumerate((wq, wk, wv)):
        keep_ref[128 * i : 128 * i + 128, :] = w[0:128, :]
        send_ref[128 * i : 128 * i + 128, :] = w[128:256, :].astype(BF16)
    ones_q = jnp.ones((8, 512), BF16)
    ones_v = jnp.ones((8, 1024), BF16)
    bq = nt(ones_q, dqt_ref[...])
    bv = nt(ones_v, dvt_ref[...])
    empty = jnp.zeros((8, 256), F32)
    keep_ref[384:392, :] = jnp.concatenate([bq[:, 0:128], bv[:, 0:128], empty], axis=1)
    send_ref[384:392, :] = jnp.concatenate([bq[:, 128:256], bv[:, 128:256], empty], axis=1).astype(BF16)


def input_kernel(tb, dqt, dkt, dvt, qa0, qb0, qa1, qb1, own_ref, par_ref, send_ref):
    def weight(part):
        return jnp.concatenate([weight_of((qa0, qb0), part), weight_of((qa1, qb1), part)], axis=1)

    wk, wv = weight(1), weight(2)
    g = nn(wk, dkt[...]) + nn(wv, dvt[...])
    send_ref[...] = g[:, 512:1024].astype(BF16)
    g0 = g[:, 0:512] + nn(weight(0), dqt[...])
    own_ref[...] = g0[:, 0:256]
    par_ref[...] = g0[:, 256:512]


def last_kernel(tb, own, sib, par, x0, mg, log, vecs, e0, e1, e2, e3, grad_ref, sums_ref, gw):
    gather_gate(tb, (e0, e1, e2, e3), 128, gw)
    total = own[...] + sib[:, 0:256].astype(F32) + par[...].astype(F32)
    ng = total.T + nt(log[...], gw[...])
    unit, inverse = norm_unit(x0[...].astype(F32))
    g = ng * vecs[0:1, :]
    back = inverse * (g - jnp.mean(g, axis=-1, keepdims=True) - unit * jnp.mean(g * unit, axis=-1, keepdims=True))
    grad_ref[...] = mg[...] + back
    sums_ref[...] = jnp.zeros((8, 512), F32)
    sums_ref[0:1, :] = jnp.sum(ng * unit, axis=0, keepdims=True)
    sums_ref[1:2, :] = jnp.sum(ng, axis=0, keepdims=True)


def run_copies(moves, sems):
    copies = [pltpu.make_async_copy(src, dst, sems.at[i]) for i, (src, dst) in enumerate(moves)]
    for copy in copies:
        copy.start()
    for copy in copies:
        copy.wait()


def pack_kernel(pos, w_in, w_back, w_out, g1, g2, wq, wk, wv, *refs):
    vectors, (s_ref, e_ref, c_ref, qa_ref, qb_ref, vecs), (sems, cut, *lines) = refs[:11], refs[11:17], refs[17:]
    start = pl.multiple_of((pos[4] & 3) * 128, 128)
    gate = pl.multiple_of((pos[4] & 3) * 32, 32)
    moves = [
        (w_in.at[:, pl.ds(start, 128)], cut),
        (w_back.at[pl.ds(start, 128), :], s_ref.at[128:256, :]),
        (g2.at[pl.ds(gate, 32), :], s_ref.at[264:296, :]),
    ]
    for i, w in enumerate((wq, wk, wv)):
        cols = slice(128 * i, 128 * i + 128)
        moves.append((w.at[0:256, :], qa_ref.at[:, cols]))
        moves.append((w.at[256:512, :], qb_ref.at[0:256, cols]))
    late = [
        (w_out, e_ref.at[0:128, :]),
        (g1, e_ref.at[128:256, :]),
        (w_out, c_ref.at[0:128, :]),
        (g1, c_ref.at[128:256, :]),
        (g2, c_ref.at[256:384, :]),
        (w_in, c_ref.at[392:904, :]),
        (w_back, c_ref.at[904:1416, :]),
    ]
    moves = moves + list(zip(vectors, lines)) + late
    copies = [pltpu.make_async_copy(src, dst, sems.at[i]) for i, (src, dst) in enumerate(moves)]
    for copy in copies:
        copy.start()
    for copy in copies[: len(moves) - len(late)]:
        copy.wait()
    for i, v in enumerate(lines[:9]):
        vecs[i : i + 1, :] = v[...].astype(F32).reshape(1, 512)
    bq = lines[9][...].astype(F32).reshape(1, 128)
    bv = lines[10][...].astype(F32).reshape(1, 128)
    vecs[9:16, :] = jnp.zeros((7, 512), F32)
    s_ref[0:128, :] = cut[...].astype(F32).T.astype(BF16)
    bias = vecs[8:9, pl.ds(start, 128)]
    s_ref[256:264, :] = jnp.broadcast_to(jnp.concatenate([bias] * 4, axis=1), (8, 512)).astype(BF16)
    c_ref[384:392, :] = jnp.broadcast_to(vecs[8:9, :], (8, 512)).astype(BF16)
    for i, bias in enumerate((bq, jnp.zeros_like(bq), bv)):
        qb_ref[256:264, 128 * i : 128 * i + 128] = jnp.broadcast_to(bias, (8, 128)).astype(BF16)
    for copy in copies[len(moves) - len(late) :]:
        copy.wait()


def half_rows_kernel(tb, keep, recv, out_ref):
    out_ref[...] = (keep[384:, :] + recv[384:, :].astype(F32)).astype(BF16)


def half_columns_kernel(tb, keep, recv, out_ref):
    half = keep.shape[1]
    out_ref[...] = (keep[...] + recv[:, half:].astype(F32)).astype(BF16)


def padded(rows, n_dp):
    unit = 8 * n_dp
    return -(-rows // unit) * unit


def bit_of(pos, b):
    return (pos[4] >> b) & 1


def sum_into(dst, at, addends, rows):
    value = None
    for ref, start in addends:
        block = ref[start : start + rows, :].astype(F32)
        value = block if value is None else value + block
    dst[at : at + rows, :] = value


def cut_rows(total, at, rows, bit, own, own_at, send, send_at):
    half = rows // 2
    mine = pl.multiple_of(at + bit * half, 8)
    other = pl.multiple_of(at + (1 - bit) * half, 8)
    own[own_at : own_at + half, :] = total[pl.ds(mine, half), :]
    send[send_at : send_at + half, :] = total[pl.ds(other, half), :].astype(BF16)


def pick(refs, groups):
    it = iter(refs)
    return [(rows, [(next(it), start) for start in starts]) for rows, starts in groups]


def halves_kernel(pos, *refs, parts, rows, bits):
    count = sum(len(starts) for groups in parts for _, starts in groups)
    ins, (own1, send1, own2, send2, total) = refs[:count], refs[count:]
    used = 0
    for groups, bit, own, send in zip(parts, bits, (own1, own2), (send1, send2)):
        need = sum(len(starts) for _, starts in groups)
        at = 0
        for size, addends in pick(ins[used : used + need], groups):
            sum_into(total, at, addends, size)
            at += size
        used += need
        if at < rows:
            total[at:, :] = jnp.zeros((rows - at, 512), F32)
        cut_rows(total, 0, rows, bit_of(pos, bit), own, 0, send, 0)


def merge_kernel(pos, own1, recv1, own2, recv2, own, send, total, *, bit):
    rows = own1.shape[0]
    for i, (o, r) in enumerate(((own1, recv1), (own2, recv2))):
        total[...] = o[...] + r[...].astype(F32)
        cut_rows(total, 0, rows, bit_of(pos, bit), own, i * rows // 2, send, i * rows // 2)


def round_kernel(pos, *refs, count, small):
    out = refs[-1]
    at = 0
    for i in range(0, count, 2):
        rows = refs[i].shape[0]
        out[at : at + rows, :] = (refs[i][...] + refs[i + 1][...].astype(F32)).astype(BF16)
        at += rows
    out[at : at + 8, :] = jnp.zeros((8, 512), BF16)
    used = count
    for first, size, starts in small:
        value = None
        for ref, start in zip(refs[used : used + len(starts)], starts):
            block = ref[start : start + size, :].astype(F32)
            value = block if value is None else value + block
        out[at + first : at + first + size, :] = value.astype(BF16)
        used += len(starts)


def both_kernel(pos, own0, recv0, own, send, total, *, bit):
    rows = own0.shape[0] // 2
    total[...] = own0[...] + recv0[...].astype(F32)
    for i in range(2):
        cut_rows(total, i * rows, rows, bit_of(pos, bit), own, i * rows // 2, send, i * rows // 2)


def settle_kernel(pos, own, recv, out):
    out[...] = (own[...].astype(F32) + recv[...].astype(F32)).astype(BF16)


def stack_kernel(pos, held, recv, out):
    size = held.shape[0]
    out[0:size] = held[...]
    out[size:] = recv[...]


def part_rows(value, at, rows, out1, out2):
    out1[at, 0:rows, :] = value[0:rows]
    out1[at, rows : rows + 8, :] = value[2 * rows :]
    out2[at] = value[rows : 2 * rows]


def settle_part_kernel(pos, own, recv, out1, out2):
    rows = (own.shape[0] - 8) // 2
    value = (own[...].astype(F32) + recv[...].astype(F32)).astype(BF16)
    part_rows(value, 0, rows, out1, out2)


def part_kernel(pos, held, recv, out1, out2):
    size, rows = held.shape[0], (held.shape[1] - 8) // 2
    for i, r in enumerate((held, recv)):
        for j in range(size):
            part_rows(r[j], i * size + j, rows, out1, out2)


def pair_kernel(pos, held1, recv1, held2, recv2, out1, out2):
    for out, h, r in ((out1, held1, recv1), (out2, held2, recv2)):
        size = h.shape[0]
        out[0:size] = h[...]
        out[size:] = r[...]


def unpack_kernel(pos, *refs, count, plans, orders, small):
    blocks1, blocks2, refs = refs[:count], refs[count : 2 * count], refs[2 * count :]
    outs, scratch, sums = refs[:-2], refs[-2], refs[-1]
    rows = blocks2[0].shape[1]
    used = 0
    for plan, order, blocks in zip(plans, orders, (blocks1, blocks2)):
        place = 0
        for b in order:
            place = place * 2 + bit_of(pos, b)
        each = blocks[0].shape[0]
        for i in range(count * each):
            at = pl.multiple_of((place ^ i) * rows, 8)
            scratch[pl.ds(at, rows), :] = blocks[i // each][i % each, 0:rows, :].astype(F32)
        for start, size, flip in plan:
            block = scratch[start : start + size, :]
            outs[used][...] = block.T if flip else block
            used += 1
    total = jnp.zeros((8, 512), F32)
    for r in blocks1:
        total = total + jnp.sum(r[:, rows:, :].astype(F32), axis=0)
    sums[...] = total
    for i, (row, start, size) in enumerate(small):
        outs[used + i][...] = sums[row : row + 1, start : start + size].reshape(size)


def body(
    layer_input, segments, norm1_gain, norm1_bias, w_query, b_query, w_key, w_value, b_value,
    w_out, b_out, gate1_w, gate1_b, norm2_gain, norm2_bias, w_in, b_in, w_back, b_back,
    gate2_w, gate2_b, cotangent, *, n_dp,
):
    def hop(value, mask):
        return lax.ppermute(value, "tensor", [(i, i ^ mask) for i in range(4)])

    def dhop(value, mask):
        return lax.ppermute(value, "dp", [(i, i ^ mask) for i in range(n_dp)])

    def after(value, *deps):
        return lax.optimization_barrier((value,) + deps)[0]

    t = lax.axis_index("tensor").astype(jnp.int32)
    me = lax.axis_index("dp").astype(jnp.int32)
    tb = jnp.where(jnp.arange(8) < 4, t ^ jnp.array(LOCAL + (0,) * 4, jnp.int32), me)
    seg = segments
    x0 = layer_input
    last = [None]

    def step(kernel, outs, args, name, scratch=(), smem=1, space=VM, then=(), limit=None, cost=HEAVY):
        pos = tb if last[0] is None else after(tb, last[0], *then)
        got = call(kernel, outs, [pos] + args, smem=smem, scratch=scratch, name=name, space=space, limit=limit, cost=COSTS.get(name, cost))
        last[0] = got[0]
        return got

    x1 = hop(x0, PX)
    x2 = hop(x0, 1)
    hbm = dict(space=pl.BlockSpec(memory_space=pltpu.MemorySpace.HBM), cost=LIGHT)
    s0, e0, c0, qa0, qb0, vecs = step(
        pack_kernel,
        [sds((296, 512), BF16), sds((256, 512), BF16), sds((1416, 512), BF16), sds((256, 384), BF16),
         sds((264, 384), BF16), sds((16, 512), F32)],
        [pltpu.with_memory_space_constraint(w, pltpu.MemorySpace.HBM) for w in
         (w_in, w_back, w_out, gate1_w, gate2_w, w_query, w_key, w_value, norm1_gain, norm1_bias, b_out, gate1_b,
          norm2_gain, norm2_bias, b_back, gate2_b, b_in, b_query, b_value)],
        "pack",
        [pltpu.SemaphoreType.DMA((27,)), pltpu.VMEM((512, 128), BF16)]
        + [pltpu.VMEM((512,), BF16)] * 9 + [pltpu.VMEM((128,), BF16)] * 2, **hbm,
    )
    qkv = [qa0, qb0, hop(qa0, 1), hop(qb0, 1)]
    sy = hop(s0, PX)
    c2 = hop(c0, 1)
    na, qt0, ka, vta = step(
        chip_kernel,
        [sds((512, 512), BF16), sds((256, 256), BF16), sds((512, 256), BF16), sds((256, 512), BF16)],
        [x0, x2, vecs] + qkv, "chip", cost=LIGHT,
    )
    x3 = hop(after(x1, na), 1)
    e1 = hop(after(e0, na), PX)
    n, qt1, k, vt, p1, ot1, att1, invl1 = step(
        first_kernel,
        [
            sds((1024, 512), BF16), sds((256, 256), BF16), sds((1024, 256), BF16),
            sds((256, 1024), BF16), sds((4, 1024, 256), BF16), sds((256, 256), BF16), sds((256, 256), BF16),
            sds((4, 8, 256), F32),
        ],
        [seg, seg, x1, x3, vecs] + qkv + [na, ka, vta],
        "first", ATT_SCRATCH, 2,
    )
    attp = hop(att1, PX)
    sy = after(sy, att1)
    sx = dhop(sy, 1)
    sz = dhop(sy, 2)
    p0, ot0, att0, invl0 = step(
        second_kernel,
        [sds((4, 1024, 256), BF16), sds((256, 256), BF16), sds((256, 256), BF16), sds((4, 8, 256), F32)],
        [seg, seg, qt0, k, vt],
        "second", ATT_SCRATCH, 2,
    )
    e3 = hop(after(e1, att0), 1)
    v, kt = step(prepare_kernel, [sds((1024, 256), BF16), sds((256, 1024), BF16)], [n, k] + qkv, "prepare")
    n2, mid, branch, gate = step(
        out_kernel,
        [sds((256, 512), BF16), sds((256, 512), F32), sds((256, 512), F32), sds((256, 512), F32)],
        [x0, n, att0, attp, vecs, e0, e1, c2, e3],
        "out", [pltpu.VMEM((512, 512), BF16)],
    )
    cut_a, cut_b = step(cut_kernel, [sds((128, 512), BF16), sds((168, 512), BF16)], [sx, sz], "cut")
    sxz_a, sxz_b = dhop(cut_a, 1), dhop(cut_b, 2)
    n2p = hop(after(n2, cut_a), PX)
    quarters = [sy, hop(after(sy, cut_a), 1), sx, hop(after(sx, cut_a), 1), sz, hop(after(sz, cut_a), 1)]
    total0, hid, slope0, slope1 = step(
        ffn_first_kernel,
        [sds((256, 512), F32), sds((256, 1024), BF16), sds((256, 1024), BF16), sds((256, 768), BF16)],
        [n2, vecs, w_in, w_back, c2] + quarters,
        "ffn_first", cost=LIGHT,
    )
    sxz_a, sxz_b = lax.optimization_barrier((sxz_a, sxz_b, total0))[0:2]
    quarters = quarters + [sxz_a, hop(sxz_a, 1), sxz_b, hop(sxz_b, 1)]
    result, fg, ltg, slope2 = step(
        ffn_kernel,
        [sds((256, 512), BF16), sds((256, 512), BF16), sds((256, 512), BF16), sds((256, 256), BF16)],
        [n2, mid, cotangent, vecs, gate2_w, c2, total0] + quarters,
        "ffn", [pltpu.VMEM((512, 512), BF16)],
    )
    fgp = hop(fg, PX)
    dot0, dotp, mg, bg, log, hg, sums = step(
        back_kernel,
        [
            sds((256, 256), BF16), sds((256, 256), BF16), sds((256, 512), F32), sds((256, 512), BF16),
            sds((256, 512), BF16), sds((256, 1024), BF16), sds((8, 512), F32),
        ],
        [fg, ltg, slope0, slope1, slope2, mid, branch, gate, cotangent, vecs, e0, e1, c2, e3, gate2_w, w_in, w_back]
        + quarters,
        "back", [pltpu.VMEM((512, 512), BF16)], then=(n2p,),
    )
    dot1 = hop(dotp, PX)
    skeep, ssend = step(
        small_weight_kernel,
        [sds((776, 512), F32), sds((776, 512), BF16)],
        [n, n2, ltg, log, att0, attp, bg, sums],
        "small_weight", [pltpu.VMEM((512, 512), F32), pltpu.VMEM((512, 512), F32)],
    )
    srecv = hop(ssend, 1)
    back_scratch = [
        pltpu.VMEM((256, 256), F32), pltpu.VMEM((4, 128, 256), BF16), pltpu.VMEM((256, 256), BF16),
        pltpu.VMEM((4, 8, 256), F32),
    ]
    dk0, dv0, dq0 = step(
        back_first_kernel,
        [sds((256, 1024), F32), sds((256, 1024), F32), sds((256, 256), BF16)],
        [seg, p0, dot0, ot0, invl0, qt0, kt, v],
        "attn_back0", back_scratch, 2,
    )
    (spar,) = step(half_rows_kernel, [sds((392, 512), BF16)], [skeep, srecv], "half_rows")
    sparr = hop(spar, PX)
    bkeep, bsend, slopep = step(
        ffn_back_weight_kernel,
        [sds((512, 512), F32), sds((512, 512), BF16), sds((256, 1024), BF16)],
        [n2p, fg, fgp, hid, vecs, w_in, c2],
        "ffn_back_weight",
    )
    brecv = hop(bsend, 1)
    ikeep, isend = step(
        ffn_in_weight_kernel,
        [sds((520, 512), F32), sds((520, 512), BF16)],
        [n2, n2p, fgp, hg, slopep, w_back, c2],
        "ffn_in_weight",
    )
    irecv = hop(isend, 1)
    bits = n_dp.bit_length() - 1

    def halves(tag, parts1, parts2, rows):
        arrays = [a for parts in (parts1, parts2) for _, group in parts for a, _ in group]
        static = tuple(
            tuple((m, tuple(start for _, start in group)) for m, group in parts) for parts in (parts1, parts2)
        )
        shapes = [sds((rows // 2, 512), F32), sds((rows // 2, 512), BF16)] * 2
        o1, s1, o2, s2 = step(
            functools.partial(halves_kernel, parts=static, rows=rows, bits=(0, 1)),
            shapes, arrays, "halves_" + tag, [pltpu.VMEM((rows, 512), F32)],
        )
        return o1, dhop(s1, 1), o2, dhop(s2, 2)

    def quarter_step(tag, o1, r1, o2, r2):
        rows = o1.shape[0]
        shapes = [sds((rows // 2, 512), F32), sds((rows // 2, 512), BF16)] * 2
        o1, s1, o2, s2 = step(
            functools.partial(halves_kernel, parts=(((rows, (0, 0)),),) * 2, rows=rows, bits=(1, 0)),
            shapes, [o1, r1, o2, r2], "quarters_" + tag, [pltpu.VMEM((rows, 512), F32)],
        )
        return o1, dhop(s1, 2), o2, dhop(s2, 1)

    def merge_step(tag, o1, r1, o2, r2, small):
        rows = o1.shape[0]
        pairs = [o1, r1, o2, r2]
        for b in range(2, bits - 1):
            kernel = merge_kernel if b == 2 else both_kernel
            own, sent = step(
                functools.partial(kernel, bit=b), [sds((rows, 512), F32), sds((rows, 512), BF16)],
                pairs, "cut_" + tag, [pltpu.VMEM((rows if b == 2 else 2 * rows, 512), F32)],
            )
            pairs, rows = [own, dhop(sent, 1 << b)], rows // 2
        static = tuple((f, m, tuple(start for _, start in group)) for f, m, group in small)
        arrays = [a for _, _, group in small for a, _ in group]
        own = step(
            functools.partial(round_kernel, count=len(pairs), small=static), [sds((2 * rows + 8, 512), BF16)],
            pairs + arrays, "merge_" + tag,
        )[0]
        return own, dhop(own, 1 << (bits - 1))

    def part_step(tag, own, recv):
        rows = (own.shape[0] - 8) // 2
        if bits > 3:
            held = step(settle_kernel, [sds(own.shape, BF16)], [own, recv], "settle")[0][None]
            for b in range(bits - 2, 2, -1):
                shape = (2 * held.shape[0],) + held.shape[1:]
                held = step(stack_kernel, [sds(shape, BF16)], [held, dhop(held, 1 << b)], "stack")[0]
            size = 2 * held.shape[0]
            kernel, args = part_kernel, [held, dhop(held, 4)]
        else:
            size, kernel, args = 1, settle_part_kernel, [own, recv]
        h1, h2 = step(kernel, [sds((size, rows + 8, 512), BF16), sds((size, rows, 512), BF16)], args, "part_" + tag)
        if tag in AHEAD:
            far1, far2 = dhop(h1, 1), dhop(h2, 2)
            r1, r2 = dhop(h1, 2), dhop(h2, 1)
            return h1, r1, far1, h2, r2, far2
        return h1, dhop(h1, 2), h2, dhop(h2, 1)

    def pair_step(tag, h1, r1, h2, r2):
        shapes = [sds((2 * h.shape[0],) + h.shape[1:], BF16) for h in (h1, h2)]
        h1, h2 = step(pair_kernel, shapes, [h1, r1, h2, r2], "pair_" + tag)
        return h1, dhop(h1, 1), h2, dhop(h2, 2)

    def unpack_step(tag, blocks, plans, small):
        shapes = [sds((512, size) if flip else (size, 512), F32) for plan in plans for _, size, flip in plan]
        rest = tuple(range(2, bits - 1))
        half = len(blocks) // 2
        rows = half * blocks[half].shape[0] * blocks[half].shape[1]
        return step(
            functools.partial(
                unpack_kernel, count=half, plans=plans, orders=((0, 1) + rest, (1, 0) + rest), small=small
            ),
            shapes + [sds((size,), F32) for _, _, size in small], list(blocks), "unpack_" + tag,
            [pltpu.VMEM((rows, 512), F32), pltpu.VMEM((8, 512), F32)],
        )

    f = halves("f", [(512, [(bkeep, 0), (brecv, 0)])], [(512, [(ikeep, 0), (irecv, 0)])], padded(512, n_dp))

    dqt, dkt, dvt, akeep, asend = step(
        back_second_kernel,
        [
            sds((256, 512), BF16), sds((256, 1024), BF16), sds((256, 1024), BF16), sds((392, 512), F32),
            sds((392, 512), BF16),
        ],
        [seg, p1, dot1, ot1, invl1, qt1, kt, v, dk0, dv0, dq0, n],
        "attn_back1", [pltpu.VMEM((256, 1024), F32), pltpu.VMEM((256, 1024), F32)] + back_scratch, 2,
    )
    arecv = hop(asend, 1)
    gown, gpar, gsend = step(
        input_kernel,
        [sds((512, 256), F32), sds((512, 256), F32), sds((512, 512), BF16)],
        [dqt, dkt, dvt] + qkv,
        "input_grad",
    )
    gsib = hop(gsend, 1)
    f = quarter_step("f", *f)
    a = halves(
        "a", [(384, [(akeep, 0), (arecv, 0)])], [(384, [(skeep, 0), (srecv, 0), (sparr, 0)])], padded(384, n_dp)
    )
    (gsum,) = step(half_columns_kernel, [sds((512, 256), BF16)], [gpar, gsib], "half_columns")
    gp = hop(gsum, PX)
    tail = [(skeep, 773), (srecv, 773), (sparr, 389)]
    f = merge_step("f", *f, [(0, 1, [(ikeep, 512), (irecv, 512)]), (1, 1, tail)])
    a = quarter_step("a", *a)
    input_grad, sums1 = step(
        last_kernel,
        [sds((256, 512), F32), sds((8, 512), F32)],
        [gown, gsib, gp, x0, mg, log, vecs, e0, e1, c2, e3],
        "last", [pltpu.VMEM((512, 512), BF16)],
    )
    sums1_b = hop(sums1, PX)
    sums1_a = hop(sums1, 1)
    sums1_c = hop(sums1, PX ^ 1)
    group = [(skeep, 768), (srecv, 768), (sparr, 384)]
    a = merge_step(
        "a", *a,
        [(0, 2, [(sums1, 0), (sums1_a, 0), (sums1_b, 0), (sums1_c, 0)]), (2, 1, [(akeep, 384), (arecv, 384)]),
         (3, 5, group)],
    )
    f = part_step("f", *f)
    h1, r1, far1, h2, r2, far2 = f
    f = [h1, r1, far1, dhop(r1, 1), h2, r2, far2, dhop(r2, 2)]
    a = part_step("a", *a)
    if "a" in AHEAD:
        h1, r1, far1, h2, r2, far2 = a
        a = [h1, r1, far1, dhop(r1, 1), h2, r2, far2, dhop(r2, 2)]
    else:
        a = pair_step("a", *a)
    g_wback, g_win, d_b_in, d_n2b = unpack_step(
        "f", f, (((0, 512, False),), ((0, 512, False),)), ((0, 0, 512), (1, 0, 512))
    )
    plans = (
        ((0, 128, True), (128, 128, True), (256, 128, True)),
        ((0, 128, False), (128, 128, False), (256, 128, False)),
    )
    small = ((0, 0, 512), (1, 0, 512), (2, 0, 128), (2, 128, 128)) + tuple((i, 0, 512) for i in range(3, 8))
    g_q, g_k, g_v, g_g2, g_g1, g_wo, d_n1g, d_n1b, d_bq, d_bv, d_b_back, d_g2b, d_b_out, d_g1b, d_n2g = unpack_step(
        "a", a, plans, small
    )
    return (
        result, input_grad, d_n1g, d_n1b, g_q, d_bq, g_k, g_v, d_bv, g_wo, d_b_out, g_g1, d_g1b, d_n2g, d_n2b,
        g_win, d_b_in, g_wback, d_b_back, g_g2, d_g2b,
    )


def solution(mesh):
    tok = P(("dp", "tensor"), None)
    col = P(None, "tensor")
    row = P("tensor", None)
    vec = P("tensor")
    rep = P()
    return jax.shard_map(
        functools.partial(body, n_dp=mesh.shape["dp"]),
        mesh=mesh,
        in_specs=(
            tok, P("dp", None), rep, rep, col, vec, col, col, vec, row, rep, row, rep, rep, rep,
            col, vec, row, rep, row, rep, tok,
        ),
        out_specs=(
            tok, tok, rep, rep, col, vec, col, col, vec, row, rep, row, rep, rep, rep,
            col, vec, row, rep, row, rep,
        ),
        check_vma=False,
    )
```

```python
import functools
import math

import jax
import jax.numpy as jnp
from jax import lax
from jax.experimental import pallas as pl
from jax.experimental.pallas import tpu as pltpu
from jax.sharding import PartitionSpec as P

HD = 64
EPSILON = 1e-05
F32 = jnp.float32
BF16 = jnp.bfloat16
NEG = -1e30
PX = 2
LOCAL = (0, PX, 1, 1 ^ PX)
SPARE = 4 * 1024 * 1024
HEAVY = 10**10
LIGHT = 0
AHEAD = ("a", "f")
COSTS = {"halves_f": 0, "halves_a": 0, "input_grad": 0, "part_f": 0, "merge_a": 0, "last": 0, "first": 0, "ffn": 0, "part_a": 0, "unpack_f": 2*10**10}


def nn(a, b):
    return lax.dot_general(a, b, (((1,), (0,)), ((), ())), preferred_element_type=F32)


def nt(a, b):
    return lax.dot_general(a, b, (((1,), (1,)), ((), ())), preferred_element_type=F32)


def tn(a, b):
    return lax.dot_general(a, b, (((0,), (0,)), ((), ())), preferred_element_type=F32)


VM = pl.BlockSpec(memory_space=pltpu.VMEM)
SM = pl.BlockSpec(memory_space=pltpu.SMEM)


def call(body, outs, args, smem=0, scratch=(), name=None, space=VM, limit=None, cost=0):
    nbytes = sum(a.size * a.dtype.itemsize for a in args) + sum(o.size * o.dtype.itemsize for o in outs)
    held = sum(math.prod(s.shape) * 4 for s in scratch)
    limit = limit or nbytes + held + SPARE
    return pl.pallas_call(
        body,
        out_shape=tuple(outs),
        in_specs=[SM] * smem + [space] * (len(args) - smem),
        out_specs=tuple([VM] * len(outs)),
        scratch_shapes=list(scratch),
        compiler_params=pltpu.CompilerParams(vmem_limit_bytes=limit),
        cost_estimate=pl.CostEstimate(flops=cost, bytes_accessed=0, transcendentals=0),
        name=name,
    )(*args)


def sds(shape, dtype):
    return jax.ShapeDtypeStruct(shape, dtype)


def norm_unit(values):
    centred = values - jnp.mean(values, axis=-1, keepdims=True)
    spread = jnp.mean(centred * centred, axis=-1, keepdims=True)
    inverse = lax.rsqrt(spread + EPSILON)
    return centred * inverse, inverse


def sigmoid(v):
    return 1.0 / (1.0 + jnp.exp(-v))


C0 = 0.7978845608028654
C1 = 0.044715


def gelu_parts(u):
    square = u * u
    t = jnp.tanh(C0 * u * (1.0 + C1 * square))
    half = 0.5 * (1.0 + t)
    value = u * half
    slope = half + (0.5 * C0) * u * (1.0 - t * t) * (1.0 + (3.0 * C1) * square)
    return value, slope


def attend_query_block(qb, tb, segs, segv, qz, k, vt, p_ref, ot_ref, invl_ref, s_sc, m_sc, l_sc, o_sc, segc):
    rows = 256
    tq = tb[qb]
    m_sc[...] = jnp.full(m_sc.shape, NEG, F32)
    l_sc[...] = jnp.zeros(l_sc.shape, F32)
    o_sc[...] = jnp.zeros(o_sc.shape, F32)
    seg_q = segv[0:1, pl.ds(pl.multiple_of(tq * rows, rows), rows)].astype(F32)

    def active(kb):
        tk = tb[kb]
        return (tk <= tq) & (segs[0, tk * rows + rows - 1] >= segs[0, tq * rows])

    @pl.loop(0, 4)
    def _(kb):
        @pl.when(active(kb))
        def _():
            tk = tb[kb]
            krows = pl.ds(pl.multiple_of(kb * rows, rows), rows)
            kpos = tk * rows + lax.broadcasted_iota(jnp.int32, (rows, rows), 0)
            qpos = tq * rows + lax.broadcasted_iota(jnp.int32, (rows, rows), 1)
            seg_k = segc[pl.ds(pl.multiple_of(tk * rows, rows), rows), 0:1]
            bias = jnp.where((kpos <= qpos) & (seg_k == seg_q), 0.0, NEG)
            for h in range(4):
                pair = 128 * (h // 2)
                s = nn(k[krows, pair : pair + 128], qz[h]) + bias
                s_sc[h, krows, :] = s
                m_sc[h] = jnp.maximum(m_sc[h], jnp.max(s.reshape(rows // 8, 8, rows), axis=0))

    for h in range(4):
        m_sc[h] = jnp.broadcast_to(jnp.max(m_sc[h], axis=0, keepdims=True), (8, rows))

    @pl.loop(0, 4)
    def _(kb):
        @pl.when(active(kb))
        def _():
            krows = pl.ds(pl.multiple_of(kb * rows, rows), rows)
            for h in range(4):
                e = jnp.exp(s_sc[h, krows, :] - m_sc[h, 0:1, :])
                l_sc[h] = l_sc[h] + jnp.sum(e.reshape(rows // 8, 8, rows), axis=0)
                pb = e.astype(BF16)
                p_ref[h, krows, :] = pb
                o_sc[h] = o_sc[h] + nn(vt[64 * h : 64 * h + 64, krows], pb)

    for h in range(4):
        invl = 1.0 / jnp.sum(l_sc[h], axis=0, keepdims=True)
        invl_ref[h] = jnp.broadcast_to(invl, (8, rows))
        ot_ref[64 * h : 64 * h + 64, :] = (o_sc[h] * invl).astype(BF16)


def fill_qz(qz, qt):
    zero = jnp.zeros((64, 256), BF16)
    for h in range(4):
        mine = qt[64 * h : 64 * h + 64, :]
        qz[h] = jnp.concatenate([mine, zero] if h % 2 == 0 else [zero, mine], axis=0)


def fill_segc(segc, segv):
    for t in range(4):
        row = jnp.broadcast_to(segv[0:1, 256 * t : 256 * t + 256].astype(F32), (128, 256))
        segc[256 * t : 256 * t + 256, :] = row.T


def weight_of(w, part):
    cols = slice(128 * part, 128 * part + 128)
    return jnp.concatenate([w[0][:, cols], w[1][0:256, cols]], axis=0)


def bias_of(w, part):
    return w[1][256:257, 128 * part : 128 * part + 128].astype(F32)


def project(n, w, c, k_ref, vt_ref, blocks):
    cols = slice(128 * c, 128 * c + 128)
    k = nn(n, weight_of(w, 1)).astype(BF16)
    vt = (nn(n, weight_of(w, 2)) + bias_of(w, 2)).T.astype(BF16)
    for i, at in enumerate(blocks):
        k_ref[at : at + 256, cols] = k[256 * i : 256 * i + 256]
        vt_ref[cols, at : at + 256] = vt[:, 256 * i : 256 * i + 256]


def query_of(n, w):
    q = nn(n, weight_of(w, 0)) + bias_of(w, 0)
    return (q.astype(BF16).astype(F32) * HD ** (-0.5)).T.astype(BF16)


def chip_kernel(pos, x0, x2, vecs, qa0, qb0, qa1, qb1, n_ref, qt_ref, k_ref, vt_ref):
    for i, x in enumerate((x0, x2)):
        unit, _ = norm_unit(x[...].astype(F32))
        n_ref[256 * i : 256 * i + 256, :] = (unit * vecs[0:1, :] + vecs[1:2, :]).astype(BF16)
    n = n_ref[...]
    for c, w in enumerate(((qa0, qb0), (qa1, qb1))):
        qt_ref[128 * c : 128 * c + 128, :] = query_of(n[0:256], w)
        project(n, w, c, k_ref, vt_ref, (0, 256))


def first_kernel(
    tb, segs, segv, x1, x3, vecs, qa0, qb0, qa1, qb1, na, ka, vta,
    n_ref, qt1_ref, k_ref, vt_ref, p_ref, ot_ref, att_ref, invl_ref,
    qz, s_sc, m_sc, l_sc, o_sc, segc,
):
    for i, x in enumerate((x1, x3)):
        unit, _ = norm_unit(x[...].astype(F32))
        n_ref[512 * i + 256 : 512 * i + 512, :] = (unit * vecs[0:1, :] + vecs[1:2, :]).astype(BF16)
    n = jnp.concatenate([n_ref[256:512, :], n_ref[768:1024, :]], axis=0)
    for c, w in enumerate(((qa0, qb0), (qa1, qb1))):
        qt1_ref[128 * c : 128 * c + 128, :] = query_of(n[0:256], w)
        project(n, w, c, k_ref, vt_ref, (256, 768))
    for i in range(2):
        src, dst = slice(256 * i, 256 * i + 256), slice(512 * i, 512 * i + 256)
        n_ref[dst, :] = na[src, :]
        k_ref[dst, :] = ka[src, :]
        vt_ref[:, dst] = vta[:, src]
    fill_segc(segc, segv)
    fill_qz(qz, qt1_ref)
    attend_query_block(1, tb, segs, segv, qz, k_ref, vt_ref, p_ref, ot_ref, invl_ref, s_sc, m_sc, l_sc, o_sc, segc)
    att_ref[...] = ot_ref[...].astype(F32).T.astype(BF16)


def second_kernel(
    tb, segs, segv, qt0, k, vt,
    p_ref, ot_ref, att_ref, invl_ref,
    qz, s_sc, m_sc, l_sc, o_sc, segc,
):
    fill_segc(segc, segv)
    fill_qz(qz, qt0)
    attend_query_block(0, tb, segs, segv, qz, k, vt, p_ref, ot_ref, invl_ref, s_sc, m_sc, l_sc, o_sc, segc)
    att_ref[...] = ot_ref[...].astype(F32).T.astype(BF16)


ATT_SCRATCH = (
    pltpu.VMEM((4, 128, 256), BF16),
    pltpu.VMEM((4, 1024, 256), F32),
    pltpu.VMEM((4, 8, 256), F32),
    pltpu.VMEM((4, 8, 256), F32),
    pltpu.VMEM((4, 64, 256), F32),
    pltpu.VMEM((1024, 128), F32),
)


def gather_gate(tb, pieces, start, scratch):
    for i, piece in enumerate(pieces):
        scratch[pl.ds(pl.multiple_of(tb[i] * 128, 128), 128), :] = piece[start : start + 128, :]


def gather_gate_two(pos, g2, c2, pieces, scratch):
    scratch[pl.ds(pl.multiple_of(pos[0] * 128, 128), 128), :] = g2[...]
    scratch[pl.ds(pl.multiple_of(pos[2] * 128, 128), 128), :] = c2[256:384, :]
    for i, piece in enumerate(pieces):
        quarter = (pos[4] ^ (i // 2)) & 3
        at = pos[1 + 2 * (i % 2)] * 128 + quarter * 32
        rows = piece.shape[0]
        scratch[pl.ds(pl.multiple_of(at, 32), 32), :] = piece[rows - 32 : rows, :]


def out_kernel(
    tb, x0, n, att, attp, vecs, e0, e1, e2, e3,
    n2_ref, mid_ref, branch_ref, gate_ref,
    gw,
):
    gather_gate(tb, (e0, e1, e2, e3), 128, gw)
    branch = nn(att[:, 0:128], e0[0:128, :]) + nn(att[:, 128:256], e2[0:128, :])
    branch = branch + nn(attp[:, 0:128], e1[0:128, :]) + nn(attp[:, 128:256], e3[0:128, :])
    branch = branch + vecs[2:3, :]
    gate = sigmoid(nn(n[0:256, :], gw[...]) + vecs[3:4, :])
    middle = x0[...].astype(F32) + gate * branch
    unit, _ = norm_unit(middle)
    n2_ref[...] = (unit * vecs[4:5, :] + vecs[5:6, :]).astype(BF16)
    mid_ref[...] = middle
    branch_ref[...] = branch
    gate_ref[...] = gate


def pair_up(a, b, start):
    return jnp.concatenate([a[start : start + 128, :], b[start : start + 128, :]], axis=0)


def pair_bias(a, b, row=256):
    return jnp.concatenate([a[row : row + 1, 0:128], b[row : row + 1, 0:128]], axis=1).astype(F32)


def cut_kernel(pos, sx, sz, a_ref, b_ref):
    a_ref[...] = sz[0:128, :]
    b_ref[...] = sx[128:296, :]


def ffn_first_kernel(
    tb, n2, vecs, win0, wback0, c2, s0, s1, s2, s3, s4, s5,
    total_ref, hid_ref, slope_ref, slope1_ref,
):
    n2v = n2[...]
    total = jnp.zeros((256, 512), F32)
    for i, (b, w, wb) in enumerate(((vecs[8:9, :], win0[...], wback0[...]), (c2[384:385, :], c2[392:904, :], c2[904:1416, :]))):
        value, slope = gelu_parts(nn(n2v, w) + b.astype(F32))
        value = value.astype(BF16)
        hid_ref[:, 512 * i : 512 * i + 512] = value
        slope_ref[:, 512 * i : 512 * i + 512] = slope.astype(BF16)
        total = total + nn(value, wb)
    for i, (a, b) in enumerate(((s0, s1), (s2, s3), (s4, s5))):
        value, slope = gelu_parts(nt(n2v, pair_up(a, b, 0)) + pair_bias(a, b))
        slope1_ref[:, 256 * i : 256 * i + 256] = slope.astype(BF16)
        total = total + nn(value.astype(BF16), pair_up(a, b, 128))
    total_ref[...] = total


def ffn_kernel(
    tb, n2, mid, ct, vecs, g2, c2, total0, s0, s1, s2, s3, s4, s5, a6, a7, b6, b7,
    out_ref, fg_ref, ltg_ref, slope_ref, gw,
):
    gather_gate_two(tb, g2, c2, (s0, s1, s2, s3, s4, s5, b6, b7), gw)
    n2v = n2[...]
    value, slope = gelu_parts(nt(n2v, pair_up(a6, a7, 0)) + pair_bias(b6, b7, 128))
    slope_ref[...] = slope.astype(BF16)
    ffn = total0[...] + nn(value.astype(BF16), pair_up(b6, b7, 0)) + vecs[6:7, :]
    gate = sigmoid(nn(n2v, gw[...]) + vecs[7:8, :])
    up = ct[...].astype(F32)
    out_ref[...] = (mid[...] + gate * ffn).astype(BF16)
    fg_ref[...] = (gate * up).astype(BF16)
    ltg_ref[...] = (up * ffn * (gate * (1.0 - gate))).astype(BF16)


def back_kernel(
    tb, fg, ltg, slope0, slope1, slope2, mid, branch, gate, ct, vecs, e0, e1, e2, e3, g2,
    win0, wback0, s0, s1, s2, s3, s4, s5, a6, a7, b6, b7,
    dot_ref, dotp_ref, mg_ref, bg_ref, log_ref, hg_ref, sums_ref,
    gw,
):
    gather_gate_two(tb, g2, e2, (s0, s1, s2, s3, s4, s5, b6, b7), gw)
    fgv = fg[...]
    ltgv = ltg[...]
    ng = nt(ltgv, gw[...])
    for i, (w, wb) in enumerate(((win0[...], wback0[...]), (e2[392:904, :], e2[904:1416, :]))):
        hg = (nt(fgv, wb) * slope0[:, 512 * i : 512 * i + 512].astype(F32)).astype(BF16)
        hg_ref[:, 512 * i : 512 * i + 512] = hg
        ng = ng + nt(hg, w)
    for i, (a, b) in enumerate(((s0, s1), (s2, s3), (s4, s5))):
        part = slope1[:, 256 * i : 256 * i + 256]
        hg = (nt(fgv, pair_up(a, b, 128)) * part.astype(F32)).astype(BF16)
        ng = ng + nn(hg, pair_up(a, b, 0))
    hg = (nt(fgv, pair_up(b6, b7, 0)) * slope2[...].astype(F32)).astype(BF16)
    ng = ng + nn(hg, pair_up(a6, a7, 0))
    unit, inverse = norm_unit(mid[...])
    g = ng * vecs[4:5, :]
    back = inverse * (g - jnp.mean(g, axis=-1, keepdims=True) - unit * jnp.mean(g * unit, axis=-1, keepdims=True))
    mg = ct[...].astype(F32) + back
    mg_ref[...] = mg
    gatev = gate[...]
    bg = (gatev * mg).astype(BF16)
    log = (mg * branch[...] * (gatev * (1.0 - gatev))).astype(BF16)
    bg_ref[...] = bg
    log_ref[...] = log
    dot_ref[0:128, :] = nt(e0[0:128, :], bg).astype(BF16)
    dot_ref[128:256, :] = nt(e2[0:128, :], bg).astype(BF16)
    dotp_ref[0:128, :] = nt(e1[0:128, :], bg).astype(BF16)
    dotp_ref[128:256, :] = nt(e3[0:128, :], bg).astype(BF16)
    rows = [fgv.astype(F32), ltgv.astype(F32), bg.astype(F32), log.astype(F32), ng * unit, ng]
    sums_ref[...] = jnp.zeros((8, 512), F32)
    for i, r in enumerate(rows):
        sums_ref[i : i + 1, :] = jnp.sum(r, axis=0, keepdims=True)


def ffn_back_weight_kernel(
    tb, n2p, fg, fgp, hid, vecs, win0, c2, keep, recv,
    keep_ref, send_ref, slope_ref, par_ref,
):
    par_ref[...] = (keep[384:, :] + recv[384:, :].astype(F32)).astype(BF16)
    fgv, fgpv, n2pv = fg[...], fgp[...], n2p[...]
    for i, (b, w) in enumerate(((vecs[8:9, :], win0[...]), (c2[384:385, :], c2[392:904, :]))):
        cols = slice(512 * i, 512 * i + 512)
        value, slope = gelu_parts(nn(n2pv, w) + b.astype(F32))
        slope_ref[:, cols] = slope.astype(BF16)
        wback = tn(hid[:, cols], fgv) + tn(value.astype(BF16), fgpv)
        dst = keep_ref if i == 0 else send_ref
        dst[...] = wback.astype(dst.dtype)


def ffn_in_weight_kernel(
    tb, n2, n2p, fgp, hg, slope, wback0, c2,
    keep_ref, send_ref,
):
    n2v, n2pv, fgpv = n2[...], n2p[...], fgp[...]
    for i, wb in enumerate((wback0[...], c2[904:1416, :])):
        cols = slice(512 * i, 512 * i + 512)
        hgp = (nt(fgpv, wb) * slope[:, cols].astype(F32)).astype(BF16)
        hgo = hg[:, cols]
        win = tn(n2v, hgo) + tn(n2pv, hgp)
        bias = jnp.sum(hgo.astype(F32), axis=0, keepdims=True) + jnp.sum(hgp.astype(F32), axis=0, keepdims=True)
        dst = keep_ref if i == 0 else send_ref
        dst[0:512, :] = win.astype(dst.dtype)
        dst[512:520, :] = jnp.broadcast_to(bias, (8, 512)).astype(dst.dtype)


def small_weight_kernel(
    tb, n, n2, ltg, log, att, attp, bg, sums, e0, e1, e2, e3,
    keep_ref, send_ref, gate_ref,
    g1, g2, gw,
):
    gather_gate(tb, (e0, e1, e2, e3), 128, gw)
    gate_ref[...] = nt(log[...], gw[...])
    keep_ref[768:776, :] = sums[...]
    send_ref[768:776, :] = sums[...].astype(BF16)
    g2[...] = tn(n2[...], ltg[...])
    g1[...] = tn(n[0:256, :], log[...])
    bgv = bg[...]
    wo = (tn(att[:, 0:128], bgv), tn(attp[:, 0:128], bgv), tn(att[:, 128:256], bgv), tn(attp[:, 128:256], bgv))
    for i in range(4):
        src = pl.ds(pl.multiple_of(tb[i] * 128, 128), 128)
        dst = keep_ref if i < 2 else send_ref
        base = 384 * (i % 2)
        dst[base : base + 128, :] = g2[src, :].astype(dst.dtype)
        dst[base + 128 : base + 256, :] = g1[src, :].astype(dst.dtype)
        dst[base + 256 : base + 384, :] = wo[i].astype(dst.dtype)


def prepare_kernel(tb, n, k, qa0, qb0, qa1, qb1, v_ref, kt_ref):
    nv = n[...]
    for c, w in enumerate(((qa0, qb0), (qa1, qb1))):
        v = nn(nv, weight_of(w, 2)) + bias_of(w, 2)
        v_ref[:, 128 * c : 128 * c + 128] = v.astype(BF16)
    kt_ref[...] = k[...].astype(F32).T.astype(BF16)


def attend_back(qb, tb, segs, p, dot, ot, invl, qt, kt, v, dk, dv, dq, doz, dos, dlt):
    rows = 256
    tq = tb[qb]
    zero = jnp.zeros((64, rows), BF16)
    for h in range(4):
        hs = slice(64 * h, 64 * h + 64)
        scale = invl[h, 0:1, :]
        dv_h = dot[hs, :].astype(F32)
        delta = jnp.sum(dv_h * ot[hs, :].astype(F32), axis=0, keepdims=True) * scale
        dlt[h] = jnp.broadcast_to(delta, (8, rows))
        mine = (dv_h * scale).astype(BF16)
        dos[hs, :] = mine
        doz[h] = jnp.concatenate([mine, zero] if h % 2 == 0 else [zero, mine], axis=0)
    dq[...] = jnp.zeros(dq.shape, F32)

    @pl.loop(0, 4)
    def _(kb):
        tk = tb[kb]

        @pl.when((tk <= tq) & (segs[0, tk * rows + rows - 1] >= segs[0, tq * rows]))
        def _():
            ks = pl.ds(pl.multiple_of(kb * rows, rows), rows)
            for h in range(4):
                pair = 128 * (h // 2)
                hs = slice(64 * h, 64 * h + 64)
                ph = p[h, ks, :]
                dp = nn(v[ks, pair : pair + 128], doz[h])
                ds = (ph.astype(F32) * (dp - dlt[h, 0:1, :])).astype(BF16)
                dv[hs, ks] = dv[hs, ks] + nt(dos[hs, :], ph)
                dk[hs, ks] = dk[hs, ks] + nt(qt[hs, :], ds)
                dq[hs, :] = dq[hs, :] + nn(kt[hs, ks], ds)


def back_first_kernel(
    tb, segs, p, dot, ot, invl, qt, kt, v,
    dk_ref, dv_ref, dq_ref,
    dq, doz, dos, dlt,
):
    dk_ref[...] = jnp.zeros(dk_ref.shape, F32)
    dv_ref[...] = jnp.zeros(dv_ref.shape, F32)
    attend_back(0, tb, segs, p, dot, ot, invl, qt, kt, v, dk_ref, dv_ref, dq, doz, dos, dlt)
    dq_ref[...] = (dq[...] * HD ** (-0.5)).astype(BF16)


def back_second_kernel(
    tb, segs, p, dot, ot, invl, qt, kt, v, dk0, dv0, dq0, n,
    dqt_ref, dkt_ref, dvt_ref, keep_ref, send_ref,
    dk, dv, dq, doz, dos, dlt,
):
    dk[...] = dk0[...]
    dv[...] = dv0[...]
    attend_back(1, tb, segs, p, dot, ot, invl, qt, kt, v, dk, dv, dq, doz, dos, dlt)
    dqt_ref[:, 0:256] = dq0[...]
    dqt_ref[:, 256:512] = (dq[...] * HD ** (-0.5)).astype(BF16)
    dkt_ref[...] = dk[...].astype(BF16)
    dvt_ref[...] = dv[...].astype(BF16)
    nv = n[...]
    wq = nn(dqt_ref[...], nv[0:512, :])
    wk = nn(dkt_ref[...], nv)
    wv = nn(dvt_ref[...], nv)
    for i, w in enumerate((wq, wk, wv)):
        keep_ref[128 * i : 128 * i + 128, :] = w[0:128, :]
        send_ref[128 * i : 128 * i + 128, :] = w[128:256, :].astype(BF16)
    ones_q = jnp.ones((8, 512), BF16)
    ones_v = jnp.ones((8, 1024), BF16)
    bq = nt(ones_q, dqt_ref[...])
    bv = nt(ones_v, dvt_ref[...])
    empty = jnp.zeros((8, 256), F32)
    keep_ref[384:392, :] = jnp.concatenate([bq[:, 0:128], bv[:, 0:128], empty], axis=1)
    send_ref[384:392, :] = jnp.concatenate([bq[:, 128:256], bv[:, 128:256], empty], axis=1).astype(BF16)


def input_kernel(tb, dqt, dkt, dvt, qa0, qb0, qa1, qb1, own_ref, par_ref, send_ref):
    def weight(part):
        return jnp.concatenate([weight_of((qa0, qb0), part), weight_of((qa1, qb1), part)], axis=1)

    wk, wv = weight(1), weight(2)
    g = nn(wk, dkt[...]) + nn(wv, dvt[...])
    send_ref[...] = g[:, 512:1024].astype(BF16)
    g0 = g[:, 0:512] + nn(weight(0), dqt[...])
    own_ref[...] = g0[:, 0:256]
    par_ref[...] = g0[:, 256:512]


def last_kernel(tb, own, sib, par, x0, mg, gate_part, vecs, grad_ref, sums_ref):
    total = own[...] + sib[:, 0:256].astype(F32) + par[...].astype(F32)
    ng = total.T + gate_part[...]
    unit, inverse = norm_unit(x0[...].astype(F32))
    g = ng * vecs[0:1, :]
    back = inverse * (g - jnp.mean(g, axis=-1, keepdims=True) - unit * jnp.mean(g * unit, axis=-1, keepdims=True))
    grad_ref[...] = mg[...] + back
    sums_ref[...] = jnp.zeros((8, 512), F32)
    sums_ref[0:1, :] = jnp.sum(ng * unit, axis=0, keepdims=True)
    sums_ref[1:2, :] = jnp.sum(ng, axis=0, keepdims=True)


def run_copies(moves, sems):
    copies = [pltpu.make_async_copy(src, dst, sems.at[i]) for i, (src, dst) in enumerate(moves)]
    for copy in copies:
        copy.start()
    for copy in copies:
        copy.wait()


def pack_kernel(pos, w_in, w_back, w_out, g1, g2, wq, wk, wv, *refs):
    vectors, (s_ref, e_ref, c_ref, qa_ref, qb_ref, vecs), (sems, cut, *lines) = refs[:11], refs[11:17], refs[17:]
    start = pl.multiple_of((pos[4] & 3) * 128, 128)
    gate = pl.multiple_of((pos[4] & 3) * 32, 32)
    moves = [
        (w_in.at[:, pl.ds(start, 128)], cut),
        (w_back.at[pl.ds(start, 128), :], s_ref.at[128:256, :]),
        (g2.at[pl.ds(gate, 32), :], s_ref.at[264:296, :]),
    ]
    for i, w in enumerate((wq, wk, wv)):
        cols = slice(128 * i, 128 * i + 128)
        moves.append((w.at[0:256, :], qa_ref.at[:, cols]))
        moves.append((w.at[256:512, :], qb_ref.at[0:256, cols]))
    late = [
        (w_out, e_ref.at[0:128, :]),
        (g1, e_ref.at[128:256, :]),
        (w_out, c_ref.at[0:128, :]),
        (g1, c_ref.at[128:256, :]),
        (g2, c_ref.at[256:384, :]),
        (w_in, c_ref.at[392:904, :]),
        (w_back, c_ref.at[904:1416, :]),
    ]
    moves = moves + list(zip(vectors, lines)) + late
    copies = [pltpu.make_async_copy(src, dst, sems.at[i]) for i, (src, dst) in enumerate(moves)]
    for copy in copies:
        copy.start()
    for copy in copies[: len(moves) - len(late)]:
        copy.wait()
    for i, v in enumerate(lines[:9]):
        vecs[i : i + 1, :] = v[...].astype(F32).reshape(1, 512)
    bq = lines[9][...].astype(F32).reshape(1, 128)
    bv = lines[10][...].astype(F32).reshape(1, 128)
    vecs[9:16, :] = jnp.zeros((7, 512), F32)
    s_ref[0:128, :] = cut[...].astype(F32).T.astype(BF16)
    bias = vecs[8:9, pl.ds(start, 128)]
    s_ref[256:264, :] = jnp.broadcast_to(jnp.concatenate([bias] * 4, axis=1), (8, 512)).astype(BF16)
    c_ref[384:392, :] = jnp.broadcast_to(vecs[8:9, :], (8, 512)).astype(BF16)
    for i, bias in enumerate((bq, jnp.zeros_like(bq), bv)):
        qb_ref[256:264, 128 * i : 128 * i + 128] = jnp.broadcast_to(bias, (8, 128)).astype(BF16)
    for copy in copies[len(moves) - len(late) :]:
        copy.wait()


def half_columns_kernel(tb, keep, recv, out_ref):
    half = keep.shape[1]
    out_ref[...] = (keep[...] + recv[:, half:].astype(F32)).astype(BF16)


def padded(rows, n_dp):
    unit = 8 * n_dp
    return -(-rows // unit) * unit


def bit_of(pos, b):
    return (pos[4] >> b) & 1


def sum_into(dst, at, addends, rows):
    value = None
    for ref, start in addends:
        block = ref[start : start + rows, :].astype(F32)
        value = block if value is None else value + block
    dst[at : at + rows, :] = value


def cut_rows(total, at, rows, bit, own, own_at, send, send_at):
    half = rows // 2
    mine = pl.multiple_of(at + bit * half, 8)
    other = pl.multiple_of(at + (1 - bit) * half, 8)
    own[own_at : own_at + half, :] = total[pl.ds(mine, half), :]
    send[send_at : send_at + half, :] = total[pl.ds(other, half), :].astype(BF16)


def pick(refs, groups):
    it = iter(refs)
    return [(rows, [(next(it), start) for start in starts]) for rows, starts in groups]


def halves_kernel(pos, *refs, parts, rows, bits):
    count = sum(len(starts) for groups in parts for _, starts in groups)
    ins, (own1, send1, own2, send2, total) = refs[:count], refs[count:]
    used = 0
    for groups, bit, own, send in zip(parts, bits, (own1, own2), (send1, send2)):
        need = sum(len(starts) for _, starts in groups)
        at = 0
        for size, addends in pick(ins[used : used + need], groups):
            sum_into(total, at, addends, size)
            at += size
        used += need
        if at < rows:
            total[at:, :] = jnp.zeros((rows - at, 512), F32)
        cut_rows(total, 0, rows, bit_of(pos, bit), own, 0, send, 0)


def merge_kernel(pos, own1, recv1, own2, recv2, own, send, total, *, bit):
    rows = own1.shape[0]
    for i, (o, r) in enumerate(((own1, recv1), (own2, recv2))):
        total[...] = o[...] + r[...].astype(F32)
        cut_rows(total, 0, rows, bit_of(pos, bit), own, i * rows // 2, send, i * rows // 2)


def round_kernel(pos, *refs, count, small):
    out = refs[-1]
    at = 0
    for i in range(0, count, 2):
        rows = refs[i].shape[0]
        out[at : at + rows, :] = (refs[i][...] + refs[i + 1][...].astype(F32)).astype(BF16)
        at += rows
    out[at : at + 8, :] = jnp.zeros((8, 512), BF16)
    used = count
    for first, size, starts in small:
        value = None
        for ref, start in zip(refs[used : used + len(starts)], starts):
            block = ref[start : start + size, :].astype(F32)
            value = block if value is None else value + block
        out[at + first : at + first + size, :] = value.astype(BF16)
        used += len(starts)


def both_kernel(pos, own0, recv0, own, send, total, *, bit):
    rows = own0.shape[0] // 2
    total[...] = own0[...] + recv0[...].astype(F32)
    for i in range(2):
        cut_rows(total, i * rows, rows, bit_of(pos, bit), own, i * rows // 2, send, i * rows // 2)


def settle_kernel(pos, own, recv, out):
    out[...] = (own[...].astype(F32) + recv[...].astype(F32)).astype(BF16)


def stack_kernel(pos, held, recv, out):
    size = held.shape[0]
    out[0:size] = held[...]
    out[size:] = recv[...]


def part_rows(value, at, rows, out1, out2):
    out1[at, 0:rows, :] = value[0:rows]
    out1[at, rows : rows + 8, :] = value[2 * rows :]
    out2[at] = value[rows : 2 * rows]


def settle_part_kernel(pos, own, recv, out1, out2):
    rows = (own.shape[0] - 8) // 2
    value = (own[...].astype(F32) + recv[...].astype(F32)).astype(BF16)
    part_rows(value, 0, rows, out1, out2)


def part_kernel(pos, held, recv, out1, out2):
    size, rows = held.shape[0], (held.shape[1] - 8) // 2
    for i, r in enumerate((held, recv)):
        for j in range(size):
            part_rows(r[j], i * size + j, rows, out1, out2)


def pair_kernel(pos, held1, recv1, held2, recv2, out1, out2):
    for out, h, r in ((out1, held1, recv1), (out2, held2, recv2)):
        size = h.shape[0]
        out[0:size] = h[...]
        out[size:] = r[...]


def unpack_kernel(pos, *refs, count, plans, orders, small):
    blocks1, blocks2, refs = refs[:count], refs[count : 2 * count], refs[2 * count :]
    outs, scratch, sums = refs[:-2], refs[-2], refs[-1]
    rows = blocks2[0].shape[1]
    used = 0
    for plan, order, blocks in zip(plans, orders, (blocks1, blocks2)):
        place = 0
        for b in order:
            place = place * 2 + bit_of(pos, b)
        each = blocks[0].shape[0]
        for i in range(count * each):
            at = pl.multiple_of((place ^ i) * rows, 8)
            scratch[pl.ds(at, rows), :] = blocks[i // each][i % each, 0:rows, :].astype(F32)
        for start, size, flip in plan:
            block = scratch[start : start + size, :]
            outs[used][...] = block.T if flip else block
            used += 1
    total = jnp.zeros((8, 512), F32)
    for r in blocks1:
        total = total + jnp.sum(r[:, rows:, :].astype(F32), axis=0)
    sums[...] = total
    for i, (row, start, size) in enumerate(small):
        outs[used + i][...] = sums[row : row + 1, start : start + size].reshape(size)


def body(
    layer_input, segments, norm1_gain, norm1_bias, w_query, b_query, w_key, w_value, b_value,
    w_out, b_out, gate1_w, gate1_b, norm2_gain, norm2_bias, w_in, b_in, w_back, b_back,
    gate2_w, gate2_b, cotangent, *, n_dp,
):
    def hop(value, mask):
        return lax.ppermute(value, "tensor", [(i, i ^ mask) for i in range(4)])

    def dhop(value, mask):
        return lax.ppermute(value, "dp", [(i, i ^ mask) for i in range(n_dp)])

    def after(value, *deps):
        return lax.optimization_barrier((value,) + deps)[0]

    t = lax.axis_index("tensor").astype(jnp.int32)
    me = lax.axis_index("dp").astype(jnp.int32)
    tb = jnp.where(jnp.arange(8) < 4, t ^ jnp.array(LOCAL + (0,) * 4, jnp.int32), me)
    seg = segments
    x0 = layer_input
    last = [None]

    def step(kernel, outs, args, name, scratch=(), smem=1, space=VM, then=(), limit=None, cost=HEAVY):
        pos = tb if last[0] is None else after(tb, last[0], *then)
        got = call(kernel, outs, [pos] + args, smem=smem, scratch=scratch, name=name, space=space, limit=limit, cost=COSTS.get(name, cost))
        last[0] = got[0]
        return got

    x1 = hop(x0, PX)
    x2 = hop(x0, 1)
    hbm = dict(space=pl.BlockSpec(memory_space=pltpu.MemorySpace.HBM), cost=LIGHT)
    s0, e0, c0, qa0, qb0, vecs = step(
        pack_kernel,
        [sds((296, 512), BF16), sds((256, 512), BF16), sds((1416, 512), BF16), sds((256, 384), BF16),
         sds((264, 384), BF16), sds((16, 512), F32)],
        [pltpu.with_memory_space_constraint(w, pltpu.MemorySpace.HBM) for w in
         (w_in, w_back, w_out, gate1_w, gate2_w, w_query, w_key, w_value, norm1_gain, norm1_bias, b_out, gate1_b,
          norm2_gain, norm2_bias, b_back, gate2_b, b_in, b_query, b_value)],
        "pack",
        [pltpu.SemaphoreType.DMA((27,)), pltpu.VMEM((512, 128), BF16)]
        + [pltpu.VMEM((512,), BF16)] * 9 + [pltpu.VMEM((128,), BF16)] * 2, **hbm,
    )
    qkv = [qa0, qb0, hop(qa0, 1), hop(qb0, 1)]
    sy = hop(s0, PX)
    c2 = hop(c0, 1)
    na, qt0, ka, vta = step(
        chip_kernel,
        [sds((512, 512), BF16), sds((256, 256), BF16), sds((512, 256), BF16), sds((256, 512), BF16)],
        [x0, x2, vecs] + qkv, "chip", cost=LIGHT,
    )
    x3 = hop(after(x1, na), 1)
    e1 = hop(after(e0, na), PX)
    n, qt1, k, vt, p1, ot1, att1, invl1 = step(
        first_kernel,
        [
            sds((1024, 512), BF16), sds((256, 256), BF16), sds((1024, 256), BF16),
            sds((256, 1024), BF16), sds((4, 1024, 256), BF16), sds((256, 256), BF16), sds((256, 256), BF16),
            sds((4, 8, 256), F32),
        ],
        [seg, seg, x1, x3, vecs] + qkv + [na, ka, vta],
        "first", ATT_SCRATCH, 2,
    )
    attp = hop(att1, PX)
    sy = after(sy, att1)
    sx = dhop(sy, 1)
    sz = dhop(sy, 2)
    p0, ot0, att0, invl0 = step(
        second_kernel,
        [sds((4, 1024, 256), BF16), sds((256, 256), BF16), sds((256, 256), BF16), sds((4, 8, 256), F32)],
        [seg, seg, qt0, k, vt],
        "second", ATT_SCRATCH, 2,
    )
    e3 = hop(after(e1, att0), 1)
    v, kt = step(prepare_kernel, [sds((1024, 256), BF16), sds((256, 1024), BF16)], [n, k] + qkv, "prepare")
    n2, mid, branch, gate = step(
        out_kernel,
        [sds((256, 512), BF16), sds((256, 512), F32), sds((256, 512), F32), sds((256, 512), F32)],
        [x0, n, att0, attp, vecs, e0, e1, c2, e3],
        "out", [pltpu.VMEM((512, 512), BF16)],
    )
    cut_a, cut_b = step(cut_kernel, [sds((128, 512), BF16), sds((168, 512), BF16)], [sx, sz], "cut")
    sxz_a, sxz_b = dhop(cut_a, 1), dhop(cut_b, 2)
    n2p = hop(after(n2, cut_a), PX)
    quarters = [sy, hop(after(sy, cut_a), 1), sx, hop(after(sx, cut_a), 1), sz, hop(after(sz, cut_a), 1)]
    total0, hid, slope0, slope1 = step(
        ffn_first_kernel,
        [sds((256, 512), F32), sds((256, 1024), BF16), sds((256, 1024), BF16), sds((256, 768), BF16)],
        [n2, vecs, w_in, w_back, c2] + quarters,
        "ffn_first", cost=LIGHT,
    )
    sxz_a, sxz_b = lax.optimization_barrier((sxz_a, sxz_b, total0))[0:2]
    quarters = quarters + [sxz_a, hop(sxz_a, 1), sxz_b, hop(sxz_b, 1)]
    result, fg, ltg, slope2 = step(
        ffn_kernel,
        [sds((256, 512), BF16), sds((256, 512), BF16), sds((256, 512), BF16), sds((256, 256), BF16)],
        [n2, mid, cotangent, vecs, gate2_w, c2, total0] + quarters,
        "ffn", [pltpu.VMEM((512, 512), BF16)],
    )
    fgp = hop(fg, PX)
    dot0, dotp, mg, bg, log, hg, sums = step(
        back_kernel,
        [
            sds((256, 256), BF16), sds((256, 256), BF16), sds((256, 512), F32), sds((256, 512), BF16),
            sds((256, 512), BF16), sds((256, 1024), BF16), sds((8, 512), F32),
        ],
        [fg, ltg, slope0, slope1, slope2, mid, branch, gate, cotangent, vecs, e0, e1, c2, e3, gate2_w, w_in, w_back]
        + quarters,
        "back", [pltpu.VMEM((512, 512), BF16)], then=(n2p,),
    )
    dot1 = hop(dotp, PX)
    skeep, ssend, gate_part = step(
        small_weight_kernel,
        [sds((776, 512), F32), sds((776, 512), BF16), sds((256, 512), F32)],
        [n, n2, ltg, log, att0, attp, bg, sums, e0, e1, c2, e3],
        "small_weight", [pltpu.VMEM((512, 512), F32), pltpu.VMEM((512, 512), F32), pltpu.VMEM((512, 512), BF16)],
    )
    srecv = hop(ssend, 1)
    back_scratch = [
        pltpu.VMEM((256, 256), F32), pltpu.VMEM((4, 128, 256), BF16), pltpu.VMEM((256, 256), BF16),
        pltpu.VMEM((4, 8, 256), F32),
    ]
    dk0, dv0, dq0 = step(
        back_first_kernel,
        [sds((256, 1024), F32), sds((256, 1024), F32), sds((256, 256), BF16)],
        [seg, p0, dot0, ot0, invl0, qt0, kt, v],
        "attn_back0", back_scratch, 2,
    )
    bkeep, bsend, slopep, spar = step(
        ffn_back_weight_kernel,
        [sds((512, 512), F32), sds((512, 512), BF16), sds((256, 1024), BF16), sds((392, 512), BF16)],
        [n2p, fg, fgp, hid, vecs, w_in, c2, skeep, srecv],
        "ffn_back_weight",
    )
    brecv = hop(bsend, 1)
    sparr = hop(spar, PX)
    ikeep, isend = step(
        ffn_in_weight_kernel,
        [sds((520, 512), F32), sds((520, 512), BF16)],
        [n2, n2p, fgp, hg, slopep, w_back, c2],
        "ffn_in_weight",
    )
    irecv = hop(isend, 1)
    bits = n_dp.bit_length() - 1

    def halves(tag, parts1, parts2, rows):
        arrays = [a for parts in (parts1, parts2) for _, group in parts for a, _ in group]
        static = tuple(
            tuple((m, tuple(start for _, start in group)) for m, group in parts) for parts in (parts1, parts2)
        )
        shapes = [sds((rows // 2, 512), F32), sds((rows // 2, 512), BF16)] * 2
        o1, s1, o2, s2 = step(
            functools.partial(halves_kernel, parts=static, rows=rows, bits=(0, 1)),
            shapes, arrays, "halves_" + tag, [pltpu.VMEM((rows, 512), F32)],
        )
        return o1, dhop(s1, 1), o2, dhop(s2, 2)

    def quarter_step(tag, o1, r1, o2, r2):
        rows = o1.shape[0]
        shapes = [sds((rows // 2, 512), F32), sds((rows // 2, 512), BF16)] * 2
        o1, s1, o2, s2 = step(
            functools.partial(halves_kernel, parts=(((rows, (0, 0)),),) * 2, rows=rows, bits=(1, 0)),
            shapes, [o1, r1, o2, r2], "quarters_" + tag, [pltpu.VMEM((rows, 512), F32)],
        )
        return o1, dhop(s1, 2), o2, dhop(s2, 1)

    def merge_step(tag, o1, r1, o2, r2, small):
        rows = o1.shape[0]
        pairs = [o1, r1, o2, r2]
        for b in range(2, bits - 1):
            kernel = merge_kernel if b == 2 else both_kernel
            own, sent = step(
                functools.partial(kernel, bit=b), [sds((rows, 512), F32), sds((rows, 512), BF16)],
                pairs, "cut_" + tag, [pltpu.VMEM((rows if b == 2 else 2 * rows, 512), F32)],
            )
            pairs, rows = [own, dhop(sent, 1 << b)], rows // 2
        static = tuple((f, m, tuple(start for _, start in group)) for f, m, group in small)
        arrays = [a for _, _, group in small for a, _ in group]
        own = step(
            functools.partial(round_kernel, count=len(pairs), small=static), [sds((2 * rows + 8, 512), BF16)],
            pairs + arrays, "merge_" + tag,
        )[0]
        return own, dhop(own, 1 << (bits - 1))

    def part_step(tag, own, recv):
        rows = (own.shape[0] - 8) // 2
        if bits > 3:
            held = step(settle_kernel, [sds(own.shape, BF16)], [own, recv], "settle")[0][None]
            for b in range(bits - 2, 2, -1):
                shape = (2 * held.shape[0],) + held.shape[1:]
                held = step(stack_kernel, [sds(shape, BF16)], [held, dhop(held, 1 << b)], "stack")[0]
            size = 2 * held.shape[0]
            kernel, args = part_kernel, [held, dhop(held, 4)]
        else:
            size, kernel, args = 1, settle_part_kernel, [own, recv]
        h1, h2 = step(kernel, [sds((size, rows + 8, 512), BF16), sds((size, rows, 512), BF16)], args, "part_" + tag)
        if tag in AHEAD:
            far1, far2 = dhop(h1, 1), dhop(h2, 2)
            r1, r2 = dhop(h1, 2), dhop(h2, 1)
            return h1, r1, far1, h2, r2, far2
        return h1, dhop(h1, 2), h2, dhop(h2, 1)

    def pair_step(tag, h1, r1, h2, r2):
        shapes = [sds((2 * h.shape[0],) + h.shape[1:], BF16) for h in (h1, h2)]
        h1, h2 = step(pair_kernel, shapes, [h1, r1, h2, r2], "pair_" + tag)
        return h1, dhop(h1, 1), h2, dhop(h2, 2)

    def unpack_step(tag, blocks, plans, small):
        shapes = [sds((512, size) if flip else (size, 512), F32) for plan in plans for _, size, flip in plan]
        rest = tuple(range(2, bits - 1))
        half = len(blocks) // 2
        rows = half * blocks[half].shape[0] * blocks[half].shape[1]
        return step(
            functools.partial(
                unpack_kernel, count=half, plans=plans, orders=((0, 1) + rest, (1, 0) + rest), small=small
            ),
            shapes + [sds((size,), F32) for _, _, size in small], list(blocks), "unpack_" + tag,
            [pltpu.VMEM((rows, 512), F32), pltpu.VMEM((8, 512), F32)],
        )

    f = halves("f", [(512, [(bkeep, 0), (brecv, 0)])], [(512, [(ikeep, 0), (irecv, 0)])], padded(512, n_dp))

    dqt, dkt, dvt, akeep, asend = step(
        back_second_kernel,
        [
            sds((256, 512), BF16), sds((256, 1024), BF16), sds((256, 1024), BF16), sds((392, 512), F32),
            sds((392, 512), BF16),
        ],
        [seg, p1, dot1, ot1, invl1, qt1, kt, v, dk0, dv0, dq0, n],
        "attn_back1", [pltpu.VMEM((256, 1024), F32), pltpu.VMEM((256, 1024), F32)] + back_scratch, 2,
    )
    arecv = hop(asend, 1)
    gown, gpar, gsend = step(
        input_kernel,
        [sds((512, 256), F32), sds((512, 256), F32), sds((512, 512), BF16)],
        [dqt, dkt, dvt] + qkv,
        "input_grad",
    )
    gsib = hop(gsend, 1)
    f = quarter_step("f", *f)
    a = halves(
        "a", [(384, [(akeep, 0), (arecv, 0)])], [(384, [(skeep, 0), (srecv, 0), (sparr, 0)])], padded(384, n_dp)
    )
    (gsum,) = step(half_columns_kernel, [sds((512, 256), BF16)], [gpar, gsib], "half_columns")
    gp = hop(gsum, PX)
    tail = [(skeep, 773), (srecv, 773), (sparr, 389)]
    f = merge_step("f", *f, [(0, 1, [(ikeep, 512), (irecv, 512)]), (1, 1, tail)])
    a = quarter_step("a", *a)
    input_grad, sums1 = step(
        last_kernel,
        [sds((256, 512), F32), sds((8, 512), F32)],
        [gown, gsib, gp, x0, mg, gate_part, vecs],
        "last",
    )
    sums1_b = hop(sums1, PX)
    sums1_a = hop(sums1, 1)
    sums1_c = hop(sums1, PX ^ 1)
    group = [(skeep, 768), (srecv, 768), (sparr, 384)]
    a = merge_step(
        "a", *a,
        [(0, 2, [(sums1, 0), (sums1_a, 0), (sums1_b, 0), (sums1_c, 0)]), (2, 1, [(akeep, 384), (arecv, 384)]),
         (3, 5, group)],
    )
    f = part_step("f", *f)
    h1, r1, far1, h2, r2, far2 = f
    f = [h1, r1, far1, dhop(r1, 1), h2, r2, far2, dhop(r2, 2)]
    a = part_step("a", *a)
    if "a" in AHEAD:
        h1, r1, far1, h2, r2, far2 = a
        a = [h1, r1, far1, dhop(r1, 1), h2, r2, far2, dhop(r2, 2)]
    else:
        a = pair_step("a", *a)
    g_wback, g_win, d_b_in, d_n2b = unpack_step(
        "f", f, (((0, 512, False),), ((0, 512, False),)), ((0, 0, 512), (1, 0, 512))
    )
    plans = (
        ((0, 128, True), (128, 128, True), (256, 128, True)),
        ((0, 128, False), (128, 128, False), (256, 128, False)),
    )
    small = ((0, 0, 512), (1, 0, 512), (2, 0, 128), (2, 128, 128)) + tuple((i, 0, 512) for i in range(3, 8))
    g_q, g_k, g_v, g_g2, g_g1, g_wo, d_n1g, d_n1b, d_bq, d_bv, d_b_back, d_g2b, d_b_out, d_g1b, d_n2g = unpack_step(
        "a", a, plans, small
    )
    return (
        result, input_grad, d_n1g, d_n1b, g_q, d_bq, g_k, g_v, d_bv, g_wo, d_b_out, g_g1, d_g1b, d_n2g, d_n2b,
        g_win, d_b_in, g_wback, d_b_back, g_g2, d_g2b,
    )


def solution(mesh):
    tok = P(("dp", "tensor"), None)
    col = P(None, "tensor")
    row = P("tensor", None)
    vec = P("tensor")
    rep = P()
    return jax.shard_map(
        functools.partial(body, n_dp=mesh.shape["dp"]),
        mesh=mesh,
        in_specs=(
            tok, P("dp", None), rep, rep, col, vec, col, col, vec, row, rep, row, rep, rep, rep,
            col, vec, row, rep, row, rep, tok,
        ),
        out_specs=(
            tok, tok, rep, rep, col, vec, col, col, vec, row, rep, row, rep, rep, rep,
            col, vec, row, rep, row, rep,
        ),
        check_vma=False,
    )
```
